128 devices in a mesh: lon: 16 (over z, x_lo, core), lat: 8 (over x_hi, y).
Axes of the slice: x: 4 (x_hi: 2, x_lo: 2; x = x_hi * 2 + x_lo), y: 4, z: 4, core: 2. Of those that a mesh axis runs over, the one named last changes fastest.
Arguments:
- tracers: float32 [2, 25, 512, 6144], P(None, None, 'lat', 'lon'), may hold values from -6 to 6
- east_speed: float32 [25, 512, 6144], P(None, 'lat', 'lon'), may hold values from -3 to 3
- north_speed: float32 [25, 512, 6144], P(None, 'lat', 'lon'), may hold values from -3 to 3
- wet: int32 [512, 6144], P('lat', 'lon'), may hold values 0 or 1
- fold_partner: int32 [6144], P('lon'), may hold values from 0 to 6143, as said below
- bergs: float32 [524288, 128], P(('lon', 'lat')), may hold values from -6 to 6
- berg_count: int32 [16384], P(('lon', 'lat')), may hold values from 0 to 32, as said below
- berg_cell: int32 [524288], P(('lon', 'lat')), may hold values from 0 to 24575
- melt_map: float32 [128, 50], replicated, may hold values from -0.5 to 0.5
Outputs:
- updated: float32 [2, 25, 512, 6144], P(None, None, 'lat', 'lon')
The draws below stay inside these ranges and needn't reach their ends.
Inputs may be any that keep to these rules, and one draw needn't show every extreme that they name: fold_partner is a permutation; the partner of column i lies among the 384 columns of block 15 - i // 384, blocks of 384 columns. `berg_count`: every source has a full owner, and some owner is full from every source.
All inputs are finite; a program needn't handle non-finite values. No bound on the sum of `wet` on one device may be relied on, other than what follows from the above.
Results may differ from the reference program's by a relative error of at most 0.000067.
Values sent between devices are 32-bit elements; how exact they have to be, the bound alone decides.
No kernel may reach another device: no remote copies, remote signals or barrier semaphores. Data moves between devices by JAX's collectives and lax.ppermute only.
A program may use at most 192 MiB of HBM per device.

```python
import jax
import jax.numpy as jnp
from jax import lax

LEV = 25
TRACERS = 2
BVAL = 128
CLAT = 64
CLON = 384
SLOT = 32
NLAT = 512
NLON = 6144
BERGS = 524288
N_LON = 16
N_LAT = 8


def block_order(key):
    return jax.random.permutation(key, CLON).astype(jnp.int32)


def draw_fold_partner(key, part):
    keys = jax.random.split(key, N_LON)
    within = jax.vmap(block_order)(keys)
    mirror = (N_LON - 1 - jnp.arange(N_LON, dtype=jnp.int32))[:, None] * CLON
    return (mirror + within).reshape(NLON).astype(jnp.int32)


def draw_berg_count(key, part):
    total = N_LON * N_LAT
    key_a, key_b, key_c = jax.random.split(key, 3)
    counts = jax.random.randint(key_a, (total, total), 0, SLOT + 1)
    favourite = jax.random.randint(key_b, (total, 1), 0, total)
    columns = jnp.arange(total, dtype=jnp.int32)[None, :]
    counts = jnp.where(columns == favourite, SLOT, counts)
    busiest = jax.random.randint(key_c, (), 0, total)
    counts = jnp.where(columns == busiest, SLOT, counts)
    return counts.reshape(total * total).astype(jnp.int32)


def draw_berg_cell(key, part):
    total = N_LON * N_LAT
    count_all = total * total * SLOT
    cells = jax.random.randint(key, (count_all,), 0, CLAT * CLON)
    position = jnp.arange(count_all, dtype=jnp.int32)
    cells = jnp.where(position == 0, 0, cells)
    cells = jnp.where(position == count_all - 1, CLAT * CLON - 1, cells)
    return cells.astype(jnp.int32)


def place_ends(drawn, rng, low, top_value):
    place = [jax.random.randint(jax.random.fold_in(rng, axis), (), 0, length) for axis, length in enumerate(drawn.shape)]
    widest = drawn.shape.index(max(drawn.shape))
    beside = place[:widest] + [(place[widest] + 1) % drawn.shape[widest]] + place[widest + 1:]
    return drawn.at[tuple(place)].set(low).at[tuple(beside)].set(top_value)


def level_of(key, shape, pieces, low, largest):
    level, own = 1.0, jax.random.fold_in(key, 6)
    for axis_at, parts in pieces:
        heights = jnp.exp(jax.random.uniform(jax.random.fold_in(own, axis_at), (parts,), jnp.float32, low / len(pieces), largest / len(pieces)))
        level = level * jnp.repeat(heights, shape[axis_at] // parts).reshape([-1 if axis == axis_at else 1 for axis in range(len(shape))])
    return level


def scatter_about(key, dims, width, reach, cuts=(), kind=jnp.bfloat16):
    array = jax.random.normal(key, dims, jnp.float32) * width
    if len(cuts) > 0:
        array = level_of(key, dims, cuts, -0.22, 0.18) * array
    return jnp.clip(array, min=-reach, max=reach).astype(kind)


def setup_inputs(seed: int = 0) -> dict:
    seeds = jax.random.split(jax.random.key(seed), 10)
    return {
        "tracers": scatter_about(seeds[0], (TRACERS, LEV, NLAT, NLON), 1.0, 6.0, ((2, 8), (3, 16)), jnp.float32),
        "east_speed": scatter_about(seeds[1], (LEV, NLAT, NLON), 0.5, 3.0, ((1, 8), (2, 16)), jnp.float32),
        "north_speed": scatter_about(seeds[2], (LEV, NLAT, NLON), 0.5, 3.0, ((1, 8), (2, 16)), jnp.float32),
        "wet": place_ends((jax.random.randint(seeds[3], (NLAT, NLON), 0, 8) < 7).astype(jnp.int32), jax.random.fold_in(seeds[3], 1), 0, 1),
        "fold_partner": draw_fold_partner(jax.random.fold_in(seeds[9], 71), 0),
        "bergs": scatter_about(seeds[5], (BERGS, BVAL), 1.0, 6.0, ((0, 128),), jnp.float32),
        "berg_count": draw_berg_count(jax.random.fold_in(seeds[9], 71), 0),
        "berg_cell": draw_berg_cell(jax.random.fold_in(seeds[9], 71), 0),
        "melt_map": scatter_about(seeds[8], (BVAL, TRACERS * LEV), BVAL ** -0.5, 0.5, (), jnp.float32),
    }


diffuse_h = 0.1
diffuse_v = 0.1
time_step = 0.5


def face_flux(value, speed, wetness, value_next, speed_next, wet_next):
    face = wetness * wet_next
    return face * (0.5 * (speed + speed_next) * (0.5 * (value + value_next)) - diffuse_h * (value_next - value))


def vertical_mix(tracers):
    zero_level = jnp.zeros_like(tracers[:, :1])
    step_diff = tracers[:, 1:] - tracers[:, :-1]
    upper = jnp.concatenate([step_diff, zero_level], axis=1)
    lower = jnp.concatenate([zero_level, step_diff], axis=1)
    return diffuse_v * upper - diffuse_v * lower


def reference(tracers, east_speed, north_speed, wet, fold_partner, bergs, berg_count, berg_cell, melt_map):
    wetness = wet.astype(jnp.float32)[None, None]
    speed_e = east_speed[None]
    speed_n = north_speed[None]
    flux_e = face_flux(tracers, speed_e, wetness, jnp.roll(tracers, -1, 3), jnp.roll(speed_e, -1, 3), jnp.roll(wetness, -1, 3))
    flux_w = jnp.roll(flux_e, 1, 3)
    fold_t = jnp.take(tracers[:, :, NLAT - 1:, :], fold_partner, axis=3)
    fold_v = -jnp.take(speed_n[:, :, NLAT - 1:, :], fold_partner, axis=3)
    fold_w = jnp.take(wetness[:, :, NLAT - 1:, :], fold_partner, axis=3)
    north_t = jnp.concatenate([tracers[:, :, 1:], fold_t], axis=2)
    north_v = jnp.concatenate([speed_n[:, :, 1:], fold_v], axis=2)
    north_w = jnp.concatenate([wetness[:, :, 1:], fold_w], axis=2)
    flux_n = face_flux(tracers, speed_n, wetness, north_t, north_v, north_w)
    flux_s = jnp.concatenate([jnp.zeros_like(flux_n[:, :, :1]), flux_n[:, :, :-1]], axis=2)
    vertical = vertical_mix(tracers)
    devices_all = N_LON * N_LAT
    live = (jnp.arange(SLOT, dtype=jnp.int32)[None, :] < berg_count[:, None]).astype(jnp.float32)
    loaded = bergs.reshape(devices_all * devices_all, SLOT, BVAL) * live[:, :, None]
    melt = jnp.einsum("psc,cm->mps", loaded, melt_map, precision=lax.Precision.HIGHEST)
    melt = melt.reshape(TRACERS * LEV, devices_all, devices_all, SLOT).transpose(0, 2, 1, 3)
    melt = melt.reshape(TRACERS * LEV, devices_all * devices_all * SLOT)
    owner = (jnp.arange(devices_all * devices_all * SLOT, dtype=jnp.int32) // (devices_all * SLOT)).astype(jnp.int32)
    global_row = (owner % N_LAT) * CLAT + berg_cell // CLON
    global_col = (owner // N_LAT) * CLON + berg_cell % CLON
    flat_cell = (global_row * NLON + global_col).astype(jnp.int32)
    sources = jnp.zeros((TRACERS * LEV, NLAT * NLON), jnp.float32).at[:, flat_cell].add(melt)
    sources = sources.reshape(TRACERS, LEV, NLAT, NLON)
    tendency = vertical - (flux_e - flux_w) - (flux_n - flux_s)
    return wetness * (tracers + time_step * tendency + sources)
```

```python
import functools

import jax
import jax.numpy as jnp
from jax import lax
from jax.experimental import pallas as pl
from jax.experimental.pallas import tpu as pltpu
from jax.sharding import PartitionSpec as P

diffuse_h = 0.1
diffuse_v = 0.1
time_step = 0.5

F32 = jnp.float32
BF16 = jnp.bfloat16
VM = pltpu.VMEM
VMEM_SPEC = pl.BlockSpec(memory_space=pltpu.VMEM)
SMEM_SPEC = pl.BlockSpec(memory_space=pltpu.SMEM)
ANY_SPEC = pl.BlockSpec(memory_space=pl.ANY)
LIMIT = 48 << 20

TR_LANES = 32
HALF = 64
WET_LANE = 127
ROW_LANE = 50
COL_LANE = 51
GROUP = 8


def split(value):
    high = value.astype(BF16)
    low = (value - high.astype(F32)).astype(BF16)
    return high, low


def dot_nt(a, b):
    return lax.dot_general(a, b, (((1,), (1,)), ((), ())), preferred_element_type=F32)


def dot_nn(a, b):
    return lax.dot_general(a, b, (((1,), (0,)), ((), ())), preferred_element_type=F32)


def melt_kernel(count_ref, berg_ref, map_ref, out_ref, weight_ref):
    maps = map_ref.shape[0]
    width = berg_ref.shape[1]
    owners = out_ref.shape[0]
    pairs = out_ref.shape[1]
    rows = owners * pairs
    weight_ref[...] = jnp.zeros_like(weight_ref)
    weight_ref[0:maps, 0:width] = map_ref[...]
    weight_ref[HALF : HALF + maps, width : 2 * width] = map_ref[...]
    w_high, w_low = split(weight_ref[...])
    even = berg_ref[pl.ds(0, rows, stride=2), :]
    odd = berg_ref[pl.ds(1, rows, stride=2), :]
    both = jnp.concatenate([even, odd], axis=1)
    b_high, b_low = split(both)
    made = dot_nt(b_high, w_high) + (dot_nt(b_high, w_low) + dot_nt(b_low, w_high))
    lane = lax.broadcasted_iota(jnp.int32, (pairs, 128), 1)
    slot = 2 * lax.broadcasted_iota(jnp.int32, (pairs, 128), 0) + (lane >= HALF).astype(jnp.int32)
    first = pl.program_id(0) * owners
    for o in range(owners):
        out_ref[o] = jnp.where(
            slot < count_ref[first + o], made[o * pairs : (o + 1) * pairs], 0.0
        )


def melt_rows(bergs, berg_count, melt_map):
    owners = berg_count.shape[0]
    slots = bergs.shape[0] // owners
    width = bergs.shape[1]
    steps = 4
    per = owners // steps
    return pl.pallas_call(
        melt_kernel,
        grid=(steps,),
        out_shape=jax.ShapeDtypeStruct((owners, slots // 2, 128), F32),
        in_specs=[
            SMEM_SPEC,
            pl.BlockSpec((per * slots, width), lambda i: (i, 0)),
            pl.BlockSpec(melt_map.shape[::-1], lambda i: (0, 0)),
        ],
        out_specs=pl.BlockSpec((per, slots // 2, 128), lambda i: (i, 0, 0)),
        scratch_shapes=[VM((128, 2 * width), F32)],
        compiler_params=pltpu.CompilerParams(vmem_limit_bytes=LIMIT),
        name="melt",
    )(berg_count, bergs, melt_map.T)


def stencil_kernel(
    tr_hbm, ea_hbm, no_hbm, wet_ref,
    part_hbm, ew_a, ew_b, ns_a, ns_b,
    tv, ev, nv, ov, m_e, m_n, wetf, west, east, sem_t, sem_e, sem_n, sem_o,
):
    levels, rows, cols = ea_hbm.shape
    strips = rows // 8

    def copies(k):
        return (
            pltpu.make_async_copy(tr_hbm.at[:, k], tv.at[:, k], sem_t.at[k]),
            pltpu.make_async_copy(ea_hbm.at[k], ev.at[k], sem_e.at[k]),
            pltpu.make_async_copy(no_hbm.at[k], nv.at[k], sem_n.at[k]),
        )

    def start_level(k, _):
        for c in copies(k):
            c.start()
        return _

    lax.fori_loop(0, levels, start_level, 0)

    odd_lon = lax.rem(lax.axis_index("lon"), 2)
    odd_lat = lax.rem(lax.axis_index("lat"), 2)
    row_a = odd_lat * (rows - 1)
    row_b = (1 - odd_lat) * (rows - 1)

    wet = wet_ref[...].astype(F32)
    wetf[...] = wet
    col = lax.broadcasted_iota(jnp.int32, (rows, cols), 1)
    row = lax.broadcasted_iota(jnp.int32, (rows, cols), 0)
    m_e[...] = jnp.where(col == cols - 1, 0.0, wet * pltpu.roll(wet, cols - 1, 1))
    m_n[...] = jnp.where(row == rows - 1, 0.0, wet * pltpu.roll(wet, rows - 1, 0))
    lane_all = lax.broadcasted_iota(jnp.int32, (rows, 128), 1)
    west[...] = jnp.where(lane_all == WET_LANE, wet[:, 0:1], 0.0)
    east[...] = jnp.where(lane_all == WET_LANE, wet[:, cols - 1 : cols], 0.0)
    ns_a[...] = jnp.zeros_like(ns_a)
    ns_b[...] = jnp.zeros_like(ns_b)
    ns_a[3 * levels : 3 * levels + 1, :] = wetf[pl.ds(row_a, 1), :]
    ns_b[3 * levels : 3 * levels + 1, :] = wetf[pl.ds(row_b, 1), :]

    lane = lax.broadcasted_iota(jnp.int32, (8, 128), 1)
    top = lax.broadcasted_iota(jnp.int32, (8, cols), 0) == 0

    def next_row(ref, lead, s):
        if s < strips - 1:
            return ref[lead + (pl.ds(8 * s + 1, 8), slice(None))]
        return pltpu.roll(ref[lead + (pl.ds(8 * s, 8), slice(None))], 7, 0)

    for c in copies(0):
        c.wait()

    def level(k, _):
        above = jnp.minimum(k + 1, levels - 1)
        below = jnp.maximum(k - 1, 0)

        @pl.when(k + 1 < levels)
        def _wait():
            for c in copies(k + 1):
                c.wait()

        in_0 = lane == k
        in_1 = lane == TR_LANES + k
        in_s = (lane == HALF + k) | (lane == HALF + TR_LANES + k)
        carried = [None, None]
        for s in range(strips):
            here = pl.ds(8 * s, 8)
            u = ev[k, here, :]
            v = nv[k, here, :]
            me = m_e[here, :]
            mn = m_n[here, :]
            w = wetf[here, :]
            s_e = (0.25 * time_step * me) * (u + pltpu.roll(u, cols - 1, 1))
            s_n = (0.25 * time_step * mn) * (v + next_row(nv, (k,), s))
            d_e = (diffuse_h * time_step) * me
            d_n = (diffuse_h * time_step) * mn
            a_e, b_e, a_n, b_n = s_e + d_e, s_e - d_e, s_n + d_n, s_n - d_n
            q_both = []
            for t in range(2):
                q = tv[t, k, here, :]
                q_both.append(q)
                up = tv[t, above, here, :]
                dn = tv[t, below, here, :]
                fe = q * a_e + pltpu.roll(q, cols - 1, 1) * b_e
                fn = q * a_n + next_row(tv, (t, k), s) * b_n
                fw = pltpu.roll(fe, 1, 1)
                turned = pltpu.roll(fn, 1, 0)
                last = jnp.zeros_like(turned) if carried[t] is None else carried[t]
                fs = jnp.where(top, last, turned)
                carried[t] = turned
                mix = (diffuse_v * time_step) * ((up - q) - (q - dn))
                ov[t, k, here, :] = w * (q + ((mix - (fe - fw)) - (fn - fs)))
            for ref, at in ((west, 0), (east, cols - 1)):
                old = ref[here, :]
                old = jnp.where(in_0, q_both[0][:, at : at + 1], old)
                old = jnp.where(in_1, q_both[1][:, at : at + 1], old)
                ref[here, :] = jnp.where(in_s, u[:, at : at + 1], old)
        for ref, at in ((ns_a, row_a), (ns_b, row_b)):
            ref[pl.ds(k, 1), :] = tv[0, k, pl.ds(at, 1), :]
            ref[pl.ds(levels + k, 1), :] = tv[1, k, pl.ds(at, 1), :]
            ref[pl.ds(2 * levels + k, 1), :] = nv[k, pl.ds(at, 1), :]
        pltpu.make_async_copy(ov.at[:, k], part_hbm.at[:, k], sem_o.at[k]).start()
        return _

    lax.fori_loop(0, levels, level, 0)
    is_odd = odd_lon == 1
    ew_a[...] = jnp.where(is_odd, west[...], east[...])
    ew_b[...] = jnp.where(is_odd, east[...], west[...])

    def finish(k, _):
        pltpu.make_async_copy(ov.at[:, k], part_hbm.at[:, k], sem_o.at[k]).wait()
        return _

    lax.fori_loop(0, levels, finish, 0)


def stencil(tracers, east_speed, north_speed, wet):
    count, levels, rows, cols = tracers.shape
    edge_rows = -(-(3 * levels + 1) // 8) * 8
    dma = pltpu.SemaphoreType.DMA((levels,))
    return pl.pallas_call(
        stencil_kernel,
        out_shape=(
            jax.ShapeDtypeStruct(tracers.shape, F32),
            jax.ShapeDtypeStruct((rows, 128), F32),
            jax.ShapeDtypeStruct((rows, 128), F32),
            jax.ShapeDtypeStruct((edge_rows, cols), F32),
            jax.ShapeDtypeStruct((edge_rows, cols), F32),
        ),
        in_specs=[ANY_SPEC, ANY_SPEC, ANY_SPEC, VMEM_SPEC],
        out_specs=(ANY_SPEC, VMEM_SPEC, VMEM_SPEC, VMEM_SPEC, VMEM_SPEC),
        scratch_shapes=[
            VM(tracers.shape, F32),
            VM(east_speed.shape, F32),
            VM(north_speed.shape, F32),
            VM(tracers.shape, F32),
            VM((rows, cols), F32),
            VM((rows, cols), F32),
            VM((rows, cols), F32),
            VM((rows, 128), F32),
            VM((rows, 128), F32),
            dma,
            dma,
            dma,
            dma,
        ],
        compiler_params=pltpu.CompilerParams(vmem_limit_bytes=LIMIT),
        name="stencil",
    )(tracers, east_speed, north_speed, wet)


def fix_kernel(
    fold_ref, ew_a, ew_b, ns_a, ns_b, ew_a_in, ew_b_in, ns_a_in, ns_b_in,
    fix_e, fix_w, fix_n, fix_s, north, south,
):
    levels = fix_n.shape[0] // 2
    cols = ns_a.shape[1]
    lon_count, lat_count = lax.axis_size("lon"), lax.axis_size("lat")
    lon_index, lat_index = lax.axis_index("lon"), lax.axis_index("lat")
    odd_lon = lax.rem(lon_index, 2) == 1
    odd_lat = lax.rem(lat_index, 2) == 1

    def faces(q, s, w, q_next, s_next, w_next):
        face = w * w_next
        speed = (0.25 * time_step) * face * (s + s_next)
        spread = (diffuse_h * time_step) * face
        return q * (speed + spread) + q_next * (speed - spread)

    def pick(odd, a, b):
        return jnp.where(odd, a, b)

    def column(value):
        return value, pltpu.roll(value, HALF, 1), value[:, WET_LANE : WET_LANE + 1]

    east_own = column(pick(odd_lon, ew_b[...], ew_a[...]))
    west_own = column(pick(odd_lon, ew_a[...], ew_b[...]))
    east_far = column(pick(odd_lon, ew_b_in[...], ew_a_in[...]))
    west_far = column(pick(odd_lon, ew_a_in[...], ew_b_in[...]))
    fix_e[...] = -(east_own[2] * faces(*east_own, *east_far))
    fix_w[...] = west_own[2] * faces(*west_far, *west_own)

    north[...] = pick(odd_lat, ns_a_in[...], ns_b_in[...])
    south[...] = pick(odd_lat, ns_b_in[...], ns_a_in[...])

    @pl.when(lat_index == lat_count - 1)
    def _fold():
        picks = fold_ref[...] - (lon_count - 1 - lon_index) * cols
        hot = (lax.broadcasted_iota(jnp.int32, (cols, cols), 0) == picks).astype(F32).astype(BF16)
        across = north[...]
        high, low = split(across)
        least = ((across - high.astype(F32)) - low.astype(F32)).astype(BF16)
        picked = dot_nn(high, hot) + (dot_nn(low, hot) + dot_nn(least, hot))
        at = lax.broadcasted_iota(jnp.int32, picked.shape, 0)
        is_speed = (at >= 2 * levels) & (at < 3 * levels)
        north[...] = jnp.where(is_speed, -picked, picked)

    def fields(value, t):
        return (
            value[t * levels : (t + 1) * levels],
            value[2 * levels : 3 * levels],
            value[3 * levels : 3 * levels + 1],
        )

    north_own = pick(odd_lat, ns_a[...], ns_b[...])
    south_own = pick(odd_lat, ns_b[...], ns_a[...])
    north_far, south_far = north[...], south[...]
    for t in range(2):
        at = pl.ds(t * levels, levels)
        own = fields(north_own, t)
        fix_n[at, :] = -(own[2] * faces(*own, *fields(north_far, t)))
        own = fields(south_own, t)
        fix_s[at, :] = own[2] * faces(*fields(south_far, t), *own)


def fixes(fold_partner, own, far, levels):
    rows, cols = own[0].shape[0], own[2].shape[1]
    return pl.pallas_call(
        fix_kernel,
        out_shape=(
            jax.ShapeDtypeStruct((rows, 128), F32),
            jax.ShapeDtypeStruct((rows, 128), F32),
            jax.ShapeDtypeStruct((2 * levels, cols), F32),
            jax.ShapeDtypeStruct((2 * levels, cols), F32),
        ),
        in_specs=[VMEM_SPEC] * 9,
        out_specs=(VMEM_SPEC,) * 4,
        scratch_shapes=[VM(own[2].shape, F32), VM(own[2].shape, F32)],
        compiler_params=pltpu.CompilerParams(vmem_limit_bytes=LIMIT),
        name="fix",
    )(fold_partner.reshape(1, cols), *own, *far)


def order_kernel(cell_ref, place_ref, start_ref, mark_ref, wide, *, cols):
    blocks = cell_ref.shape[0]
    buckets = 2 * GROUP
    cell = cell_ref[...]
    band = cell // (8 * cols)
    odd = lax.rem(lax.broadcasted_iota(jnp.int32, cell.shape, 1), 2)
    bucket = odd * GROUP + band
    hot = jnp.concatenate([(bucket == b).astype(F32) for b in range(buckets)], axis=0)
    hot16 = hot.astype(BF16)
    before = (
        lax.broadcasted_iota(jnp.int32, (128, 128), 0) < lax.broadcasted_iota(jnp.int32, (128, 128), 1)
    ).astype(F32).astype(BF16)
    within = dot_nn(hot16, before)
    totals = dot_nn(hot16, jnp.ones((128, 128), BF16))
    n = buckets * blocks
    earlier = (
        lax.broadcasted_iota(jnp.int32, (n, n), 1) < lax.broadcasted_iota(jnp.int32, (n, n), 0)
    ).astype(F32).astype(BF16)
    base = dot_nn(earlier, totals.astype(BF16))
    place = jnp.zeros(cell.shape, F32)
    start_ref[...] = jnp.full(start_ref.shape, blocks * 128, jnp.int32)
    for b in range(buckets):
        rows = slice(b * blocks, (b + 1) * blocks)
        place = place + hot[rows] * (base[rows] + within[rows])
        start_ref[b : b + 1, :] = base[b * blocks : b * blocks + 1].astype(jnp.int32)
    place_ref[...] = place.astype(jnp.int32)
    lane = lax.broadcasted_iota(jnp.int32, (128, 128), 1)
    row_f = (cell // cols).astype(F32)
    col_f = lax.rem(cell, cols).astype(F32)
    is_row = lax.rem(lane, HALF) == ROW_LANE
    is_col = lax.rem(lane, HALF) == COL_LANE
    for i in range(blocks):
        r = jnp.broadcast_to(row_f[i : i + 1], (128, 128)).T
        c = jnp.broadcast_to(col_f[i : i + 1], (128, 128)).T
        wide[i * 128 : (i + 1) * 128, :] = jnp.where(is_row, r, jnp.where(is_col, c, 0.0))
    half = blocks * 64
    low = lax.broadcasted_iota(jnp.int32, (half, 128), 1) < HALF
    mark_ref[...] = jnp.where(low, wide[pl.ds(0, half, stride=2), :], wide[pl.ds(1, half, stride=2), :])


def order(berg_cell, cols):
    blocks = berg_cell.shape[0] // 128
    return pl.pallas_call(
        functools.partial(order_kernel, cols=cols),
        out_shape=(
            jax.ShapeDtypeStruct((blocks, 128), jnp.int32),
            jax.ShapeDtypeStruct((3 * GROUP, 128), jnp.int32),
            jax.ShapeDtypeStruct((blocks * 64, 128), F32),
        ),
        in_specs=[VMEM_SPEC],
        out_specs=(VMEM_SPEC,) * 3,
        scratch_shapes=[VM((blocks * 128, 128), F32)],
        compiler_params=pltpu.CompilerParams(vmem_limit_bytes=LIMIT),
        name="order",
    )(berg_cell.reshape(blocks, 128))


def final_kernel(
    place_ref, start_ref, recv_ref, mark_ref, part_hbm, wet_ref, fix_e, fix_w, fix_n, fix_s,
    out_hbm,
    rows_v, sorted_v, pv, wetf, acc, lhs_h, lhs_l, hot_v, sem_i, sem_o,
):
    _, levels, rows, cols = pv.shape
    groups = rows // 8
    maps = 2 * levels
    n_rows = recv_ref.shape[0]

    def load(g):
        here = pl.ds(pl.multiple_of(8 * g, 8), 8)
        return pltpu.make_async_copy(part_hbm.at[:, :, here], pv.at[:, :, here], sem_i.at[g])

    def store(g):
        here = pl.ds(pl.multiple_of(8 * g, 8), 8)
        return pltpu.make_async_copy(pv.at[:, :, here], out_hbm.at[:, :, here], sem_o.at[g])

    for g in range(groups):
        load(g).start()
    rows_v[...] = recv_ref[...] + mark_ref[...]
    wetf[...] = wet_ref[...].astype(F32)

    unroll = 16

    def spread(i, _):
        for j in range(unroll):
            r = i * unroll + j
            line = rows_v[pl.ds(r, 1), :]
            sorted_v[pl.ds(place_ref[2 * r], 1), :] = line
            sorted_v[pl.ds(place_ref[2 * r + 1], 1), :] = line
        return _

    lax.fori_loop(0, n_rows // unroll, spread, 0)

    sub = lax.broadcasted_iota(jnp.int32, (8, 128), 0)
    subf = sub.astype(F32)
    lane = lax.broadcasted_iota(jnp.int32, (8, 128), 1)
    colf = lax.broadcasted_iota(jnp.int32, (128, cols), 1).astype(F32)
    last_chunk = n_rows // 128 - 1

    def group(g, _):
        here = pl.ds(pl.multiple_of(8 * g, 8), 8)
        first = []
        for h in range(2):
            s = start_ref[h * GROUP + g, 0]
            e = start_ref[h * GROUP + g + 1, 0]
            c = lax.div(s, 128)
            first.append((c, jnp.where(e > s, lax.div(e + 127, 128) - c, 0)))
        acc[...] = jnp.zeros_like(acc)

        def chunk(j, _):
            for h in range(2):
                c, n = first[h]
                at = jnp.minimum(c + j, h * (last_chunk + 1) + last_chunk)
                lines = sorted_v[pl.ds(pl.multiple_of(at * 128, 128), 128), :]
                flipped = lines.T
                off = h * HALF
                shift = (8 * g + jnp.where(j < n, 0, 4 * rows)).astype(F32)
                hit = subf == (flipped[off + ROW_LANE : off + ROW_LANE + 1, :] - shift)
                body = flipped[off : off + 56]
                high = body.astype(BF16).astype(F32)
                low = body - high
                for m in range(0, maps, 2):
                    for ref, src in ((lhs_h, high), (lhs_l, low)):
                        a = jnp.where(hit, src[m : m + 1, :], 0.0)
                        b = jnp.where(hit, src[m + 1 : m + 2, :], 0.0)
                        ref[8 * m : 8 * m + 16, h * 128 : (h + 1) * 128] = jnp.concatenate(
                            [a, b], axis=0
                        ).astype(BF16)
                hot = colf == lines[:, off + COL_LANE : off + COL_LANE + 1]
                hot_v[h * 128 : (h + 1) * 128, :] = hot.astype(F32).astype(BF16)
            acc[...] += dot_nn(lhs_h[...], hot_v[...]) + dot_nn(lhs_l[...], hot_v[...])
            return _

        lax.fori_loop(0, jnp.maximum(first[0][1], first[1][1]), chunk, 0)

        load(g).wait()
        w = wetf[here, :]
        e_fix = fix_e[here, :]
        w_fix = fix_w[here, :]
        at_n = (sub == 7) & (g == groups - 1)
        at_s = (sub == 0) & (g == 0)
        for m in range(maps):
            t, k = m // levels, m % levels
            at = t * TR_LANES + k
            for c in range(cols // 128):
                lanes = slice(c * 128, (c + 1) * 128)
                value = pv[t, k, here, lanes] + w[:, lanes] * acc[8 * m : 8 * m + 8, lanes]
                value += jnp.where(at_n, fix_n[m : m + 1, lanes], 0.0)
                value += jnp.where(at_s, fix_s[m : m + 1, lanes], 0.0)
                if c == 0:
                    value += jnp.where(lane == 0, w_fix[:, at : at + 1], 0.0)
                if c == cols // 128 - 1:
                    value += jnp.where(lane == 127, e_fix[:, at : at + 1], 0.0)
                pv[t, k, here, lanes] = value
        store(g).start()
        return _

    lax.fori_loop(0, groups, group, 0)
    for g in range(groups):
        store(g).wait()


def finish(place, start, recv, mark, part, wet, fix):
    count, levels, rows, cols = part.shape
    maps = count * levels
    dma = pltpu.SemaphoreType.DMA((rows // 8,))
    return pl.pallas_call(
        final_kernel,
        out_shape=jax.ShapeDtypeStruct(part.shape, F32),
        in_specs=[SMEM_SPEC, SMEM_SPEC, VMEM_SPEC, VMEM_SPEC, ANY_SPEC] + [VMEM_SPEC] * 5,
        out_specs=ANY_SPEC,
        scratch_shapes=[
            VM(recv.shape, F32),
            VM((2 * recv.shape[0], 128), F32),
            VM(part.shape, F32),
            VM((rows, cols), F32),
            VM((maps * 8, cols), F32),
            VM((maps * 8, 256), BF16),
            VM((maps * 8, 256), BF16),
            VM((256, cols), BF16),
            dma,
            dma,
        ],
        compiler_params=pltpu.CompilerParams(vmem_limit_bytes=LIMIT),
        name="final",
    )(place, start, recv, mark, part, wet, *fix)


def swap(value, axes, pairs):
    return lax.ppermute(value, axes, pairs + [(b, a) for a, b in pairs])


def shards(
    tracers, east_speed, north_speed, wet, fold_partner, bergs, berg_count, berg_cell, melt_map
):
    lon_count, lat_count = lax.axis_size("lon"), lax.axis_size("lat")
    levels, cols = tracers.shape[1], tracers.shape[3]

    melt = melt_rows(bergs, berg_count, melt_map)
    recv = lax.all_to_all(melt, ("lon", "lat"), split_axis=0, concat_axis=0, tiled=True)
    part, *own = stencil(tracers, east_speed, north_speed, wet)
    ew_a, ew_b, ns_a, ns_b = own

    lon_even = [(i, i + 1) for i in range(0, lon_count, 2)]
    lon_odd = [(i, (i + 1) % lon_count) for i in range(1, lon_count, 2)]

    def place(i, j):
        return i * lat_count + j

    lat_odd = [(place(i, j), place(i, j + 1)) for i in range(lon_count) for j in range(1, lat_count - 1, 2)]
    lat_odd += [
        (place(i, lat_count - 1), place(lon_count - 1 - i, lat_count - 1))
        for i in range(lon_count // 2)
    ]
    lat_even = [(j, j + 1) for j in range(0, lat_count, 2)]
    far = (
        swap(ew_a, "lon", lon_even),
        swap(ew_b, "lon", lon_odd),
        swap(ns_a, ("lon", "lat"), lat_odd),
        swap(ns_b, "lat", lat_even),
    )
    fix = fixes(fold_partner, own, far, levels)
    spots, start, mark = order(berg_cell, cols)
    recv = recv.reshape(-1, 128)
    return finish(spots.reshape(-1), start, recv, mark, part, wet, fix)


def solution(mesh):
    in_specs = (
        P(None, None, "lat", "lon"),
        P(None, "lat", "lon"),
        P(None, "lat", "lon"),
        P("lat", "lon"),
        P("lon"),
        P(("lon", "lat"), None),
        P(("lon", "lat")),
        P(("lon", "lat")),
        P(),
    )
    out_specs = P(None, None, "lat", "lon")
    return jax.shard_map(shards, mesh=mesh, in_specs=in_specs, out_specs=out_specs, check_vma=False)
```

```python
import functools

import jax
import jax.numpy as jnp
from jax import lax
from jax.experimental import pallas as pl
from jax.experimental.pallas import tpu as pltpu
from jax.sharding import PartitionSpec as P

diffuse_h = 0.1
diffuse_v = 0.1
time_step = 0.5

F32 = jnp.float32
BF16 = jnp.bfloat16
VM = pltpu.VMEM
VMEM_SPEC = pl.BlockSpec(memory_space=pltpu.VMEM)
SMEM_SPEC = pl.BlockSpec(memory_space=pltpu.SMEM)
ANY_SPEC = pl.BlockSpec(memory_space=pl.ANY)
LIMIT = 12 << 20

TR_LANES = 32
HALF = 64
WET_LANE = 127
WINDOW = 128
CELL_LANE = 50


def in_hbm(*values):
    return tuple(pltpu.with_memory_space_constraint(v, pltpu.HBM) for v in values)


def split(value):
    high = value.astype(BF16)
    low = (value - high.astype(F32)).astype(BF16)
    return high, low


def dot_nt(a, b):
    return lax.dot_general(a, b, (((1,), (1,)), ((), ())), preferred_element_type=F32)


def dot_nn(a, b):
    return lax.dot_general(a, b, (((1,), (0,)), ((), ())), preferred_element_type=F32)


def melt_kernel(count_ref, berg_ref, map_ref, out_ref, weight_ref):
    maps = map_ref.shape[0]
    width = berg_ref.shape[1]
    owners = out_ref.shape[0]
    pairs = out_ref.shape[1]
    rows = owners * pairs
    weight_ref[...] = jnp.zeros_like(weight_ref)
    weight_ref[0:maps, 0:width] = map_ref[...]
    weight_ref[HALF : HALF + maps, width : 2 * width] = map_ref[...]
    w_high, w_low = split(weight_ref[...])
    w_both = jnp.concatenate([w_high, w_low], axis=0)
    slots = berg_ref[...].reshape(owners, 2, pairs, width)
    both = jnp.concatenate([slots[:, h].reshape(rows, width) for h in range(2)], axis=1)
    b_high, b_low = split(both)
    wide = dot_nt(b_high, w_both)
    made = wide[:, :128] + (wide[:, 128:] + dot_nt(b_low, w_high))
    lane = lax.broadcasted_iota(jnp.int32, (pairs, 128), 1)
    slot = lax.broadcasted_iota(jnp.int32, (pairs, 128), 0) + jnp.where(lane >= HALF, pairs, 0)
    first = pl.program_id(0) * owners
    for o in range(owners):
        out_ref[o] = jnp.where(
            slot < count_ref[first + o], made[o * pairs : (o + 1) * pairs], 0.0
        )


def melt_rows(bergs, berg_count, melt_map):
    owners = berg_count.shape[0]
    slots = bergs.shape[0] // owners
    width = bergs.shape[1]
    steps = 4
    per = owners // steps
    return pl.pallas_call(
        melt_kernel,
        grid=(steps,),
        out_shape=jax.ShapeDtypeStruct((owners, slots // 2, 128), F32),
        in_specs=[
            SMEM_SPEC,
            pl.BlockSpec((per * slots, width), lambda i: (i, 0)),
            pl.BlockSpec(melt_map.shape[::-1], lambda i: (0, 0)),
        ],
        out_specs=pl.BlockSpec((per, slots // 2, 128), lambda i: (i, 0, 0)),
        scratch_shapes=[VM((128, 2 * width), F32)],
        compiler_params=pltpu.CompilerParams(vmem_limit_bytes=LIMIT),
        name="melt",
    )(*in_hbm(berg_count, bergs, melt_map.T))


def stencil_kernel(
    tr_hbm, ea_hbm, no_hbm, wet_ref,
    part_hbm, ew_a, ew_b, ns_a, ns_b,
    tv, ev, nv, ov, m_e, m_n, wetf, sem_t, sem_e, sem_n, sem_o,
):
    levels, rows, cols = ea_hbm.shape
    strips = rows // 8

    def copies(k):
        return (
            pltpu.make_async_copy(tr_hbm.at[:, k], tv.at[:, k], sem_t.at[k]),
            pltpu.make_async_copy(ea_hbm.at[k], ev.at[k], sem_e.at[k]),
            pltpu.make_async_copy(no_hbm.at[k], nv.at[k], sem_n.at[k]),
        )

    def result(k):
        return pltpu.make_async_copy(ov.at[:, k], part_hbm.at[:, k], sem_o.at[k])

    def start_level(k, _):
        for c in copies(k):
            c.start()
        return _

    lax.fori_loop(0, levels, start_level, 0)
    odd_lon = lax.rem(lax.axis_index("lon"), 2)
    odd_lat = lax.rem(lax.axis_index("lat"), 2)
    row_a = odd_lat * (rows - 1)
    row_b = (1 - odd_lat) * (rows - 1)

    wet = wet_ref[...].astype(F32)
    wetf[...] = wet
    col = lax.broadcasted_iota(jnp.int32, (rows, cols), 1)
    row = lax.broadcasted_iota(jnp.int32, (rows, cols), 0)
    m_e[...] = jnp.where(col == cols - 1, 0.0, wet * pltpu.roll(wet, cols - 1, 1))
    m_n[...] = jnp.where(row == rows - 1, 0.0, wet * pltpu.roll(wet, rows - 1, 0))
    lane_all = lax.broadcasted_iota(jnp.int32, (rows, 128), 1)
    ns_a[...] = jnp.zeros_like(ns_a)
    ns_b[...] = jnp.zeros_like(ns_b)
    ns_a[3 * levels : 3 * levels + 1, :] = wetf[pl.ds(row_a, 1), :]
    ns_b[3 * levels : 3 * levels + 1, :] = wetf[pl.ds(row_b, 1), :]

    lane = lax.broadcasted_iota(jnp.int32, (8, 128), 1)
    top = lax.broadcasted_iota(jnp.int32, (8, cols), 0) == 0
    marks = [lane == 0, lane == TR_LANES, lane == HALF]

    def next_row(ref, lead, s):
        if s < strips - 1:
            return ref[lead + (pl.ds(8 * s + 1, 8), slice(None))]
        return pltpu.roll(ref[lead + (pl.ds(8 * s, 8), slice(None))], 7, 0)

    for c in copies(0):
        c.wait()

    def level(k, packs):
        packs = list(packs)
        above = jnp.minimum(k + 1, levels - 1)
        below = jnp.maximum(k - 1, 0)

        @pl.when(k + 1 < levels)
        def _wait():
            for c in copies(k + 1):
                c.wait()

        carried = [None, None]
        for s in range(strips):
            here = pl.ds(8 * s, 8)
            u = ev[k, here, :]
            v = nv[k, here, :]
            me = m_e[here, :]
            mn = m_n[here, :]
            w = wetf[here, :]
            s_e = (0.25 * time_step * me) * (u + pltpu.roll(u, cols - 1, 1))
            s_n = (0.25 * time_step * mn) * (v + next_row(nv, (k,), s))
            d_e = (diffuse_h * time_step) * me
            d_n = (diffuse_h * time_step) * mn
            a_e, b_e, a_n, b_n = s_e + d_e, s_e - d_e, s_n + d_n, s_n - d_n
            edge = []
            for t in range(2):
                q = tv[t, k, here, :]
                edge.append(q)
                up = tv[t, above, here, :]
                dn = tv[t, below, here, :]
                fe = q * a_e + pltpu.roll(q, cols - 1, 1) * b_e
                fn = q * a_n + next_row(tv, (t, k), s) * b_n
                fw = pltpu.roll(fe, 1, 1)
                turned = pltpu.roll(fn, 1, 0)
                last = jnp.zeros_like(turned) if carried[t] is None else carried[t]
                fs = jnp.where(top, last, turned)
                carried[t] = turned
                mix = (diffuse_v * time_step) * ((up - q) - (q - dn))
                ov[t, k, here, :] = w * (q + ((mix - (fe - fw)) - (fn - fs)))
            edge.append(u)
            for side, lanes, shift in ((0, slice(0, 128), 0), (1, slice(cols - 128, cols), 1)):
                old = pltpu.roll(packs[2 * s + side], 1, 1)
                for at, (field, mark) in enumerate(zip(edge, marks)):
                    turn = at * TR_LANES + shift
                    moved = pltpu.roll(field[:, lanes], turn, 1) if turn else field[:, lanes]
                    old = jnp.where(mark, moved, old)
                packs[2 * s + side] = old
        for ref, at in ((ns_a, row_a), (ns_b, row_b)):
            ref[pl.ds(k, 1), :] = tv[0, k, pl.ds(at, 1), :]
            ref[pl.ds(levels + k, 1), :] = tv[1, k, pl.ds(at, 1), :]
            ref[pl.ds(2 * levels + k, 1), :] = nv[k, pl.ds(at, 1), :]
        result(k).start()
        return tuple(packs)

    packs = lax.fori_loop(0, levels, level, (jnp.zeros((8, 128), F32),) * (2 * strips))
    west = jnp.concatenate(packs[0::2], axis=0)
    east = jnp.concatenate(packs[1::2], axis=0)

    def again(value, mask):
        speed = (lane_all >= HALF + TR_LANES) & (lane_all < HALF + TR_LANES + levels)
        value = jnp.where(speed, pltpu.roll(value, TR_LANES, 1), value)
        return jnp.where(lane_all == WET_LANE, mask, value)

    is_odd = odd_lon == 1
    west_all, east_all = again(west, wetf[:, 0:1]), again(east, wetf[:, cols - 1 : cols])
    ew_a[...] = jnp.where(is_odd, west_all, east_all)
    ew_b[...] = jnp.where(is_odd, east_all, west_all)

    def done(k, _):
        result(k).wait()
        return _

    lax.fori_loop(0, levels, done, 0)


def stencil(tracers, east_speed, north_speed, wet):
    count, levels, rows, cols = tracers.shape
    edge_rows = -(-(3 * levels + 1) // 8) * 8
    dma = pltpu.SemaphoreType.DMA((levels,))
    return pl.pallas_call(
        stencil_kernel,
        out_shape=(
            pltpu.HBM(tracers.shape, F32),
            jax.ShapeDtypeStruct((rows, 128), F32),
            jax.ShapeDtypeStruct((rows, 128), F32),
            jax.ShapeDtypeStruct((edge_rows, cols), F32),
            jax.ShapeDtypeStruct((edge_rows, cols), F32),
        ),
        in_specs=[ANY_SPEC] * 3 + [VMEM_SPEC],
        out_specs=(ANY_SPEC,) + (VMEM_SPEC,) * 4,
        scratch_shapes=[
            VM(tracers.shape, F32),
            VM(east_speed.shape, F32),
            VM(north_speed.shape, F32),
            VM(tracers.shape, F32),
            VM((rows, cols), F32),
            VM((rows, cols), F32),
            VM((rows, cols), F32),
            dma,
            dma,
            dma,
            dma,
        ],
        compiler_params=pltpu.CompilerParams(vmem_limit_bytes=20 << 20),
        name="stencil",
    )(*in_hbm(tracers, east_speed, north_speed, wet))


def fix_kernel(
    fold_ref, ew_a, ew_b, ns_a, ns_b, ew_a_in, ew_b_in, ns_a_in, ns_b_in,
    fix_e, fix_w, fix_n, fix_s, north, south,
):
    levels = fix_n.shape[0] // 2
    cols = ns_a.shape[1]
    lon_count, lat_count = lax.axis_size("lon"), lax.axis_size("lat")
    lon_index, lat_index = lax.axis_index("lon"), lax.axis_index("lat")
    odd_lon = lax.rem(lon_index, 2) == 1
    odd_lat = lax.rem(lat_index, 2) == 1

    def faces(q, s, w, q_next, s_next, w_next):
        face = w * w_next
        speed = (0.25 * time_step) * face * (s + s_next)
        spread = (diffuse_h * time_step) * face
        return q * (speed + spread) + q_next * (speed - spread)

    def pick(odd, a, b):
        return jnp.where(odd, a, b)

    def column(value):
        return value, pltpu.roll(value, HALF, 1), value[:, WET_LANE : WET_LANE + 1]

    east_own = column(pick(odd_lon, ew_b[...], ew_a[...]))
    west_own = column(pick(odd_lon, ew_a[...], ew_b[...]))
    east_far = column(pick(odd_lon, ew_b_in[...], ew_a_in[...]))
    west_far = column(pick(odd_lon, ew_a_in[...], ew_b_in[...]))
    fix_e[...] = -(east_own[2] * faces(*east_own, *east_far))
    fix_w[...] = west_own[2] * faces(*west_far, *west_own)

    north[...] = pick(odd_lat, ns_a_in[...], ns_b_in[...])
    south[...] = pick(odd_lat, ns_b_in[...], ns_a_in[...])

    @pl.when(lat_index == lat_count - 1)
    def _fold():
        picks = fold_ref[...] - (lon_count - 1 - lon_index) * cols
        hot = (lax.broadcasted_iota(jnp.int32, (cols, cols), 0) == picks).astype(F32).astype(BF16)
        across = north[...]
        high, low = split(across)
        least = ((across - high.astype(F32)) - low.astype(F32)).astype(BF16)
        picked = dot_nn(high, hot) + (dot_nn(low, hot) + dot_nn(least, hot))
        at = lax.broadcasted_iota(jnp.int32, picked.shape, 0)
        is_speed = (at >= 2 * levels) & (at < 3 * levels)
        north[...] = jnp.where(is_speed, -picked, picked)

    def fields(value, t):
        return (
            value[t * levels : (t + 1) * levels],
            value[2 * levels : 3 * levels],
            value[3 * levels : 3 * levels + 1],
        )

    north_own = pick(odd_lat, ns_a[...], ns_b[...])
    south_own = pick(odd_lat, ns_b[...], ns_a[...])
    north_far, south_far = north[...], south[...]
    for t in range(2):
        at = pl.ds(t * levels, levels)
        own = fields(north_own, t)
        fix_n[at, :] = -(own[2] * faces(*own, *fields(north_far, t)))
        own = fields(south_own, t)
        fix_s[at, :] = own[2] * faces(*fields(south_far, t), *own)


def fixes(fold_partner, own, far, levels):
    rows, cols = own[0].shape[0], own[2].shape[1]
    return pl.pallas_call(
        fix_kernel,
        out_shape=(
            jax.ShapeDtypeStruct((rows, 128), F32),
            jax.ShapeDtypeStruct((rows, 128), F32),
            jax.ShapeDtypeStruct((2 * levels, cols), F32),
            jax.ShapeDtypeStruct((2 * levels, cols), F32),
        ),
        in_specs=[VMEM_SPEC] * 9,
        out_specs=(VMEM_SPEC,) * 4,
        scratch_shapes=[VM(own[2].shape, F32), VM(own[2].shape, F32)],
        compiler_params=pltpu.CompilerParams(vmem_limit_bytes=LIMIT),
        name="fix",
    )(*in_hbm(fold_partner.reshape(1, cols)), *own, *far)


def order_kernel(cell_ref, place_ref, start_ref, mark_ref, base_ref, *, rows, cols, pairs):
    blocks = cell_ref.shape[0]
    count = blocks * 128
    half = count // 2
    cell = cell_ref[...].astype(F32)
    row = jnp.floor((cell + 0.5) * (1.0 / cols))
    hot = [jnp.where(row == float(r), 1.0, 0.0) for r in range(rows)]
    hot16 = jnp.concatenate([h.astype(BF16) for h in hot], axis=0)
    down = lax.broadcasted_iota(jnp.int32, (128, 128), 0)
    along = lax.broadcasted_iota(jnp.int32, (128, 128), 1)
    before = jnp.where(down < along, 1.0, 0.0).astype(BF16)
    after = jnp.where(along < down, 1.0, 0.0).astype(BF16)
    ones = jnp.ones((128, 128), BF16)
    within = dot_nn(hot16, before)
    totals = dot_nn(hot16, ones)
    carry = jnp.zeros((1, 128), F32)
    place = jnp.zeros(cell.shape, F32)
    per = 128 // blocks
    for c in range(rows // per):
        part = totals[c * 128 : (c + 1) * 128]
        base = dot_nn(after, part.astype(BF16)) + carry
        carry = base[127:128] + part[127:128]
        base_ref[c * 128 : (c + 1) * 128, :] = base
        spot = base + within[c * 128 : (c + 1) * 128]
        for j in range(per):
            place = place + hot[c * per + j] * spot[j * blocks : (j + 1) * blocks]
    place_ref[...] = place.astype(jnp.int32)
    starts = base_ref[pl.ds(0, rows, stride=blocks), :]
    high = jnp.floor(starts * (1.0 / 128))
    low = starts - 128 * high
    first = jnp.where(along[:8] == 0, 1.0, 0.0).astype(BF16)
    starts = 128 * dot_nt(first, high.astype(BF16)) + dot_nt(first, low.astype(BF16))
    start_ref[...] = jnp.full(start_ref.shape, count, jnp.int32)
    start_ref[:, 0:rows] = starts.astype(jnp.int32)
    for i in range(blocks):
        turned = jnp.broadcast_to(cell[i : i + 1], (128, 128)).T
        for j in range(128 // pairs):
            at = (j % 2) * half + (i * (128 // pairs) + j) // 2 * pairs
            mark_ref[at : at + pairs, :] = turned[j * pairs : (j + 1) * pairs]


def order(berg_cell, rows, cols, pairs):
    count = berg_cell.shape[0]
    blocks = count // 128
    return pl.pallas_call(
        functools.partial(order_kernel, rows=rows, cols=cols, pairs=pairs),
        out_shape=(
            jax.ShapeDtypeStruct((blocks, 128), jnp.int32),
            jax.ShapeDtypeStruct((8, 128), jnp.int32),
            jax.ShapeDtypeStruct((count, 128), F32),
        ),
        in_specs=[VMEM_SPEC],
        out_specs=(VMEM_SPEC,) * 3,
        scratch_shapes=[VM((blocks * rows, 128), F32)],
        compiler_params=pltpu.CompilerParams(vmem_limit_bytes=LIMIT),
        name="order",
    )(*in_hbm(berg_cell.reshape(blocks, 128)))


def final_kernel(
    place_ref, start_ref, recv_ref, mark_ref, part_hbm, wet_ref, fix_e, fix_w, fix_n, fix_s,
    out_hbm,
    rows_v, sorted_v, pv, wetf, acc, sem_i, sem_o, *, pairs,
):
    _, levels, rows, cols = pv.shape
    groups = rows // 8
    tiles = cols // 128
    maps = 2 * levels
    n_rows = recv_ref.shape[0]
    count = 2 * n_rows

    def load(g):
        here = pl.ds(pl.multiple_of(8 * g, 8), 8)
        return pltpu.make_async_copy(part_hbm.at[:, :, here], pv.at[:, :, here], sem_i.at[g])

    def store(g):
        here = pl.ds(pl.multiple_of(8 * g, 8), 8)
        return pltpu.make_async_copy(pv.at[:, :, here], out_hbm.at[:, :, here], sem_o.at[g])

    for g in range(groups):
        load(g).start()
    lane_all = lax.broadcasted_iota(jnp.int32, (128, 128), 1)
    low_half = lane_all < HALF
    cell_lane = lane_all == CELL_LANE

    def halves(i, _):
        at = pl.multiple_of(i * 128, 128)
        both = recv_ref[pl.ds(at, 128), :]
        high = both.astype(BF16).astype(F32)
        low = both - high
        for h, body in enumerate(
            (
                jnp.where(low_half, high, pltpu.roll(low, HALF, 1)),
                jnp.where(low_half, pltpu.roll(high, HALF, 1), low),
            )
        ):
            there = pl.ds(pl.multiple_of(h * n_rows + at, 128), 128)
            rows_v[there, :] = jnp.where(cell_lane, mark_ref[there, :], body)
        return _

    lax.fori_loop(0, n_rows // 128, halves, 0)
    wetf[...] = wet_ref[...].astype(F32)
    sorted_v[count:, :] = jnp.full((WINDOW, 128), -1.0, F32)

    def spread(i, _):
        first = pl.multiple_of(i * pairs, pairs)
        for j in range(pairs):
            for h in range(2):
                to = place_ref[2 * first + h * pairs + j]
                sorted_v[pl.ds(to, 1), :] = rows_v[pl.ds(h * n_rows + first + j, 1), :]
        return _

    lax.fori_loop(0, n_rows // pairs, spread, 0)

    lane = lax.broadcasted_iota(jnp.int32, (8, 128), 1)
    lanef = lax.broadcasted_iota(jnp.int32, (WINDOW, 128), 1).astype(F32)

    def row_sources(r, at):
        at = pl.multiple_of(at, 8)
        lines = sorted_v[pl.ds(at, WINDOW), :]
        lhs = lines.T.astype(BF16)
        near = lines[:, CELL_LANE : CELL_LANE + 1] - (r * cols).astype(F32)
        hot = [jnp.where(near - float(128 * c) == lanef, 1.0, 0.0).astype(BF16) for c in range(tiles)]
        both = dot_nn(lhs, jnp.concatenate(hot, axis=1))
        return both[:HALF] + both[HALF:]

    def group(g, _):
        here = pl.ds(pl.multiple_of(8 * g, 8), 8)
        firsts, windows = [], []
        for j in range(8):
            s = start_ref[0, 8 * g + j]
            e = start_ref[0, 8 * g + j + 1]
            first = lax.div(s, 8) * 8
            firsts.append(first)
            windows.append(lax.div(e - first + (WINDOW - 1), WINDOW))
        for j in range(8):
            made = row_sources(8 * g + j, firsts[j])
            for c in range(tiles):
                acc[c, j * HALF : (j + 1) * HALF, :] = made[:, c * 128 : (c + 1) * 128]
        most = functools.reduce(jnp.maximum, windows)

        @pl.when(most > 1)
        def _more():
            for j in range(8):

                def again(i, _, j=j):
                    made = row_sources(8 * g + j, firsts[j] + i * WINDOW)
                    for c in range(tiles):
                        acc[c, j * HALF : (j + 1) * HALF, :] += made[:, c * 128 : (c + 1) * 128]
                    return _

                lax.fori_loop(1, windows[j], again, 0)

        load(g).wait()
        w = wetf[here, :]
        e_fix = fix_e[here, :]
        w_fix = fix_w[here, :]

        for edge, ref, at in ((groups - 1, fix_n, rows - 1), (0, fix_s, 0)):

            @pl.when(g == edge)
            def _edge_row(ref=ref, at=at):
                for m in range(maps):
                    t, k = m // levels, m % levels
                    pv[t, k, at : at + 1, :] += ref[m : m + 1, :]

        for m in range(maps):
            t, k = m // levels, m % levels
            at = t * TR_LANES + levels - 1 - k
            for c in range(tiles):
                lanes = slice(c * 128, (c + 1) * 128)
                value = pv[t, k, here, lanes] + w[:, lanes] * acc[c, pl.ds(m, 8, stride=HALF), :]
                if c == 0:
                    value += jnp.where(lane == 0, pltpu.roll(w_fix, (128 - at) % 128, 1), 0.0)
                if c == tiles - 1:
                    value += jnp.where(lane == 127, pltpu.roll(e_fix, 127 - at, 1), 0.0)
                pv[t, k, here, lanes] = value
        store(g).start()
        return _

    lax.fori_loop(0, groups, group, 0)
    for g in range(groups):
        store(g).wait()


def finish(place, start, recv, mark, part, wet, fix, pairs):
    _, levels, rows, cols = part.shape
    dma = pltpu.SemaphoreType.DMA((rows // 8,))
    return pl.pallas_call(
        functools.partial(final_kernel, pairs=pairs),
        out_shape=jax.ShapeDtypeStruct(part.shape, F32),
        in_specs=[SMEM_SPEC] * 2 + [VMEM_SPEC] * 2 + [ANY_SPEC] + [VMEM_SPEC] * 5,
        out_specs=ANY_SPEC,
        scratch_shapes=[
            VM((2 * recv.shape[0], 128), F32),
            VM((2 * recv.shape[0] + WINDOW, 128), F32),
            VM(part.shape, F32),
            VM((rows, cols), F32),
            VM((cols // 128, 8 * HALF, 128), F32),
            dma,
            dma,
        ],
        compiler_params=pltpu.CompilerParams(vmem_limit_bytes=24 << 20),
        name="final",
    )(place, start, recv, mark, *in_hbm(part, wet), *fix)


def swap(value, axes, pairs):
    return lax.ppermute(value, axes, pairs + [(b, a) for a, b in pairs])


def shards(
    tracers, east_speed, north_speed, wet, fold_partner, bergs, berg_count, berg_cell, melt_map
):
    lon_count, lat_count = lax.axis_size("lon"), lax.axis_size("lat")
    levels, cols = tracers.shape[1], tracers.shape[3]

    melt = melt_rows(bergs, berg_count, melt_map)
    recv = lax.all_to_all(melt, ("lon", "lat"), split_axis=0, concat_axis=0, tiled=True)
    part, *own = stencil(tracers, east_speed, north_speed, wet)
    ew_a, ew_b, ns_a, ns_b = own

    lon_even = [(i, i + 1) for i in range(0, lon_count, 2)]
    lon_odd = [(i, (i + 1) % lon_count) for i in range(1, lon_count, 2)]

    def place(i, j):
        return i * lat_count + j

    lat_odd = [(place(i, j), place(i, j + 1)) for i in range(lon_count) for j in range(1, lat_count - 1, 2)]
    lat_odd += [
        (place(i, lat_count - 1), place(lon_count - 1 - i, lat_count - 1))
        for i in range(lon_count // 2)
    ]
    lat_even = [(j, j + 1) for j in range(0, lat_count, 2)]
    far = (
        swap(ew_a, "lon", lon_even),
        swap(ew_b, "lon", lon_odd),
        swap(ns_a, ("lon", "lat"), lat_odd),
        swap(ns_b, "lat", lat_even),
    )
    fix = fixes(fold_partner, own, far, levels)
    pairs = melt.shape[1]
    spots, start, mark = order(berg_cell, tracers.shape[2], cols, pairs)
    recv = recv.reshape(-1, 128)
    return finish(spots.reshape(-1), start, recv, mark, part, wet, fix, pairs)


def solution(mesh):
    in_specs = (
        P(None, None, "lat", "lon"),
        P(None, "lat", "lon"),
        P(None, "lat", "lon"),
        P("lat", "lon"),
        P("lon"),
        P(("lon", "lat"), None),
        P(("lon", "lat")),
        P(("lon", "lat")),
        P(),
    )
    out_specs = P(None, None, "lat", "lon")
    return jax.shard_map(shards, mesh=mesh, in_specs=in_specs, out_specs=out_specs, check_vma=False)
```

```python
import functools

import jax
import jax.numpy as jnp
from jax import lax
from jax.experimental import pallas as pl
from jax.experimental.pallas import tpu as pltpu
from jax.sharding import PartitionSpec as P

diffuse_h = 0.1
diffuse_v = 0.1
time_step = 0.5

F32 = jnp.float32
BF16 = jnp.bfloat16
VM = pltpu.VMEM
VMEM_SPEC = pl.BlockSpec(memory_space=pltpu.VMEM)
SMEM_SPEC = pl.BlockSpec(memory_space=pltpu.SMEM)
ANY_SPEC = pl.BlockSpec(memory_space=pl.ANY)
LIMIT = 12 << 20

TR_LANES = 32
HALF = 64
WET_LANE = 127
AHEAD = 5
WINDOW = 128
CELL_LANE = 50


def in_hbm(*values):
    return tuple(pltpu.with_memory_space_constraint(v, pltpu.HBM) for v in values)


def split(value):
    high = value.astype(BF16)
    low = (value - high.astype(F32)).astype(BF16)
    return high, low


def dot_nt(a, b):
    return lax.dot_general(a, b, (((1,), (1,)), ((), ())), preferred_element_type=F32)


def dot_nn(a, b):
    return lax.dot_general(a, b, (((1,), (0,)), ((), ())), preferred_element_type=F32)


def melt_kernel(count_ref, berg_ref, map_ref, out_ref, weight_ref, both_ref):
    maps = map_ref.shape[0]
    width = berg_ref.shape[1]
    owners = out_ref.shape[0]
    pairs = out_ref.shape[1]
    rows = owners * pairs

    @pl.when(pl.program_id(0) == 0)
    def _weights():
        weight_ref[...] = jnp.zeros_like(weight_ref)
        weight_ref[0:maps, 0:width] = map_ref[...]
        weight_ref[HALF : HALF + maps, width : 2 * width] = map_ref[...]
        both_ref[...] = jnp.concatenate(split(weight_ref[...]), axis=0)

    w_both = both_ref[...]
    w_high = w_both[:128]
    slots = berg_ref[...].reshape(owners, 2, pairs, width)
    both = jnp.concatenate([slots[:, h].reshape(rows, width) for h in range(2)], axis=1)
    b_high, b_low = split(both)
    wide = dot_nt(b_high, w_both)
    made = wide[:, :128] + (wide[:, 128:] + dot_nt(b_low, w_high))
    lane = lax.broadcasted_iota(jnp.int32, (pairs, 128), 1)
    slot = lax.broadcasted_iota(jnp.int32, (pairs, 128), 0) + jnp.where(lane >= HALF, pairs, 0)
    first = pl.program_id(0) * owners
    for o in range(owners):
        out_ref[o] = jnp.where(
            slot < count_ref[first + o], made[o * pairs : (o + 1) * pairs], 0.0
        )


def melt_rows(bergs, berg_count, melt_map):
    owners = berg_count.shape[0]
    slots = bergs.shape[0] // owners
    width = bergs.shape[1]
    steps = 8
    per = owners // steps
    return pl.pallas_call(
        melt_kernel,
        grid=(steps,),
        out_shape=jax.ShapeDtypeStruct((owners, slots // 2, 128), F32),
        in_specs=[
            SMEM_SPEC,
            pl.BlockSpec((per * slots, width), lambda i: (i, 0)),
            pl.BlockSpec(melt_map.shape[::-1], lambda i: (0, 0)),
        ],
        out_specs=pl.BlockSpec((per, slots // 2, 128), lambda i: (i, 0, 0)),
        scratch_shapes=[VM((128, 2 * width), F32), VM((256, 2 * width), BF16)],
        compiler_params=pltpu.CompilerParams(vmem_limit_bytes=LIMIT),
        name="melt",
    )(*in_hbm(berg_count, bergs, melt_map.T))


def stencil_kernel(
    tr_hbm, ea_hbm, no_hbm, wet_ref,
    part_hbm, ew_a, ew_b, ns_a, ns_b,
    tv, ev, nv, ov, m_e, m_n, wetf, sem_t, sem_e, sem_n, sem_o,
):
    levels, rows, cols = ea_hbm.shape
    strips = rows // 8

    def copies(k):
        return (
            pltpu.make_async_copy(tr_hbm.at[:, k], tv.at[:, k], sem_t.at[k]),
            pltpu.make_async_copy(ea_hbm.at[k], ev.at[k], sem_e.at[k]),
            pltpu.make_async_copy(no_hbm.at[k], nv.at[k], sem_n.at[k]),
        )

    def result(k):
        return pltpu.make_async_copy(ov.at[:, k], part_hbm.at[:, k], sem_o.at[k])

    for k in range(AHEAD):
        for c in copies(k):
            c.start()
    odd_lon = lax.rem(lax.axis_index("lon"), 2)
    odd_lat = lax.rem(lax.axis_index("lat"), 2)
    row_a = odd_lat * (rows - 1)
    row_b = (1 - odd_lat) * (rows - 1)

    wet = wet_ref[...].astype(F32)
    wetf[...] = wet
    col = lax.broadcasted_iota(jnp.int32, (rows, cols), 1)
    row = lax.broadcasted_iota(jnp.int32, (rows, cols), 0)
    m_e[...] = jnp.where(col == cols - 1, 0.0, wet * pltpu.roll(wet, cols - 1, 1))
    m_n[...] = jnp.where(row == rows - 1, 0.0, wet * pltpu.roll(wet, rows - 1, 0))
    lane_all = lax.broadcasted_iota(jnp.int32, (rows, 128), 1)
    ns_a[...] = jnp.zeros_like(ns_a)
    ns_b[...] = jnp.zeros_like(ns_b)
    ns_a[3 * levels : 3 * levels + 1, :] = wetf[pl.ds(row_a, 1), :]
    ns_b[3 * levels : 3 * levels + 1, :] = wetf[pl.ds(row_b, 1), :]

    lane = lax.broadcasted_iota(jnp.int32, (8, 128), 1)
    top = lax.broadcasted_iota(jnp.int32, (8, cols), 0) == 0
    marks = [lane == 0, lane == TR_LANES, lane == HALF]

    def next_row(ref, lead, s):
        if s < strips - 1:
            return ref[lead + (pl.ds(8 * s + 1, 8), slice(None))]
        return pltpu.roll(ref[lead + (pl.ds(8 * s, 8), slice(None))], 7, 0)

    for c in copies(0):
        c.wait()

    def level(k, packs):
        packs = list(packs)
        above = jnp.minimum(k + 1, levels - 1)
        below = jnp.maximum(k - 1, 0)

        @pl.when(k + AHEAD < levels)
        def _start():
            for c in copies(k + AHEAD):
                c.start()

        @pl.when(k + 1 < levels)
        def _wait():
            for c in copies(k + 1):
                c.wait()

        carried = [None, None]
        for s in range(strips):
            here = pl.ds(8 * s, 8)
            u = ev[k, here, :]
            v = nv[k, here, :]
            me = m_e[here, :]
            mn = m_n[here, :]
            w = wetf[here, :]
            s_e = (0.25 * time_step * me) * (u + pltpu.roll(u, cols - 1, 1))
            s_n = (0.25 * time_step * mn) * (v + next_row(nv, (k,), s))
            d_e = (diffuse_h * time_step) * me
            d_n = (diffuse_h * time_step) * mn
            a_e, b_e, a_n, b_n = s_e + d_e, s_e - d_e, s_n + d_n, s_n - d_n
            edge = []
            for t in range(2):
                q = tv[t, k, here, :]
                edge.append(q)
                up = tv[t, above, here, :]
                dn = tv[t, below, here, :]
                fe = q * a_e + pltpu.roll(q, cols - 1, 1) * b_e
                fn = q * a_n + next_row(tv, (t, k), s) * b_n
                fw = pltpu.roll(fe, 1, 1)
                turned = pltpu.roll(fn, 1, 0)
                last = jnp.zeros_like(turned) if carried[t] is None else carried[t]
                fs = jnp.where(top, last, turned)
                carried[t] = turned
                mix = (diffuse_v * time_step) * ((up - q) - (q - dn))
                ov[t, k, here, :] = w * (q + ((mix - (fe - fw)) - (fn - fs)))
            edge.append(u)
            for side, lanes, shift in ((0, slice(0, 128), 0), (1, slice(cols - 128, cols), 1)):
                old = pltpu.roll(packs[2 * s + side], 1, 1)
                for at, (field, mark) in enumerate(zip(edge, marks)):
                    turn = at * TR_LANES + shift
                    moved = pltpu.roll(field[:, lanes], turn, 1) if turn else field[:, lanes]
                    old = jnp.where(mark, moved, old)
                packs[2 * s + side] = old
        for ref, at in ((ns_a, row_a), (ns_b, row_b)):
            ref[pl.ds(k, 1), :] = tv[0, k, pl.ds(at, 1), :]
            ref[pl.ds(levels + k, 1), :] = tv[1, k, pl.ds(at, 1), :]
            ref[pl.ds(2 * levels + k, 1), :] = nv[k, pl.ds(at, 1), :]
        result(k).start()
        return tuple(packs)

    packs = lax.fori_loop(0, levels, level, (jnp.zeros((8, 128), F32),) * (2 * strips))
    west = jnp.concatenate(packs[0::2], axis=0)
    east = jnp.concatenate(packs[1::2], axis=0)

    def again(value, mask):
        speed = (lane_all >= HALF + TR_LANES) & (lane_all < HALF + TR_LANES + levels)
        value = jnp.where(speed, pltpu.roll(value, TR_LANES, 1), value)
        return jnp.where(lane_all == WET_LANE, mask, value)

    is_odd = odd_lon == 1
    west_all, east_all = again(west, wetf[:, 0:1]), again(east, wetf[:, cols - 1 : cols])
    ew_a[...] = jnp.where(is_odd, west_all, east_all)
    ew_b[...] = jnp.where(is_odd, east_all, west_all)

    def done(k, _):
        result(k).wait()
        return _

    lax.fori_loop(0, levels, done, 0)


def stencil(tracers, east_speed, north_speed, wet):
    count, levels, rows, cols = tracers.shape
    edge_rows = -(-(3 * levels + 1) // 8) * 8
    dma = pltpu.SemaphoreType.DMA((levels,))
    return pl.pallas_call(
        stencil_kernel,
        out_shape=(
            pltpu.HBM(tracers.shape, F32),
            jax.ShapeDtypeStruct((rows, 128), F32),
            jax.ShapeDtypeStruct((rows, 128), F32),
            jax.ShapeDtypeStruct((edge_rows, cols), F32),
            jax.ShapeDtypeStruct((edge_rows, cols), F32),
        ),
        in_specs=[ANY_SPEC] * 3 + [VMEM_SPEC],
        out_specs=(ANY_SPEC,) + (VMEM_SPEC,) * 4,
        scratch_shapes=[
            VM(tracers.shape, F32),
            VM(east_speed.shape, F32),
            VM(north_speed.shape, F32),
            VM(tracers.shape, F32),
            VM((rows, cols), F32),
            VM((rows, cols), F32),
            VM((rows, cols), F32),
            dma,
            dma,
            dma,
            dma,
        ],
        compiler_params=pltpu.CompilerParams(vmem_limit_bytes=20 << 20),
        name="stencil",
    )(*in_hbm(tracers, east_speed, north_speed, wet))


def fix_kernel(
    fold_ref, ew_a, ew_b, ns_a, ns_b, ew_a_in, ew_b_in, ns_a_in, ns_b_in,
    fix_e, fix_w, fix_n, fix_s, north, south,
):
    levels = fix_n.shape[0] // 2
    cols = ns_a.shape[1]
    lon_count, lat_count = lax.axis_size("lon"), lax.axis_size("lat")
    lon_index, lat_index = lax.axis_index("lon"), lax.axis_index("lat")
    odd_lon = lax.rem(lon_index, 2) == 1
    odd_lat = lax.rem(lat_index, 2) == 1

    def faces(q, s, w, q_next, s_next, w_next):
        face = w * w_next
        speed = (0.25 * time_step) * face * (s + s_next)
        spread = (diffuse_h * time_step) * face
        return q * (speed + spread) + q_next * (speed - spread)

    def pick(odd, a, b):
        return jnp.where(odd, a, b)

    def column(value):
        return value, pltpu.roll(value, HALF, 1), value[:, WET_LANE : WET_LANE + 1]

    east_own = column(pick(odd_lon, ew_b[...], ew_a[...]))
    west_own = column(pick(odd_lon, ew_a[...], ew_b[...]))
    east_far = column(pick(odd_lon, ew_b_in[...], ew_a_in[...]))
    west_far = column(pick(odd_lon, ew_a_in[...], ew_b_in[...]))
    fix_e[...] = -(east_own[2] * faces(*east_own, *east_far))
    fix_w[...] = west_own[2] * faces(*west_far, *west_own)

    north[...] = pick(odd_lat, ns_a_in[...], ns_b_in[...])
    south[...] = pick(odd_lat, ns_b_in[...], ns_a_in[...])

    @pl.when(lat_index == lat_count - 1)
    def _fold():
        picks = fold_ref[...].reshape(1, cols) - (lon_count - 1 - lon_index) * cols
        hot = (lax.broadcasted_iota(jnp.int32, (cols, cols), 0) == picks).astype(F32).astype(BF16)
        across = north[...]
        high, low = split(across)
        least = ((across - high.astype(F32)) - low.astype(F32)).astype(BF16)
        picked = dot_nn(high, hot) + (dot_nn(low, hot) + dot_nn(least, hot))
        at = lax.broadcasted_iota(jnp.int32, picked.shape, 0)
        is_speed = (at >= 2 * levels) & (at < 3 * levels)
        north[...] = jnp.where(is_speed, -picked, picked)

    def fields(value, t):
        return (
            value[t * levels : (t + 1) * levels],
            value[2 * levels : 3 * levels],
            value[3 * levels : 3 * levels + 1],
        )

    north_own = pick(odd_lat, ns_a[...], ns_b[...])
    south_own = pick(odd_lat, ns_b[...], ns_a[...])
    north_far, south_far = north[...], south[...]
    for t in range(2):
        at = pl.ds(t * levels, levels)
        own = fields(north_own, t)
        fix_n[at, :] = -(own[2] * faces(*own, *fields(north_far, t)))
        own = fields(south_own, t)
        fix_s[at, :] = own[2] * faces(*fields(south_far, t), *own)


def fixes(fold_partner, own, far, levels):
    rows, cols = own[0].shape[0], own[2].shape[1]
    return pl.pallas_call(
        fix_kernel,
        out_shape=(
            jax.ShapeDtypeStruct((rows, 128), F32),
            jax.ShapeDtypeStruct((rows, 128), F32),
            jax.ShapeDtypeStruct((2 * levels, cols), F32),
            jax.ShapeDtypeStruct((2 * levels, cols), F32),
        ),
        in_specs=[VMEM_SPEC] * 9,
        out_specs=(VMEM_SPEC,) * 4,
        scratch_shapes=[VM(own[2].shape, F32), VM(own[2].shape, F32)],
        compiler_params=pltpu.CompilerParams(vmem_limit_bytes=LIMIT),
        name="fix",
    )(*in_hbm(fold_partner), *own, *far)


def order_kernel(cell_ref, place_ref, start_ref, mark_ref, base_ref, *, rows, cols, pairs):
    blocks = cell_ref.shape[0]
    count = blocks * 128
    half = count // 2
    cell = cell_ref[...].astype(F32)
    row = jnp.floor((cell + 0.5) * (1.0 / cols))
    hot = [jnp.where(row == float(r), 1.0, 0.0) for r in range(rows)]
    hot16 = jnp.concatenate([h.astype(BF16) for h in hot], axis=0)
    down = lax.broadcasted_iota(jnp.int32, (128, 128), 0)
    along = lax.broadcasted_iota(jnp.int32, (128, 128), 1)
    before = jnp.where(down < along, 1.0, 0.0).astype(BF16)
    after = jnp.where(along < down, 1.0, 0.0).astype(BF16)
    ones = jnp.ones((128, 128), BF16)
    within = dot_nn(hot16, before)
    totals = dot_nn(hot16, ones)
    carry = jnp.zeros((1, 128), F32)
    place = jnp.zeros(cell.shape, F32)
    per = 128 // blocks
    for c in range(rows // per):
        part = totals[c * 128 : (c + 1) * 128]
        base = dot_nn(after, part.astype(BF16)) + carry
        carry = base[127:128] + part[127:128]
        base_ref[c * 128 : (c + 1) * 128, :] = base
        spot = base + within[c * 128 : (c + 1) * 128]
        for j in range(per):
            place = place + hot[c * per + j] * spot[j * blocks : (j + 1) * blocks]
    place_ref[...] = place.astype(jnp.int32)
    starts = base_ref[pl.ds(0, rows, stride=blocks), :]
    high = jnp.floor(starts * (1.0 / 128))
    low = starts - 128 * high
    first = jnp.where(along[:8] == 0, 1.0, 0.0).astype(BF16)
    starts = 128 * dot_nt(first, high.astype(BF16)) + dot_nt(first, low.astype(BF16))
    start_ref[...] = jnp.full(start_ref.shape, count, jnp.int32)
    start_ref[:, 0:rows] = starts.astype(jnp.int32)
    for i in range(blocks):
        turned = jnp.broadcast_to(cell[i : i + 1], (128, 128)).T
        for j in range(128 // pairs):
            at = (j % 2) * half + (i * (128 // pairs) + j) // 2 * pairs
            mark_ref[at : at + pairs, :] = turned[j * pairs : (j + 1) * pairs]


def order(berg_cell, rows, cols, pairs):
    count = berg_cell.shape[0]
    blocks = count // 128
    return pl.pallas_call(
        functools.partial(order_kernel, rows=rows, cols=cols, pairs=pairs),
        out_shape=(
            jax.ShapeDtypeStruct((blocks, 128), jnp.int32),
            jax.ShapeDtypeStruct((8, 128), jnp.int32),
            jax.ShapeDtypeStruct((count, 128), F32),
        ),
        in_specs=[VMEM_SPEC],
        out_specs=(VMEM_SPEC,) * 3,
        scratch_shapes=[VM((blocks * rows, 128), F32)],
        compiler_params=pltpu.CompilerParams(vmem_limit_bytes=LIMIT),
        name="order",
    )(*in_hbm(berg_cell.reshape(blocks, 128)))


def final_kernel(
    place_ref, start_ref, recv_ref, mark_ref, part_hbm, wet_ref, fix_e, fix_w, fix_n, fix_s,
    out_hbm,
    rows_v, sorted_v, pv, wetf, acc, sem_i, sem_o, *, pairs,
):
    _, levels, rows, cols = pv.shape
    groups = rows // 8
    tiles = cols // 128
    maps = 2 * levels
    n_rows = recv_ref.shape[0]
    count = 2 * n_rows

    def load(g):
        here = pl.ds(pl.multiple_of(8 * g, 8), 8)
        return pltpu.make_async_copy(part_hbm.at[:, :, here], pv.at[:, :, here], sem_i.at[g])

    def store(g):
        here = pl.ds(pl.multiple_of(8 * g, 8), 8)
        return pltpu.make_async_copy(pv.at[:, :, here], out_hbm.at[:, :, here], sem_o.at[g])

    for g in range(groups):
        load(g).start()
    lane_all = lax.broadcasted_iota(jnp.int32, (128, 128), 1)
    low_half = lane_all < HALF
    cell_lane = lane_all == CELL_LANE

    def halves(i, _):
        at = pl.multiple_of(i * 128, 128)
        both = recv_ref[pl.ds(at, 128), :]
        high = both.astype(BF16).astype(F32)
        low = both - high
        for h, body in enumerate(
            (
                jnp.where(low_half, high, pltpu.roll(low, HALF, 1)),
                jnp.where(low_half, pltpu.roll(high, HALF, 1), low),
            )
        ):
            there = pl.ds(pl.multiple_of(h * n_rows + at, 128), 128)
            rows_v[there, :] = jnp.where(cell_lane, mark_ref[there, :], body)
        return _

    lax.fori_loop(0, n_rows // 128, halves, 0)
    wetf[...] = wet_ref[...].astype(F32)
    sorted_v[count:, :] = jnp.full((WINDOW, 128), -1.0, F32)

    def spread(i, _):
        first = pl.multiple_of(i * pairs, pairs)
        places = place_ref.at[pl.ds(2 * first, 2 * pairs)]
        for j in range(pairs):
            for h in range(2):
                to = places[h * pairs + j]
                sorted_v[pl.ds(to, 1), :] = rows_v[pl.ds(h * n_rows + first + j, 1), :]
        return _

    lax.fori_loop(0, n_rows // pairs, spread, 0)

    lane = lax.broadcasted_iota(jnp.int32, (8, 128), 1)
    lanef = lax.broadcasted_iota(jnp.int32, (WINDOW, 128), 1).astype(F32)

    def row_sources(r, at):
        at = pl.multiple_of(at, 8)
        lines = sorted_v[pl.ds(at, WINDOW), :]
        lhs = lines.astype(BF16).T
        near = jnp.broadcast_to(lines[:, CELL_LANE : CELL_LANE + 1], (WINDOW, 128)) - (r * cols).astype(F32)
        hot = [jnp.where(near - float(128 * c) == lanef, 1.0, 0.0).astype(BF16) for c in range(tiles)]
        both = dot_nn(lhs, jnp.concatenate(hot, axis=1))
        return both[:HALF] + both[HALF:]

    def group(g, _):
        here = pl.ds(pl.multiple_of(8 * g, 8), 8)
        firsts, windows = [], []
        for j in range(8):
            s = start_ref[0, 8 * g + j]
            e = start_ref[0, 8 * g + j + 1]
            first = lax.div(s, 8) * 8
            firsts.append(first)
            windows.append(lax.div(e - first + (WINDOW - 1), WINDOW))
        for j in range(8):
            made = row_sources(8 * g + j, firsts[j])
            for c in range(tiles):
                for m in range(0, maps, 8):
                    acc[c, pl.ds(m * 9 + j, 8, stride=9), :] = made[m : m + 8, c * 128 : (c + 1) * 128]
        most = functools.reduce(jnp.maximum, windows)

        @pl.when(most > 1)
        def _more():
            for j in range(8):

                def again(i, _, j=j):
                    made = row_sources(8 * g + j, firsts[j] + i * WINDOW)
                    for c in range(tiles):
                        for m in range(0, maps, 8):
                            acc[c, pl.ds(m * 9 + j, 8, stride=9), :] += made[
                                m : m + 8, c * 128 : (c + 1) * 128
                            ]
                    return _

                lax.fori_loop(1, windows[j], again, 0)

        load(g).wait()
        w = wetf[here, :]
        e_fix = fix_e[here, :]
        w_fix = fix_w[here, :]

        for edge, ref, at in ((groups - 1, fix_n, rows - 1), (0, fix_s, 0)):

            @pl.when(g == edge)
            def _edge_row(ref=ref, at=at):
                for m in range(maps):
                    t, k = m // levels, m % levels
                    pv[t, k, at : at + 1, :] += ref[m : m + 1, :]

        for m in range(maps):
            t, k = m // levels, m % levels
            at = t * TR_LANES + levels - 1 - k
            for c in range(tiles):
                lanes = slice(c * 128, (c + 1) * 128)
                value = pv[t, k, here, lanes] + w[:, lanes] * acc[c, 9 * m : 9 * m + 8, :]
                if c == 0:
                    value += jnp.where(lane == 0, pltpu.roll(w_fix, (128 - at) % 128, 1), 0.0)
                if c == tiles - 1:
                    value += jnp.where(lane == 127, pltpu.roll(e_fix, 127 - at, 1), 0.0)
                pv[t, k, here, lanes] = value
        store(g).start()
        return _

    lax.fori_loop(0, groups, group, 0)
    for g in range(groups):
        store(g).wait()


def finish(place, start, recv, mark, part, wet, fix, pairs):
    _, levels, rows, cols = part.shape
    dma = pltpu.SemaphoreType.DMA((rows // 8,))
    return pl.pallas_call(
        functools.partial(final_kernel, pairs=pairs),
        out_shape=jax.ShapeDtypeStruct(part.shape, F32),
        in_specs=[SMEM_SPEC] * 2 + [VMEM_SPEC] * 2 + [ANY_SPEC] + [VMEM_SPEC] * 5,
        out_specs=ANY_SPEC,
        scratch_shapes=[
            VM((2 * recv.shape[0], 128), F32),
            VM((2 * recv.shape[0] + WINDOW, 128), F32),
            VM(part.shape, F32),
            VM((rows, cols), F32),
            VM((cols // 128, 9 * HALF, 128), F32),
            dma,
            dma,
        ],
        compiler_params=pltpu.CompilerParams(vmem_limit_bytes=24 << 20),
        name="final",
    )(place, start, recv, mark, *in_hbm(part, wet), *fix)


def swap(value, axes, pairs):
    return lax.ppermute(value, axes, pairs + [(b, a) for a, b in pairs])


def shards(
    tracers, east_speed, north_speed, wet, fold_partner, bergs, berg_count, berg_cell, melt_map
):
    lon_count, lat_count = lax.axis_size("lon"), lax.axis_size("lat")
    levels, cols = tracers.shape[1], tracers.shape[3]

    melt = melt_rows(bergs, berg_count, melt_map)
    recv = lax.all_to_all(melt, ("lon", "lat"), split_axis=0, concat_axis=0, tiled=True)
    part, *own = stencil(tracers, east_speed, north_speed, wet)
    ew_a, ew_b, ns_a, ns_b = own

    lon_even = [(i, i + 1) for i in range(0, lon_count, 2)]
    lon_odd = [(i, (i + 1) % lon_count) for i in range(1, lon_count, 2)]

    def place(i, j):
        return i * lat_count + j

    lat_odd = [(place(i, j), place(i, j + 1)) for i in range(lon_count) for j in range(1, lat_count - 1, 2)]
    lat_odd += [
        (place(i, lat_count - 1), place(lon_count - 1 - i, lat_count - 1))
        for i in range(lon_count // 2)
    ]
    lat_even = [(j, j + 1) for j in range(0, lat_count, 2)]
    far = (
        swap(ew_a, "lon", lon_even),
        swap(ew_b, "lon", lon_odd),
        swap(ns_a, ("lon", "lat"), lat_odd),
        swap(ns_b, "lat", lat_even),
    )
    fix = fixes(fold_partner, own, far, levels)
    pairs = melt.shape[1]
    spots, start, mark = order(berg_cell, tracers.shape[2], cols, pairs)
    recv = recv.reshape(-1, 128)
    return finish(spots.reshape(-1), start, recv, mark, part, wet, fix, pairs)


def solution(mesh):
    in_specs = (
        P(None, None, "lat", "lon"),
        P(None, "lat", "lon"),
        P(None, "lat", "lon"),
        P("lat", "lon"),
        P("lon"),
        P(("lon", "lat"), None),
        P(("lon", "lat")),
        P(("lon", "lat")),
        P(),
    )
    out_specs = P(None, None, "lat", "lon")
    return jax.shard_map(shards, mesh=mesh, in_specs=in_specs, out_specs=out_specs, check_vma=False)
```

```python
import functools

import jax
import jax.numpy as jnp
from jax import lax
from jax.experimental import pallas as pl
from jax.experimental.pallas import tpu as pltpu
from jax.sharding import PartitionSpec as P

diffuse_h = 0.1
diffuse_v = 0.1
time_step = 0.5

F32 = jnp.float32
BF16 = jnp.bfloat16
VM = pltpu.VMEM
VMEM_SPEC = pl.BlockSpec(memory_space=pltpu.VMEM)
SMEM_SPEC = pl.BlockSpec(memory_space=pltpu.SMEM)
ANY_SPEC = pl.BlockSpec(memory_space=pl.ANY)
LIMIT = 12 << 20

TR_LANES = 32
HALF = 64
WET_LANE = 127
MELT_STEPS = 4
FIRSTS = (0, 1, 5, 13)
PARTS = (0, 2)
WINDOW = 128
CELL_LANE = 25


def in_hbm(*values):
    return tuple(pltpu.with_memory_space_constraint(v, pltpu.HBM) for v in values)


def split(value):
    high = value.astype(BF16)
    low = (value - high.astype(F32)).astype(BF16)
    return high, low


def dot_nt(a, b):
    return lax.dot_general(a, b, (((1,), (1,)), ((), ())), preferred_element_type=F32)


def dot_nn(a, b):
    return lax.dot_general(a, b, (((1,), (0,)), ((), ())), preferred_element_type=F32)


def melt_kernel(count_ref, berg_hbm, map_ref, out_hbm, berg_v, out_v, weight_ref, sem_i, sem_o):
    maps = map_ref.shape[0]
    width = berg_v.shape[1]
    owners, pairs = out_v.shape[:2]
    steps = MELT_STEPS
    per = owners // steps
    rows = per * pairs

    def load(i):
        span = pl.ds(i * 2 * rows, 2 * rows)
        return pltpu.make_async_copy(berg_hbm.at[span], berg_v.at[span], sem_i.at[i])

    def store(i):
        span = pl.ds(i * per, per)
        return pltpu.make_async_copy(out_v.at[span], out_hbm.at[span], sem_o)

    for i in range(steps):
        load(i).start()
    weight_ref[...] = jnp.zeros_like(weight_ref)
    for h in range(2):
        for t in range(2):
            place = h * HALF + t * TR_LANES
            weight_ref[place : place + maps // 2, h * width : (h + 1) * width] = map_ref[
                t * (maps // 2) : (t + 1) * (maps // 2), :
            ]
    w_high, w_low = split(weight_ref[...])
    w_both = jnp.concatenate([w_high, w_low], axis=0)
    lane = lax.broadcasted_iota(jnp.int32, (pairs, 128), 1)
    slot = lax.broadcasted_iota(jnp.int32, (pairs, 128), 0) + jnp.where(lane >= HALF, pairs, 0)
    for i in range(steps):
        load(i).wait()
        slots = berg_v[i * 2 * rows : (i + 1) * 2 * rows, :].reshape(per, 2, pairs, width)
        both = jnp.concatenate([slots[:, h].reshape(rows, width) for h in range(2)], axis=1)
        b_high, b_low = split(both)
        wide = dot_nt(b_high, w_both)
        made = wide[:, :128] + (wide[:, 128:] + dot_nt(b_low, w_high))
        for o in range(per):
            out_v[i * per + o] = jnp.where(
                slot < count_ref[i * per + o], made[o * pairs : (o + 1) * pairs], 0.0
            )
        store(i).start()
    pltpu.make_async_copy(out_v, out_hbm, sem_o).wait()


def melt_rows(bergs, berg_count, melt_map):
    owners = berg_count.shape[0]
    pairs = bergs.shape[0] // owners // 2
    width = bergs.shape[1]
    dma = pltpu.SemaphoreType.DMA((MELT_STEPS,))
    return pl.pallas_call(
        melt_kernel,
        out_shape=jax.ShapeDtypeStruct((owners, pairs, 128), F32),
        in_specs=[SMEM_SPEC, ANY_SPEC, VMEM_SPEC],
        out_specs=ANY_SPEC,
        scratch_shapes=[
            VM(bergs.shape, F32),
            VM((owners, pairs, 128), F32),
            VM((128, 2 * width), F32),
            dma,
            pltpu.SemaphoreType.DMA,
        ],
        compiler_params=pltpu.CompilerParams(vmem_limit_bytes=LIMIT),
        name="melt",
    )(*in_hbm(berg_count, bergs, melt_map.T))


def stencil_kernel(
    tr_hbm, ea_hbm, no_hbm, wet_ref,
    part_hbm, ew_a, ew_b, ns_a, ns_b,
    tv, ev, nv, ov, faces, wetf, packs, sem_t, sem_e, sem_n, sem_o,
):
    levels, rows, cols = ea_hbm.shape
    strips = rows // 8

    firsts = FIRSTS
    lasts = firsts[1:] + (levels,)

    def copies(c):
        span = pl.ds(firsts[c], lasts[c] - firsts[c])
        return (
            pltpu.make_async_copy(tr_hbm.at[:, span], tv.at[:, span], sem_t.at[c]),
            pltpu.make_async_copy(ea_hbm.at[span], ev.at[span], sem_e.at[c]),
            pltpu.make_async_copy(no_hbm.at[span], nv.at[span], sem_n.at[c]),
        )

    def result(c):
        span = pl.ds(firsts[c], lasts[c] - firsts[c])
        return pltpu.make_async_copy(ov.at[:, span], part_hbm.at[:, span], sem_o)

    for c in range(len(firsts)):
        for copy in copies(c):
            copy.start()
    odd_lon = lax.rem(lax.axis_index("lon"), 2)
    odd_lat = lax.rem(lax.axis_index("lat"), 2)
    row_a = odd_lat * (rows - 1)
    row_b = (1 - odd_lat) * (rows - 1)

    wet = wet_ref[...].astype(F32)
    wetf[...] = wet
    col = lax.broadcasted_iota(jnp.int32, (rows, cols), 1)
    row = lax.broadcasted_iota(jnp.int32, (rows, cols), 0)
    for at, face in enumerate(
        (
            jnp.where(col == cols - 1, 0.0, wet * pltpu.roll(wet, cols - 1, 1)),
            jnp.where(row == rows - 1, 0.0, wet * pltpu.roll(wet, rows - 1, 0)),
        )
    ):
        faces[2 * at] = (0.25 * time_step) * face
        faces[2 * at + 1] = (diffuse_h * time_step) * face
    lane_all = lax.broadcasted_iota(jnp.int32, (rows, 128), 1)
    ns_a[...] = jnp.zeros_like(ns_a)
    ns_b[...] = jnp.zeros_like(ns_b)
    ns_a[3 * levels : 3 * levels + 1, :] = wetf[pl.ds(row_a, 1), :]
    ns_b[3 * levels : 3 * levels + 1, :] = wetf[pl.ds(row_b, 1), :]

    lane = lax.broadcasted_iota(jnp.int32, (8, 128), 1)
    top = lax.broadcasted_iota(jnp.int32, (8, cols), 0) == 0
    last_lane = lane == 127
    packs[...] = jnp.zeros_like(packs)

    bottom = lax.broadcasted_iota(jnp.int32, (8, cols), 0) == 7

    def level(k, _):
        above = jnp.minimum(k + 1, levels - 1)
        below = jnp.maximum(k - 1, 0)
        for c in range(len(firsts)):

            @pl.when(k == max(firsts[c] - 1, 0))
            def _wait(c=c):
                for copy in copies(c):
                    copy.wait()

        carried = [None, None]
        fields = [tv.at[0, k], tv.at[1, k], nv.at[k]]
        own = [f[0:8, :] for f in fields]
        risen = [pltpu.roll(f, 7, 0) for f in own]
        for s in range(strips):
            here = pl.ds(8 * s, 8)
            if s < strips - 1:
                later = [f[8 * s + 8 : 8 * s + 16, :] for f in fields]
                later_risen = [pltpu.roll(f, 7, 0) for f in later]
                north = [jnp.where(bottom, b, a) for a, b in zip(risen, later_risen)]
            else:
                later, later_risen, north = own, risen, risen
            u = ev[k, here, :]
            v = own[2]
            w = wetf[here, :]
            u_next = pltpu.roll(u, cols - 1, 1)
            s_e = faces[0, here, :] * (u + u_next)
            s_n = faces[2, here, :] * (v + north[2])
            d_e = faces[1, here, :]
            d_n = faces[3, here, :]
            a_e, b_e, a_n, b_n = s_e + d_e, s_e - d_e, s_n + d_n, s_n - d_n
            ends = [None, None, (u_next, u)]
            for t in range(2):
                q = own[t]
                up = tv[t, above, here, :]
                dn = tv[t, below, here, :]
                q_next = pltpu.roll(q, cols - 1, 1)
                ends[t] = (q_next, q)
                fe = q * a_e + q_next * b_e
                fn = q * a_n + north[t] * b_n
                fw = pltpu.roll(fe, 1, 1)
                turned = pltpu.roll(fn, 1, 0)
                last = jnp.zeros_like(turned) if carried[t] is None else carried[t]
                fs = jnp.where(top, last, turned)
                carried[t] = turned
                mix = (1 - 2 * diffuse_v * time_step) * q + (diffuse_v * time_step) * (up + dn)
                ov[t, k, here, :] = w * ((mix - (fe - fw)) - (fn - fs))
            for at in range(3):
                for side in range(2):
                    end = ends[at][side][:, cols - 128 :]
                    packs[at, side, here, :] = jnp.where(
                        last_lane, end, pltpu.roll(packs[at, side, here, :], 127, 1)
                    )
            own, risen = later, later_risen
        for ref, at in ((ns_a, row_a), (ns_b, row_b)):
            ref[pl.ds(k, 1), :] = tv[0, k, pl.ds(at, 1), :]
            ref[pl.ds(levels + k, 1), :] = tv[1, k, pl.ds(at, 1), :]
            ref[pl.ds(2 * levels + k, 1), :] = nv[k, pl.ds(at, 1), :]
        for c in range(len(firsts)):

            @pl.when(k == lasts[c] - 1)
            def _send(c=c):
                result(c).start()

        return _

    lax.fori_loop(0, levels, level, 0)

    def packed(side, mask):
        value = jnp.where(lane_all == WET_LANE, mask, 0.0)
        for at, place in ((0, 0), (1, TR_LANES), (2, HALF), (2, HALF + TR_LANES)):
            here = (lane_all >= place) & (lane_all < place + levels)
            value = jnp.where(here, pltpu.roll(packs[at, side], levels + place, 1), value)
        return value

    is_odd = odd_lon == 1
    west, east = packed(0, wetf[:, 0:1]), packed(1, wetf[:, cols - 1 : cols])
    ew_a[...] = jnp.where(is_odd, west, east)
    ew_b[...] = jnp.where(is_odd, east, west)
    pltpu.make_async_copy(ov, part_hbm, sem_o).wait()


def stencil(tracers, east_speed, north_speed, wet):
    count, levels, rows, cols = tracers.shape
    edge_rows = -(-(3 * levels + 1) // 8) * 8
    dma = pltpu.SemaphoreType.DMA((len(FIRSTS),))
    return pl.pallas_call(
        stencil_kernel,
        out_shape=(
            pltpu.HBM(tracers.shape, F32),
            jax.ShapeDtypeStruct((rows, 128), F32),
            jax.ShapeDtypeStruct((rows, 128), F32),
            jax.ShapeDtypeStruct((edge_rows, cols), F32),
            jax.ShapeDtypeStruct((edge_rows, cols), F32),
        ),
        in_specs=[ANY_SPEC] * 3 + [VMEM_SPEC],
        out_specs=(ANY_SPEC,) + (VMEM_SPEC,) * 4,
        scratch_shapes=[
            VM(tracers.shape, F32),
            VM(east_speed.shape, F32),
            VM(north_speed.shape, F32),
            VM(tracers.shape, F32),
            VM((4, rows, cols), F32),
            VM((rows, cols), F32),
            VM((3, 2, rows, 128), F32),
            dma,
            dma,
            dma,
            pltpu.SemaphoreType.DMA,
        ],
        compiler_params=pltpu.CompilerParams(vmem_limit_bytes=20 << 20),
        name="stencil",
    )(*in_hbm(tracers, east_speed, north_speed, wet))


def fix_kernel(
    fold_ref, ew_a, ew_b, ns_a, ns_b, ew_a_in, ew_b_in, ns_a_in, ns_b_in,
    fix_c, fix_n, fix_s, north, south,
):
    levels = fix_n.shape[0] // 2
    cols = ns_a.shape[1]
    lon_count, lat_count = lax.axis_size("lon"), lax.axis_size("lat")
    lon_index, lat_index = lax.axis_index("lon"), lax.axis_index("lat")
    odd_lon = lax.rem(lon_index, 2) == 1
    odd_lat = lax.rem(lat_index, 2) == 1

    def faces(q, s, w, q_next, s_next, w_next):
        face = w * w_next
        speed = (0.25 * time_step) * face * (s + s_next)
        spread = (diffuse_h * time_step) * face
        return q * (speed + spread) + q_next * (speed - spread)

    def pick(odd, a, b):
        return jnp.where(odd, a, b)

    def column(value):
        return value, pltpu.roll(value, HALF, 1), value[:, WET_LANE : WET_LANE + 1]

    east_own = column(pick(odd_lon, ew_b[...], ew_a[...]))
    west_own = column(pick(odd_lon, ew_a[...], ew_b[...]))
    east_far = column(pick(odd_lon, ew_b_in[...], ew_a_in[...]))
    west_far = column(pick(odd_lon, ew_a_in[...], ew_b_in[...]))
    lane = lax.broadcasted_iota(jnp.int32, ew_a.shape, 1)
    first = lax.broadcasted_iota(jnp.int32, ew_a.shape, 0) * cols
    for at, value, cell in (
        (0, -(east_own[2] * faces(*east_own, *east_far)), first + (cols - 1)),
        (1, west_own[2] * faces(*west_far, *west_own), first),
    ):
        high = value.astype(BF16).astype(F32)
        body = jnp.where(lane < HALF, high, pltpu.roll(value - high, HALF, 1))
        fix_c[at] = jnp.where(lane == CELL_LANE, cell.astype(F32), body)


    north[...] = pick(odd_lat, ns_a_in[...], ns_b_in[...])
    south[...] = pick(odd_lat, ns_b_in[...], ns_a_in[...])

    @pl.when(lat_index == lat_count - 1)
    def _fold():
        picks = fold_ref[...].reshape(1, cols) - (lon_count - 1 - lon_index) * cols
        hot = (lax.broadcasted_iota(jnp.int32, (cols, cols), 0) == picks).astype(F32).astype(BF16)
        across = north[...]
        high, low = split(across)
        least = ((across - high.astype(F32)) - low.astype(F32)).astype(BF16)
        picked = dot_nn(high, hot) + (dot_nn(low, hot) + dot_nn(least, hot))
        at = lax.broadcasted_iota(jnp.int32, picked.shape, 0)
        is_speed = (at >= 2 * levels) & (at < 3 * levels)
        north[...] = jnp.where(is_speed, -picked, picked)

    def fields(value, t):
        return (
            value[t * levels : (t + 1) * levels],
            value[2 * levels : 3 * levels],
            value[3 * levels : 3 * levels + 1],
        )

    north_own = pick(odd_lat, ns_a[...], ns_b[...])
    south_own = pick(odd_lat, ns_b[...], ns_a[...])
    north_far, south_far = north[...], south[...]
    for t in range(2):
        at = pl.ds(t * levels, levels)
        own = fields(north_own, t)
        fix_n[at, :] = -(own[2] * faces(*own, *fields(north_far, t)))
        own = fields(south_own, t)
        fix_s[at, :] = own[2] * faces(*fields(south_far, t), *own)


def fixes(fold_partner, own, far, levels):
    rows, cols = own[0].shape[0], own[2].shape[1]
    return pl.pallas_call(
        fix_kernel,
        out_shape=(
            jax.ShapeDtypeStruct((2, rows, 128), F32),
            jax.ShapeDtypeStruct((2 * levels, cols), F32),
            jax.ShapeDtypeStruct((2 * levels, cols), F32),
        ),
        in_specs=[VMEM_SPEC] * 9,
        out_specs=(VMEM_SPEC,) * 3,
        scratch_shapes=[VM(own[2].shape, F32), VM(own[2].shape, F32)],
        compiler_params=pltpu.CompilerParams(vmem_limit_bytes=LIMIT),
        name="fix",
    )(*in_hbm(fold_partner), *own, *far)


def order_kernel(cell_ref, place_ref, start_ref, mark_ref, base_ref, *, rows, cols, pairs):
    blocks = cell_ref.shape[0]
    count = blocks * 128
    half = count // 2
    cell = cell_ref[...].astype(F32)
    row = jnp.floor((cell + 0.5) * (1.0 / cols))
    hot = [jnp.where(row == float(r), 1.0, 0.0) for r in range(rows)]
    hot16 = jnp.concatenate([h.astype(BF16) for h in hot], axis=0)
    down = lax.broadcasted_iota(jnp.int32, (128, 128), 0)
    along = lax.broadcasted_iota(jnp.int32, (128, 128), 1)
    before = jnp.where(down < along, 1.0, 0.0).astype(BF16)
    after = jnp.where(along < down, 1.0, 0.0).astype(BF16)
    ones = jnp.ones((128, 128), BF16)
    within = dot_nn(hot16, before)
    totals = dot_nn(hot16, ones)
    carry = jnp.zeros((1, 128), F32)
    place = jnp.zeros(cell.shape, F32)
    per = 128 // blocks
    for c in range(rows // per):
        part = totals[c * 128 : (c + 1) * 128]
        base = dot_nn(after, part.astype(BF16)) + carry
        carry = base[127:128] + part[127:128]
        base_ref[c * 128 : (c + 1) * 128, :] = base
        spot = base + within[c * 128 : (c + 1) * 128]
        for j in range(per):
            extra = 2.0 * (c * per + j + 1)
            place = place + hot[c * per + j] * (spot[j * blocks : (j + 1) * blocks] + extra)
    place_ref[...] = place.astype(jnp.int32)
    starts = base_ref[pl.ds(0, rows, stride=blocks), :]
    high = jnp.floor(starts * (1.0 / 128))
    low = starts - 128 * high
    first = jnp.where(along[:8] == 0, 1.0, 0.0).astype(BF16)
    starts = 128 * dot_nt(first, high.astype(BF16)) + dot_nt(first, low.astype(BF16))
    extra = 2.0 * lax.broadcasted_iota(jnp.int32, starts.shape, 1).astype(F32)
    start_ref[...] = jnp.full(start_ref.shape, count + 2 * rows, jnp.int32)
    start_ref[:, 0:rows] = (starts + extra).astype(jnp.int32)
    for i in range(blocks):
        turned = jnp.broadcast_to(cell[i : i + 1], (128, 128)).T
        for j in range(128 // pairs):
            at = (j % 2) * half + (i * (128 // pairs) + j) // 2 * pairs
            mark_ref[at : at + pairs, :] = turned[j * pairs : (j + 1) * pairs]


def order(berg_cell, rows, cols, pairs):
    count = berg_cell.shape[0]
    blocks = count // 128
    return pl.pallas_call(
        functools.partial(order_kernel, rows=rows, cols=cols, pairs=pairs),
        out_shape=(
            jax.ShapeDtypeStruct((blocks, 128), jnp.int32),
            jax.ShapeDtypeStruct((8, 128), jnp.int32),
            jax.ShapeDtypeStruct((count, 128), F32),
        ),
        in_specs=[VMEM_SPEC],
        out_specs=(VMEM_SPEC,) * 3,
        scratch_shapes=[VM((blocks * rows, 128), F32)],
        compiler_params=pltpu.CompilerParams(vmem_limit_bytes=LIMIT),
        name="order",
    )(*in_hbm(berg_cell.reshape(blocks, 128)))


def final_kernel(
    place_ref, start_ref, recv_ref, mark_ref, part_hbm, wet_ref, fix_c, fix_n, fix_s,
    out_hbm,
    rows_v, sorted_v, pv, wetf, acc, sem_i, sem_o, *, pairs,
):
    _, levels, rows, cols = pv.shape
    groups = rows // 8
    tiles = cols // 128
    maps = 2 * levels
    n_rows = recv_ref.shape[0]
    count = 2 * (n_rows + rows)

    def load(i):
        here = pl.ds(8 * PARTS[i], 8 * ((PARTS[1:] + (groups,))[i] - PARTS[i]))
        return pltpu.make_async_copy(part_hbm.at[:, :, here], pv.at[:, :, here], sem_i.at[i])

    def store(g):
        here = pl.ds(pl.multiple_of(8 * g, 8), 8)
        return pltpu.make_async_copy(pv.at[:, :, here], out_hbm.at[:, :, here], sem_o)

    for i in range(len(PARTS)):
        load(i).start()
    lane_all = lax.broadcasted_iota(jnp.int32, (128, 128), 1)
    low_half = lane_all < HALF
    cell_lane = lane_all == CELL_LANE

    def halves(i, _):
        at = pl.multiple_of(i * 128, 128)
        both = recv_ref[pl.ds(at, 128), :]
        high = both.astype(BF16).astype(F32)
        low = both - high
        for h, body in enumerate(
            (
                jnp.where(low_half, high, pltpu.roll(low, HALF, 1)),
                jnp.where(low_half, pltpu.roll(high, HALF, 1), low),
            )
        ):
            there = pl.ds(pl.multiple_of(h * n_rows + at, 128), 128)
            rows_v[there, :] = jnp.where(cell_lane, mark_ref[there, :], body)
        return _

    lax.fori_loop(0, n_rows // 128, halves, 0)
    wetf[...] = wet_ref[...].astype(F32)
    sorted_v[count:, :] = jnp.full((WINDOW, 128), -1.0, F32)

    def spread(i, _):
        first = pl.multiple_of(i * pairs, pairs)
        places = place_ref.at[pl.ds(2 * first, 2 * pairs)]
        for j in range(pairs):
            for h in range(2):
                to = places[h * pairs + j]
                sorted_v[pl.ds(to, 1), :] = rows_v[pl.ds(h * n_rows + first + j, 1), :]
        return _

    lax.fori_loop(0, n_rows // pairs, spread, 0)
    for r in range(rows):
        first = start_ref[0, r]
        for h in range(2):
            sorted_v[pl.ds(first + h, 1), :] = fix_c[h, r : r + 1, :]

    lanef = lax.broadcasted_iota(jnp.int32, (WINDOW, 128), 1).astype(F32)

    def row_sources(r, at):
        at = pl.multiple_of(at, 8)
        lines = sorted_v[pl.ds(at, WINDOW), :]
        lhs = lines.astype(BF16).T
        near = jnp.broadcast_to(lines[:, CELL_LANE : CELL_LANE + 1], (WINDOW, 128)) - (r * cols).astype(F32)
        hot = [jnp.where(near - float(128 * c) == lanef, 1.0, 0.0).astype(BF16) for c in range(tiles)]
        both = dot_nn(lhs, jnp.concatenate(hot, axis=1))
        return both[:HALF] + both[HALF:]

    def group(g, _):
        here = pl.ds(pl.multiple_of(8 * g, 8), 8)
        firsts, windows = [], []
        for j in range(8):
            s = start_ref[0, 8 * g + j]
            e = start_ref[0, 8 * g + j + 1]
            first = lax.div(s, 8) * 8
            firsts.append(first)
            windows.append(lax.div(e - first + (WINDOW - 1), WINDOW))
        for j in range(8):
            made = row_sources(8 * g + j, firsts[j])
            for c in range(tiles):
                for m in range(0, HALF, 8):
                    acc[c, pl.ds(m * 9 + j, 8, stride=9), :] = made[m : m + 8, c * 128 : (c + 1) * 128]
        most = functools.reduce(jnp.maximum, windows)

        @pl.when(most > 1)
        def _more():
            for j in range(8):

                def again(i, _, j=j):
                    made = row_sources(8 * g + j, firsts[j] + i * WINDOW)
                    for c in range(tiles):
                        for m in range(0, HALF, 8):
                            acc[c, pl.ds(m * 9 + j, 8, stride=9), :] += made[
                                m : m + 8, c * 128 : (c + 1) * 128
                            ]
                    return _

                lax.fori_loop(1, windows[j], again, 0)

        for i in range(len(PARTS)):

            @pl.when(g == PARTS[i])
            def _wait(i=i):
                load(i).wait()

        w = wetf[here, :]

        for edge, ref, at in ((groups - 1, fix_n, rows - 1), (0, fix_s, 0)):

            @pl.when(g == edge)
            def _edge_row(ref=ref, at=at):
                for m in range(maps):
                    t, k = m // levels, m % levels
                    pv[t, k, at : at + 1, :] += ref[m : m + 1, :]

        for m in range(maps):
            t, k = m // levels, m % levels
            at = 9 * (t * TR_LANES + k)
            for c in range(tiles):
                lanes = slice(c * 128, (c + 1) * 128)
                pv[t, k, here, lanes] += w[:, lanes] * acc[c, at : at + 8, :]
        store(g).start()
        return _

    lax.fori_loop(0, groups, group, 0)
    pltpu.make_async_copy(pv, out_hbm, sem_o).wait()


def finish(place, start, recv, mark, part, wet, fix, pairs):
    _, levels, rows, cols = part.shape
    return pl.pallas_call(
        functools.partial(final_kernel, pairs=pairs),
        out_shape=jax.ShapeDtypeStruct(part.shape, F32),
        in_specs=[SMEM_SPEC] * 2 + [VMEM_SPEC] * 2 + [ANY_SPEC] + [VMEM_SPEC] * 4,
        out_specs=ANY_SPEC,
        scratch_shapes=[
            VM((2 * recv.shape[0], 128), F32),
            VM((2 * recv.shape[0] + 2 * rows + WINDOW, 128), F32),
            VM(part.shape, F32),
            VM((rows, cols), F32),
            VM((cols // 128, 9 * HALF, 128), F32),
            pltpu.SemaphoreType.DMA((len(PARTS),)),
            pltpu.SemaphoreType.DMA,
        ],
        compiler_params=pltpu.CompilerParams(vmem_limit_bytes=24 << 20),
        name="final",
    )(place, start, recv, mark, *in_hbm(part, wet), *fix)


def swap(value, axes, pairs):
    return lax.ppermute(value, axes, pairs + [(b, a) for a, b in pairs])


def shards(
    tracers, east_speed, north_speed, wet, fold_partner, bergs, berg_count, berg_cell, melt_map
):
    lon_count, lat_count = lax.axis_size("lon"), lax.axis_size("lat")
    levels, cols = tracers.shape[1], tracers.shape[3]

    melt = melt_rows(bergs, berg_count, melt_map)
    recv = lax.all_to_all(melt, ("lon", "lat"), split_axis=0, concat_axis=0, tiled=True)
    part, *own = stencil(tracers, east_speed, north_speed, wet)
    ew_a, ew_b, ns_a, ns_b = own

    lon_even = [(i, i + 1) for i in range(0, lon_count, 2)]
    lon_odd = [(i, (i + 1) % lon_count) for i in range(1, lon_count, 2)]

    def place(i, j):
        return i * lat_count + j

    lat_odd = [(place(i, j), place(i, j + 1)) for i in range(lon_count) for j in range(1, lat_count - 1, 2)]
    lat_odd += [
        (place(i, lat_count - 1), place(lon_count - 1 - i, lat_count - 1))
        for i in range(lon_count // 2)
    ]
    lat_even = [(j, j + 1) for j in range(0, lat_count, 2)]
    far = (
        swap(ew_a, "lon", lon_even),
        swap(ew_b, "lon", lon_odd),
        swap(ns_a, ("lon", "lat"), lat_odd),
        swap(ns_b, "lat", lat_even),
    )
    fix = fixes(fold_partner, own, far, levels)
    pairs = melt.shape[1]
    spots, start, mark = order(berg_cell, tracers.shape[2], cols, pairs)
    recv = recv.reshape(-1, 128)
    return finish(spots.reshape(-1), start, recv, mark, part, wet, fix, pairs)


def solution(mesh):
    in_specs = (
        P(None, None, "lat", "lon"),
        P(None, "lat", "lon"),
        P(None, "lat", "lon"),
        P("lat", "lon"),
        P("lon"),
        P(("lon", "lat"), None),
        P(("lon", "lat")),
        P(("lon", "lat")),
        P(),
    )
    out_specs = P(None, None, "lat", "lon")
    return jax.shard_map(shards, mesh=mesh, in_specs=in_specs, out_specs=out_specs, check_vma=False)
```

```python
import functools

import jax
import jax.numpy as jnp
from jax import lax
from jax.experimental import pallas as pl
from jax.experimental.pallas import tpu as pltpu
from jax.sharding import PartitionSpec as P

diffuse_h = 0.1
diffuse_v = 0.1
time_step = 0.5

F32 = jnp.float32
BF16 = jnp.bfloat16
VM = pltpu.VMEM
VMEM_SPEC = pl.BlockSpec(memory_space=pltpu.VMEM)
SMEM_SPEC = pl.BlockSpec(memory_space=pltpu.SMEM)
ANY_SPEC = pl.BlockSpec(memory_space=pl.ANY)
LIMIT = 12 << 20

EAST_WET = 126
WEST_WET = 127
MELT_STEPS = 4
FIRSTS = (0, 1, 4, 9, 16)
SENDS = (6, 12, 18, 22, 24)
PARTS = (0, 2)
WINDOW = 128
CELL_LANE = 100


def in_hbm(*values):
    return tuple(pltpu.with_memory_space_constraint(v, pltpu.HBM) for v in values)


def split(value):
    high = value.astype(BF16)
    low = (value - high.astype(F32)).astype(BF16)
    return high, low


def dot_nt(a, b):
    return lax.dot_general(a, b, (((1,), (1,)), ((), ())), preferred_element_type=F32)


def dot_nn(a, b):
    return lax.dot_general(a, b, (((1,), (0,)), ((), ())), preferred_element_type=F32)


def melt_kernel(
    count_hbm, berg_hbm, map_hbm, out_hbm,
    berg_v, out_v, weight_ref, map_v, count_ref, sem_i, sem_o, sem_s,
):
    maps = map_v.shape[0]
    width = berg_v.shape[1]
    owners, pairs = out_v.shape[:2]
    steps = MELT_STEPS
    per = owners // steps
    rows = per * pairs

    def load(i):
        span = pl.ds(i * 2 * rows, 2 * rows)
        return pltpu.make_async_copy(berg_hbm.at[span], berg_v.at[span], sem_i.at[i])

    def store(i):
        span = pl.ds(i * per, per)
        return pltpu.make_async_copy(out_v.at[span], out_hbm.at[span], sem_o)

    small = (
        pltpu.make_async_copy(map_hbm, map_v, sem_s.at[0]),
        pltpu.make_async_copy(count_hbm, count_ref, sem_s.at[1]),
    )
    for copy in small:
        copy.start()
    for i in range(steps):
        load(i).start()
    for copy in small:
        copy.wait()
    weight_ref[...] = jnp.zeros_like(weight_ref)
    for h in range(2):
        weight_ref[h, pl.ds(h, maps, stride=2), :] = map_v[...]
    w_high, w_low = split(jnp.concatenate([weight_ref[0], weight_ref[1]], axis=1))
    w_both = jnp.concatenate([w_high, w_low], axis=0)
    lane = lax.broadcasted_iota(jnp.int32, (pairs, 128), 1)
    slot = lax.broadcasted_iota(jnp.int32, (pairs, 128), 0) + pairs * jnp.bitwise_and(lane, 1)
    for i in range(steps):
        load(i).wait()
        slots = berg_v[i * 2 * rows : (i + 1) * 2 * rows, :].reshape(per, 2, pairs, width)
        both = jnp.concatenate([slots[:, h].reshape(rows, width) for h in range(2)], axis=1)
        b_high, b_low = split(both)
        wide = dot_nt(b_high, w_both)
        made = wide[:, :128] + (wide[:, 128:] + dot_nt(b_low, w_high))
        for o in range(per):
            out_v[i * per + o] = jnp.where(
                slot < count_ref[i * per + o], made[o * pairs : (o + 1) * pairs], 0.0
            )
        store(i).start()
    pltpu.make_async_copy(out_v, out_hbm, sem_o).wait()


def melt_rows(bergs, berg_count, melt_map):
    owners = berg_count.shape[0]
    pairs = bergs.shape[0] // owners // 2
    width = bergs.shape[1]
    dma = pltpu.SemaphoreType.DMA((MELT_STEPS,))
    return pl.pallas_call(
        melt_kernel,
        out_shape=jax.ShapeDtypeStruct((owners, pairs, 128), F32),
        in_specs=[ANY_SPEC] * 3,
        out_specs=ANY_SPEC,
        scratch_shapes=[
            VM(bergs.shape, F32),
            VM((owners, pairs, 128), F32),
            VM((2, 128, width), F32),
            VM(melt_map.shape[::-1], F32),
            pltpu.SMEM((owners,), jnp.int32),
            dma,
            pltpu.SemaphoreType.DMA,
            pltpu.SemaphoreType.DMA((2,)),
        ],
        compiler_params=pltpu.CompilerParams(vmem_limit_bytes=LIMIT),
        name="melt",
    )(*in_hbm(berg_count, bergs, melt_map.T))


def stencil_kernel(
    tr_hbm, ea_hbm, no_hbm, wet_hbm,
    part_hbm, ew, ns_a, ns_b,
    tv, ev, nv, ov, faces, wetf, wet_v, sem_t, sem_e, sem_n, sem_o, sem_w,
):
    levels, rows, cols = ea_hbm.shape
    strips = rows // 8

    firsts = FIRSTS
    lasts = firsts[1:] + (levels,)
    sent = (0,) + SENDS + (levels,)

    def copies(c):
        span = pl.ds(firsts[c], lasts[c] - firsts[c])
        return (
            pltpu.make_async_copy(tr_hbm.at[:, span], tv.at[:, span], sem_t.at[c]),
            pltpu.make_async_copy(ea_hbm.at[span], ev.at[span], sem_e.at[c]),
            pltpu.make_async_copy(no_hbm.at[span], nv.at[span], sem_n.at[c]),
        )

    def result(c):
        span = pl.ds(sent[c], sent[c + 1] - sent[c])
        return pltpu.make_async_copy(ov.at[:, span], part_hbm.at[:, span], sem_o)

    mask_copy = pltpu.make_async_copy(wet_hbm, wet_v, sem_w)
    mask_copy.start()
    for c in range(len(firsts)):
        for copy in copies(c):
            copy.start()
    mask_copy.wait()
    odd_lat = lax.rem(lax.axis_index("lat"), 2)
    row_a = odd_lat * (rows - 1)
    row_b = (1 - odd_lat) * (rows - 1)

    wet = wet_v[...].astype(F32)
    wetf[...] = wet
    col = lax.broadcasted_iota(jnp.int32, (rows, cols), 1)
    row = lax.broadcasted_iota(jnp.int32, (rows, cols), 0)
    for at, face in enumerate(
        (
            jnp.where(col == cols - 1, 0.0, wet * pltpu.roll(wet, cols - 1, 1)),
            jnp.where(row == rows - 1, 0.0, wet * pltpu.roll(wet, rows - 1, 0)),
        )
    ):
        faces[2 * at] = (0.25 * time_step) * face
        faces[2 * at + 1] = (diffuse_h * time_step) * face
    lane_all = lax.broadcasted_iota(jnp.int32, (rows, 128), 1)
    ns_a[...] = jnp.zeros_like(ns_a)
    ns_b[...] = jnp.zeros_like(ns_b)
    ns_a[3 * levels : 3 * levels + 1, :] = wetf[pl.ds(row_a, 1), :]
    ns_b[3 * levels : 3 * levels + 1, :] = wetf[pl.ds(row_b, 1), :]

    lane = lax.broadcasted_iota(jnp.int32, (8, 128), 1)
    top = lax.broadcasted_iota(jnp.int32, (8, cols), 0) == 0

    bottom = lax.broadcasted_iota(jnp.int32, (8, cols), 0) == 7

    def level(k, _):
        above = jnp.minimum(k + 1, levels - 1)
        below = jnp.maximum(k - 1, 0)
        for c in range(len(firsts)):

            @pl.when(k == max(firsts[c] - 1, 0))
            def _wait(c=c):
                for copy in copies(c):
                    copy.wait()

        carried = [None, None]
        fields = [tv.at[0, k], tv.at[1, k], nv.at[k]]
        own = [f[0:8, :] for f in fields]
        risen = [pltpu.roll(f, 7, 0) for f in own]
        for s in range(strips):
            here = pl.ds(8 * s, 8)
            if s < strips - 1:
                later = [f[8 * s + 8 : 8 * s + 16, :] for f in fields]
                later_risen = [pltpu.roll(f, 7, 0) for f in later]
                north = [jnp.where(bottom, b, a) for a, b in zip(risen, later_risen)]
            else:
                later, later_risen, north = own, risen, risen
            u = ev[k, here, :]
            v = own[2]
            w = wetf[here, :]
            u_next = pltpu.roll(u, cols - 1, 1)
            s_e = faces[0, here, :] * (u + u_next)
            s_n = faces[2, here, :] * (v + north[2])
            d_e = faces[1, here, :]
            d_n = faces[3, here, :]
            a_e, b_e, a_n, b_n = s_e + d_e, s_e - d_e, s_n + d_n, s_n - d_n
            for t in range(2):
                q = own[t]
                up = tv[t, above, here, :]
                dn = tv[t, below, here, :]
                q_next = pltpu.roll(q, cols - 1, 1)
                fe = q * a_e + q_next * b_e
                fn = q * a_n + north[t] * b_n
                fw = pltpu.roll(fe, 1, 1)
                turned = pltpu.roll(fn, 1, 0)
                last = jnp.zeros_like(turned) if carried[t] is None else carried[t]
                fs = jnp.where(top, last, turned)
                carried[t] = turned
                mix = (1 - 2 * diffuse_v * time_step) * q + (diffuse_v * time_step) * (up + dn)
                ov[t, k, here, :] = w * ((mix - (fe - fw)) - (fn - fs))
            own, risen = later, later_risen
        for ref, at in ((ns_a, row_a), (ns_b, row_b)):
            ref[pl.ds(k, 1), :] = tv[0, k, pl.ds(at, 1), :]
            ref[pl.ds(levels + k, 1), :] = tv[1, k, pl.ds(at, 1), :]
            ref[pl.ds(2 * levels + k, 1), :] = nv[k, pl.ds(at, 1), :]
        for c in range(len(sent) - 1):

            @pl.when(k == sent[c + 1] - 1)
            def _send(c=c):
                result(c).start()

        return _

    lax.fori_loop(0, levels, level, 0)

    west_lanes = lane < 64
    ends = (lane == 0) | (lane == 127)

    def inserted(packs, field):
        made = []
        for s, pack in enumerate(packs):
            here = pl.ds(8 * s, 8)
            both = jnp.where(west_lanes, field[here, 0:128], field[here, cols - 128 : cols])
            made.append(jnp.where(ends, both, pltpu.roll(pack, 2, 1)))
        return tuple(made)

    def second(i, packs):
        return inserted(packs, tv.at[1, levels - 1 - i])

    def first(i, packs):
        k = levels - 1 - i
        return inserted(packs[0], tv.at[0, k]), inserted(packs[1], ev.at[k])

    blank = (jnp.zeros((8, 128), F32),) * strips
    fields = lax.fori_loop(0, levels, second, blank)
    fields, speeds = lax.fori_loop(0, levels, first, (fields, blank))
    fields = pltpu.roll(jnp.concatenate(fields, axis=0), 1, 1)
    fields = jnp.where(lane_all == EAST_WET, wetf[:, cols - 1 : cols], fields)
    ew[:, 0:128] = jnp.where(lane_all == WEST_WET, wetf[:, 0:1], fields)
    speeds = jnp.concatenate(speeds, axis=0)
    ew[:, 128:256] = jnp.where(
        lane_all < 2 * levels, pltpu.roll(speeds, 1, 1), pltpu.roll(speeds, 2 * levels + 1, 1)
    )
    pltpu.make_async_copy(ov, part_hbm, sem_o).wait()


def stencil(tracers, east_speed, north_speed, wet):
    count, levels, rows, cols = tracers.shape
    edge_rows = -(-(3 * levels + 1) // 8) * 8
    dma = pltpu.SemaphoreType.DMA((len(FIRSTS),))
    return pl.pallas_call(
        stencil_kernel,
        out_shape=(
            pltpu.HBM(tracers.shape, F32),
            jax.ShapeDtypeStruct((rows, 256), F32),
            jax.ShapeDtypeStruct((edge_rows, cols), F32),
            jax.ShapeDtypeStruct((edge_rows, cols), F32),
        ),
        in_specs=[ANY_SPEC] * 4,
        out_specs=(ANY_SPEC,) + (VMEM_SPEC,) * 3,
        scratch_shapes=[
            VM(tracers.shape, F32),
            VM(east_speed.shape, F32),
            VM(north_speed.shape, F32),
            VM(tracers.shape, F32),
            VM((4, rows, cols), F32),
            VM((rows, cols), F32),
            VM((rows, cols), jnp.int32),
            dma,
            dma,
            dma,
            pltpu.SemaphoreType.DMA,
            pltpu.SemaphoreType.DMA,
        ],
        compiler_params=pltpu.CompilerParams(vmem_limit_bytes=20 << 20),
        name="stencil",
    )(*in_hbm(tracers, east_speed, north_speed, wet))


def fix_kernel(
    fold_ref, ew, ns_a, ns_b, ew_a_in, ew_b_in, ns_a_in, ns_b_in,
    fix_c, fix_n, fix_s, north, south,
):
    levels = fix_n.shape[0] // 2
    cols = ns_a.shape[1]
    lon_count, lat_count = lax.axis_size("lon"), lax.axis_size("lat")
    lon_index, lat_index = lax.axis_index("lon"), lax.axis_index("lat")
    odd_lon = lax.rem(lon_index, 2) == 1
    odd_lat = lax.rem(lat_index, 2) == 1

    def faces(q, s, w, q_next, s_next, w_next):
        face = w * w_next
        speed = (0.25 * time_step) * face * (s + s_next)
        spread = (diffuse_h * time_step) * face
        return q * (speed + spread) + q_next * (speed - spread)

    def pick(odd, a, b):
        return jnp.where(odd, a, b)

    def column(value, turn, mask):
        field, speed = value[:, 0:128], value[:, 128:256]
        if turn:
            field, speed = pltpu.roll(field, turn, 1), pltpu.roll(speed, turn, 1)
        return field, speed, value[:, mask : mask + 1]

    own, far_a, far_b = ew[...], ew_a_in[...], ew_b_in[...]
    east_own = column(own, 0, EAST_WET)
    west_own = column(own, 0, WEST_WET)
    east_far = column(pick(odd_lon, far_b, far_a), 127, WEST_WET)
    west_far = column(pick(odd_lon, far_a, far_b), 1, EAST_WET)
    lane = lax.broadcasted_iota(jnp.int32, (own.shape[0], 128), 1)
    even = jnp.bitwise_and(lane, 1) == 0
    first = lax.broadcasted_iota(jnp.int32, lane.shape, 0) * cols
    for at, value, cell in (
        (0, -(east_own[2] * faces(*east_own, *east_far)), first + (cols - 1)),
        (1, west_own[2] * faces(*west_far, *west_own), first),
    ):
        high = value.astype(BF16).astype(F32)
        low = value - high
        if at:
            body = jnp.where(even, pltpu.roll(high, 127, 1), low)
        else:
            body = jnp.where(even, high, pltpu.roll(low, 1, 1))
        fix_c[at] = jnp.where(lane == CELL_LANE, cell.astype(F32), body)

    north[...] = pick(odd_lat, ns_a_in[...], ns_b_in[...])
    south[...] = pick(odd_lat, ns_b_in[...], ns_a_in[...])

    @pl.when(lat_index == lat_count - 1)
    def _fold():
        picks = fold_ref[...].reshape(1, cols) - (lon_count - 1 - lon_index) * cols
        hot = (lax.broadcasted_iota(jnp.int32, (cols, cols), 0) == picks).astype(F32).astype(BF16)
        across = north[...]
        high, low = split(across)
        least = ((across - high.astype(F32)) - low.astype(F32)).astype(BF16)
        picked = dot_nn(high, hot) + (dot_nn(low, hot) + dot_nn(least, hot))
        at = lax.broadcasted_iota(jnp.int32, picked.shape, 0)
        is_speed = (at >= 2 * levels) & (at < 3 * levels)
        north[...] = jnp.where(is_speed, -picked, picked)

    def fields(value, t):
        return (
            value[t * levels : (t + 1) * levels],
            value[2 * levels : 3 * levels],
            value[3 * levels : 3 * levels + 1],
        )

    north_own = pick(odd_lat, ns_a[...], ns_b[...])
    south_own = pick(odd_lat, ns_b[...], ns_a[...])
    north_far, south_far = north[...], south[...]
    for t in range(2):
        at = pl.ds(t * levels, levels)
        own = fields(north_own, t)
        fix_n[at, :] = -(own[2] * faces(*own, *fields(north_far, t)))
        own = fields(south_own, t)
        fix_s[at, :] = own[2] * faces(*fields(south_far, t), *own)


def fixes(fold_partner, own, far, levels):
    rows, cols = own[0].shape[0], own[1].shape[1]
    return pl.pallas_call(
        fix_kernel,
        out_shape=(
            jax.ShapeDtypeStruct((2, rows, 128), F32),
            jax.ShapeDtypeStruct((2 * levels, cols), F32),
            jax.ShapeDtypeStruct((2 * levels, cols), F32),
        ),
        in_specs=[VMEM_SPEC] * 8,
        out_specs=(VMEM_SPEC,) * 3,
        scratch_shapes=[VM(own[1].shape, F32), VM(own[1].shape, F32)],
        compiler_params=pltpu.CompilerParams(vmem_limit_bytes=LIMIT),
        name="fix",
    )(*in_hbm(fold_partner), *own, *far)


def order_kernel(cell_ref, place_ref, start_ref, mark_ref, base_ref, *, rows, cols, pairs):
    blocks = cell_ref.shape[0]
    count = blocks * 128
    half = count // 2
    cell = cell_ref[...].astype(F32)
    row = jnp.floor((cell + 0.5) * (1.0 / cols))
    hot = [jnp.where(row == float(r), 1.0, 0.0) for r in range(rows)]
    hot16 = jnp.concatenate([h.astype(BF16) for h in hot], axis=0)
    down = lax.broadcasted_iota(jnp.int32, (128, 128), 0)
    along = lax.broadcasted_iota(jnp.int32, (128, 128), 1)
    before = jnp.where(down < along, 1.0, 0.0).astype(BF16)
    after = jnp.where(along < down, 1.0, 0.0).astype(BF16)
    ones = jnp.ones((128, 128), BF16)
    within = dot_nn(hot16, before)
    totals = dot_nn(hot16, ones)
    carry = jnp.zeros((1, 128), F32)
    place = jnp.zeros(cell.shape, F32)
    per = 128 // blocks
    for c in range(rows // per):
        part = totals[c * 128 : (c + 1) * 128]
        base = dot_nn(after, part.astype(BF16)) + carry
        carry = base[127:128] + part[127:128]
        base_ref[c * 128 : (c + 1) * 128, :] = base
        spot = base + within[c * 128 : (c + 1) * 128]
        for j in range(per):
            extra = 2.0 * (c * per + j + 1)
            place = place + hot[c * per + j] * (spot[j * blocks : (j + 1) * blocks] + extra)
    place_ref[...] = place.astype(jnp.int32)
    starts = base_ref[pl.ds(0, rows, stride=blocks), :]
    high = jnp.floor(starts * (1.0 / 128))
    low = starts - 128 * high
    first = jnp.where(along[:8] == 0, 1.0, 0.0).astype(BF16)
    starts = 128 * dot_nt(first, high.astype(BF16)) + dot_nt(first, low.astype(BF16))
    extra = 2.0 * lax.broadcasted_iota(jnp.int32, starts.shape, 1).astype(F32)
    start_ref[...] = jnp.full(start_ref.shape, count + 2 * rows, jnp.int32)
    start_ref[:, 0:rows] = (starts + extra).astype(jnp.int32)
    for i in range(blocks):
        turned = jnp.broadcast_to(cell[i : i + 1], (128, 128)).T
        for j in range(128 // pairs):
            at = (j % 2) * half + (i * (128 // pairs) + j) // 2 * pairs
            mark_ref[at : at + pairs, :] = turned[j * pairs : (j + 1) * pairs]


def order(berg_cell, rows, cols, pairs):
    count = berg_cell.shape[0]
    blocks = count // 128
    return pl.pallas_call(
        functools.partial(order_kernel, rows=rows, cols=cols, pairs=pairs),
        out_shape=(
            jax.ShapeDtypeStruct((blocks, 128), jnp.int32),
            jax.ShapeDtypeStruct((8, 128), jnp.int32),
            jax.ShapeDtypeStruct((count, 128), F32),
        ),
        in_specs=[VMEM_SPEC],
        out_specs=(VMEM_SPEC,) * 3,
        scratch_shapes=[VM((blocks * rows, 128), F32)],
        compiler_params=pltpu.CompilerParams(vmem_limit_bytes=LIMIT),
        name="order",
    )(*in_hbm(berg_cell.reshape(blocks, 128)))


def final_kernel(
    place_in, start_in, recv_ref, mark_ref, part_hbm, wet_hbm, fix_c, fix_n, fix_s,
    out_hbm,
    rows_v, sorted_v, pv, wet_v, wetf, acc, place_ref, start_ref, sem_i, sem_o, sem_s, *, pairs,
):
    _, levels, rows, cols = pv.shape
    groups = rows // 8
    tiles = cols // 128
    maps = 2 * levels
    n_rows = recv_ref.shape[0]
    count = 2 * (n_rows + rows)

    def load(i):
        here = pl.ds(8 * PARTS[i], 8 * ((PARTS[1:] + (groups,))[i] - PARTS[i]))
        return pltpu.make_async_copy(part_hbm.at[:, :, here], pv.at[:, :, here], sem_i.at[i])

    def store(g):
        here = pl.ds(pl.multiple_of(8 * g, 8), 8)
        return pltpu.make_async_copy(pv.at[:, :, here], out_hbm.at[:, :, here], sem_o)

    small = (
        pltpu.make_async_copy(place_in, place_ref, sem_s.at[0]),
        pltpu.make_async_copy(start_in, start_ref, sem_s.at[1]),
        pltpu.make_async_copy(wet_hbm, wet_v, sem_s.at[2]),
    )
    for copy in small:
        copy.start()
    for i in range(len(PARTS)):
        load(i).start()
    lane_all = lax.broadcasted_iota(jnp.int32, (128, 128), 1)
    even = jnp.bitwise_and(lane_all, 1) == 0
    cell_lane = lane_all == CELL_LANE

    def halves(i, _):
        at = pl.multiple_of(i * 128, 128)
        both = recv_ref[pl.ds(at, 128), :]
        high = both.astype(BF16).astype(F32)
        low = both - high
        for h, body in enumerate(
            (
                jnp.where(even, high, pltpu.roll(low, 1, 1)),
                jnp.where(even, pltpu.roll(high, 127, 1), low),
            )
        ):
            there = pl.ds(pl.multiple_of(h * n_rows + at, 128), 128)
            rows_v[there, :] = jnp.where(cell_lane, mark_ref[there, :], body)
        return _

    lax.fori_loop(0, n_rows // 128, halves, 0)
    for copy in small:
        copy.wait()
    wetf[...] = wet_v[...].astype(F32)
    sorted_v[count:, :] = jnp.full((WINDOW, 128), -1.0, F32)

    def spread(i, _):
        first = pl.multiple_of(i * 64, 64)
        for j in range(128):
            source, h, pair = j // (2 * pairs), j // pairs % 2, j % pairs
            line = rows_v[pl.ds(h * n_rows + first + source * pairs + pair, 1), :]
            sorted_v[pl.ds(place_ref[i, j], 1), :] = line
        return _

    lax.fori_loop(0, place_ref.shape[0], spread, 0)
    for r in range(rows):
        first = start_ref[0, r]
        for h in range(2):
            sorted_v[pl.ds(first + h, 1), :] = fix_c[h, r : r + 1, :]

    lanef = lax.broadcasted_iota(jnp.int32, (WINDOW, 128), 1).astype(F32)

    def row_sources(r, at):
        at = pl.multiple_of(at, 8)
        lines = sorted_v[pl.ds(at, WINDOW), :]
        lhs = lines.astype(BF16).T
        near = jnp.broadcast_to(lines[:, CELL_LANE : CELL_LANE + 1], (WINDOW, 128)) - (r * cols).astype(F32)
        hot = [jnp.where(near - float(128 * c) == lanef, 1.0, 0.0).astype(BF16) for c in range(tiles)]
        return dot_nn(lhs, jnp.concatenate(hot, axis=1))

    def group(g, _):
        here = pl.ds(pl.multiple_of(8 * g, 8), 8)
        firsts, windows = [], []
        for j in range(8):
            s = start_ref[0, 8 * g + j]
            e = start_ref[0, 8 * g + j + 1]
            first = lax.div(s, 8) * 8
            firsts.append(first)
            windows.append(lax.div(e - first + (WINDOW - 1), WINDOW))
        for j in range(8):
            made = row_sources(8 * g + j, firsts[j])
            for c in range(tiles):
                for m in range(0, 2 * maps, 8):
                    acc[c, pl.ds(m * 9 + j, 8, stride=9), :] = made[m : m + 8, c * 128 : (c + 1) * 128]
        most = functools.reduce(jnp.maximum, windows)

        @pl.when(most > 1)
        def _more():
            for j in range(8):

                def again(i, _, j=j):
                    made = row_sources(8 * g + j, firsts[j] + i * WINDOW)
                    for c in range(tiles):
                        for m in range(0, 2 * maps, 8):
                            acc[c, pl.ds(m * 9 + j, 8, stride=9), :] += made[
                                m : m + 8, c * 128 : (c + 1) * 128
                            ]
                    return _

                lax.fori_loop(1, windows[j], again, 0)

        for i in range(len(PARTS)):

            @pl.when(g == PARTS[i])
            def _wait(i=i):
                load(i).wait()

        w = wetf[here, :]

        for edge, ref, at in ((groups - 1, fix_n, rows - 1), (0, fix_s, 0)):

            @pl.when(g == edge)
            def _edge_row(ref=ref, at=at):
                for m in range(maps):
                    t, k = m // levels, m % levels
                    pv[t, k, at : at + 1, :] += ref[m : m + 1, :]

        for m in range(maps):
            t, k = m // levels, m % levels
            at = 18 * m
            for c in range(tiles):
                lanes = slice(c * 128, (c + 1) * 128)
                pv[t, k, here, lanes] += w[:, lanes] * (acc[c, at : at + 8, :] + acc[c, at + 9 : at + 17, :])
        store(g).start()
        return _

    lax.fori_loop(0, groups, group, 0)
    pltpu.make_async_copy(pv, out_hbm, sem_o).wait()


def finish(place, start, recv, mark, part, wet, fix, pairs):
    _, levels, rows, cols = part.shape
    return pl.pallas_call(
        functools.partial(final_kernel, pairs=pairs),
        out_shape=jax.ShapeDtypeStruct(part.shape, F32),
        in_specs=[VMEM_SPEC] * 4 + [ANY_SPEC] * 2 + [VMEM_SPEC] * 3,
        out_specs=ANY_SPEC,
        scratch_shapes=[
            VM((2 * recv.shape[0], 128), F32),
            VM((2 * recv.shape[0] + 2 * rows + WINDOW, 128), F32),
            VM(part.shape, F32),
            VM((rows, cols), jnp.int32),
            VM((rows, cols), F32),
            VM((cols // 128, 9 * 128, 128), F32),
            pltpu.SMEM(place.shape, jnp.int32),
            pltpu.SMEM(start.shape, jnp.int32),
            pltpu.SemaphoreType.DMA((len(PARTS),)),
            pltpu.SemaphoreType.DMA,
            pltpu.SemaphoreType.DMA((3,)),
        ],
        compiler_params=pltpu.CompilerParams(vmem_limit_bytes=24 << 20),
        name="final",
    )(place, start, recv, mark, *in_hbm(part, wet), *fix)


def swap(value, axes, pairs):
    return lax.ppermute(value, axes, pairs + [(b, a) for a, b in pairs])


def shards(
    tracers, east_speed, north_speed, wet, fold_partner, bergs, berg_count, berg_cell, melt_map
):
    lon_count, lat_count = lax.axis_size("lon"), lax.axis_size("lat")
    levels, cols = tracers.shape[1], tracers.shape[3]

    melt = melt_rows(bergs, berg_count, melt_map)
    recv = lax.all_to_all(melt, ("lon", "lat"), split_axis=0, concat_axis=0, tiled=True)
    part, *own = stencil(tracers, east_speed, north_speed, wet)
    ew, ns_a, ns_b = own

    lon_even = [(i, i + 1) for i in range(0, lon_count, 2)]
    lon_odd = [(i, (i + 1) % lon_count) for i in range(1, lon_count, 2)]

    def place(i, j):
        return i * lat_count + j

    lat_odd = [(place(i, j), place(i, j + 1)) for i in range(lon_count) for j in range(1, lat_count - 1, 2)]
    lat_odd += [
        (place(i, lat_count - 1), place(lon_count - 1 - i, lat_count - 1))
        for i in range(lon_count // 2)
    ]
    lat_even = [(j, j + 1) for j in range(0, lat_count, 2)]
    far = (
        swap(ew, "lon", lon_even),
        swap(ew, "lon", lon_odd),
        swap(ns_a, ("lon", "lat"), lat_odd),
        swap(ns_b, "lat", lat_even),
    )
    fix = fixes(fold_partner, own, far, levels)
    pairs = melt.shape[1]
    spots, start, mark = order(berg_cell, tracers.shape[2], cols, pairs)
    recv = recv.reshape(-1, 128)
    return finish(spots, start, recv, mark, part, wet, fix, pairs)


def solution(mesh):
    in_specs = (
        P(None, None, "lat", "lon"),
        P(None, "lat", "lon"),
        P(None, "lat", "lon"),
        P("lat", "lon"),
        P("lon"),
        P(("lon", "lat"), None),
        P(("lon", "lat")),
        P(("lon", "lat")),
        P(),
    )
    out_specs = P(None, None, "lat", "lon")
    return jax.shard_map(shards, mesh=mesh, in_specs=in_specs, out_specs=out_specs, check_vma=False)
```

```python
import functools

import jax
import jax.numpy as jnp
from jax import lax
from jax.experimental import pallas as pl
from jax.experimental.pallas import tpu as pltpu
from jax.sharding import PartitionSpec as P

diffuse_h = 0.1
diffuse_v = 0.1
time_step = 0.5

F32 = jnp.float32
BF16 = jnp.bfloat16
VM = pltpu.VMEM
VMEM_SPEC = pl.BlockSpec(memory_space=pltpu.VMEM)
SMEM_SPEC = pl.BlockSpec(memory_space=pltpu.SMEM)
ANY_SPEC = pl.BlockSpec(memory_space=pl.ANY)
LIMIT = 12 << 20

EAST_WET = 126
WEST_WET = 127
MELT_STEPS = 4
FIRSTS = (0, 1, 3, 6, 10, 15, 20)
AHEAD = 3
SENDS = (6, 12, 18, 22, 24)
PARTS = (0, 2)
WINDOW = 128
CELL_LANE = 100


def in_hbm(*values):
    return tuple(pltpu.with_memory_space_constraint(v, pltpu.HBM) for v in values)


def split(value):
    high = value.astype(BF16)
    low = (value - high.astype(F32)).astype(BF16)
    return high, low


def dot_nt(a, b):
    return lax.dot_general(a, b, (((1,), (1,)), ((), ())), preferred_element_type=F32)


def dot_nn(a, b):
    return lax.dot_general(a, b, (((1,), (0,)), ((), ())), preferred_element_type=F32)


def melt_kernel(
    count_hbm, berg_hbm, map_hbm, out_hbm,
    berg_v, out_v, weight_ref, map_v, count_ref, sem_i, sem_o, sem_s,
):
    maps = map_v.shape[0]
    width = berg_v.shape[1]
    owners, pairs = out_v.shape[:2]
    steps = MELT_STEPS
    per = owners // steps
    rows = per * pairs

    def load(i):
        span = pl.ds(i * 2 * rows, 2 * rows)
        return pltpu.make_async_copy(berg_hbm.at[span], berg_v.at[span], sem_i.at[i])

    def store(i):
        span = pl.ds(i * per, per)
        return pltpu.make_async_copy(out_v.at[span], out_hbm.at[span], sem_o)

    small = (
        pltpu.make_async_copy(map_hbm, map_v, sem_s.at[0]),
        pltpu.make_async_copy(count_hbm, count_ref, sem_s.at[1]),
    )
    for copy in small:
        copy.start()
    for i in range(steps):
        load(i).start()
    for copy in small:
        copy.wait()
    weight_ref[...] = jnp.zeros_like(weight_ref)
    for h in range(2):
        weight_ref[h, pl.ds(h, maps, stride=2), :] = map_v[...]
    w_high, w_low = split(jnp.concatenate([weight_ref[0], weight_ref[1]], axis=1))
    w_both = jnp.concatenate([w_high, w_low], axis=0)
    lane = lax.broadcasted_iota(jnp.int32, (pairs, 128), 1)
    slot = lax.broadcasted_iota(jnp.int32, (pairs, 128), 0) + pairs * jnp.bitwise_and(lane, 1)
    for i in range(steps):
        load(i).wait()
        slots = berg_v[i * 2 * rows : (i + 1) * 2 * rows, :].reshape(per, 2, pairs, width)
        both = jnp.concatenate([slots[:, h].reshape(rows, width) for h in range(2)], axis=1)
        b_high, b_low = split(both)
        wide = dot_nt(b_high, w_both)
        made = wide[:, :128] + (wide[:, 128:] + dot_nt(b_low, w_high))
        for o in range(per):
            out_v[i * per + o] = jnp.where(
                slot < count_ref[i * per + o], made[o * pairs : (o + 1) * pairs], 0.0
            )
        store(i).start()
    pltpu.make_async_copy(out_v, out_hbm, sem_o).wait()


def melt_rows(bergs, berg_count, melt_map):
    owners = berg_count.shape[0]
    pairs = bergs.shape[0] // owners // 2
    width = bergs.shape[1]
    dma = pltpu.SemaphoreType.DMA((MELT_STEPS,))
    return pl.pallas_call(
        melt_kernel,
        out_shape=jax.ShapeDtypeStruct((owners, pairs, 128), F32),
        in_specs=[ANY_SPEC] * 3,
        out_specs=ANY_SPEC,
        scratch_shapes=[
            VM(bergs.shape, F32),
            VM((owners, pairs, 128), F32),
            VM((2, 128, width), F32),
            VM(melt_map.shape[::-1], F32),
            pltpu.SMEM((owners,), jnp.int32),
            dma,
            pltpu.SemaphoreType.DMA,
            pltpu.SemaphoreType.DMA((2,)),
        ],
        compiler_params=pltpu.CompilerParams(vmem_limit_bytes=LIMIT),
        name="melt",
    )(*in_hbm(berg_count, bergs, melt_map.T))


def stencil_kernel(
    tr_hbm, ev, no_hbm, wet_hbm,
    part_hbm, ew, ns_a, ns_b,
    tv, nv, ov, faces, wetf, wet_v, sem_t, sem_n, sem_o, sem_w,
):
    levels, rows, cols = no_hbm.shape
    strips = rows // 8

    firsts = FIRSTS
    lasts = firsts[1:] + (levels,)
    sent = (0,) + SENDS + (levels,)

    def copies(c):
        span = pl.ds(firsts[c], lasts[c] - firsts[c])
        return (
            pltpu.make_async_copy(tr_hbm.at[:, span], tv.at[:, span], sem_t.at[c]),
            pltpu.make_async_copy(no_hbm.at[span], nv.at[span], sem_n.at[c]),
        )

    def result(c):
        span = pl.ds(sent[c], sent[c + 1] - sent[c])
        return pltpu.make_async_copy(ov.at[:, span], part_hbm.at[:, span], sem_o)

    mask_copy = pltpu.make_async_copy(wet_hbm, wet_v, sem_w)
    mask_copy.start()
    for c in range(AHEAD):
        for copy in copies(c):
            copy.start()
    mask_copy.wait()
    odd_lat = lax.rem(lax.axis_index("lat"), 2)
    row_a = odd_lat * (rows - 1)
    row_b = (1 - odd_lat) * (rows - 1)

    wet = wet_v[...].astype(F32)
    wetf[...] = wet
    col = lax.broadcasted_iota(jnp.int32, (rows, cols), 1)
    row = lax.broadcasted_iota(jnp.int32, (rows, cols), 0)
    for at, face in enumerate(
        (
            jnp.where(col == cols - 1, 0.0, wet * pltpu.roll(wet, cols - 1, 1)),
            jnp.where(row == rows - 1, 0.0, wet * pltpu.roll(wet, rows - 1, 0)),
        )
    ):
        faces[2 * at] = (0.25 * time_step) * face
        faces[2 * at + 1] = (diffuse_h * time_step) * face
    lane_all = lax.broadcasted_iota(jnp.int32, (rows, 128), 1)
    ns_a[...] = jnp.zeros_like(ns_a)
    ns_b[...] = jnp.zeros_like(ns_b)
    ns_a[3 * levels : 3 * levels + 1, :] = wetf[pl.ds(row_a, 1), :]
    ns_b[3 * levels : 3 * levels + 1, :] = wetf[pl.ds(row_b, 1), :]

    lane = lax.broadcasted_iota(jnp.int32, (8, 128), 1)
    top = lax.broadcasted_iota(jnp.int32, (8, cols), 0) == 0

    bottom = lax.broadcasted_iota(jnp.int32, (8, cols), 0) == 7

    def level(k, _):
        above = jnp.minimum(k + 1, levels - 1)
        below = jnp.maximum(k - 1, 0)
        for c in range(len(firsts)):

            @pl.when(k == max(firsts[c] - 1, 0))
            def _wait(c=c):
                for copy in copies(c):
                    copy.wait()
                if c + AHEAD < len(firsts):
                    for copy in copies(c + AHEAD):
                        copy.start()

        carried = [None, None]
        fields = [tv.at[0, k], tv.at[1, k], nv.at[k]]
        own = [f[0:8, :] for f in fields]
        risen = [pltpu.roll(f, 7, 0) for f in own]
        for s in range(strips):
            here = pl.ds(8 * s, 8)
            if s < strips - 1:
                later = [f[8 * s + 8 : 8 * s + 16, :] for f in fields]
                later_risen = [pltpu.roll(f, 7, 0) for f in later]
                north = [jnp.where(bottom, b, a) for a, b in zip(risen, later_risen)]
            else:
                later, later_risen, north = own, risen, risen
            u = ev[k, here, :]
            v = own[2]
            w = wetf[here, :]
            u_next = pltpu.roll(u, cols - 1, 1)
            s_e = faces[0, here, :] * (u + u_next)
            s_n = faces[2, here, :] * (v + north[2])
            d_e = faces[1, here, :]
            d_n = faces[3, here, :]
            a_e, b_e, a_n, b_n = s_e + d_e, s_e - d_e, s_n + d_n, s_n - d_n
            for t in range(2):
                q = own[t]
                up = tv[t, above, here, :]
                dn = tv[t, below, here, :]
                q_next = pltpu.roll(q, cols - 1, 1)
                fe = q * a_e + q_next * b_e
                fn = q * a_n + north[t] * b_n
                fw = pltpu.roll(fe, 1, 1)
                turned = pltpu.roll(fn, 1, 0)
                last = jnp.zeros_like(turned) if carried[t] is None else carried[t]
                fs = jnp.where(top, last, turned)
                carried[t] = turned
                mix = (1 - 2 * diffuse_v * time_step) * q + (diffuse_v * time_step) * (up + dn)
                ov[t, k, here, :] = w * ((mix - (fe - fw)) - (fn - fs))
            own, risen = later, later_risen
        for ref, at in ((ns_a, row_a), (ns_b, row_b)):
            ref[pl.ds(k, 1), :] = tv[0, k, pl.ds(at, 1), :]
            ref[pl.ds(levels + k, 1), :] = tv[1, k, pl.ds(at, 1), :]
            ref[pl.ds(2 * levels + k, 1), :] = nv[k, pl.ds(at, 1), :]
        for c in range(len(sent) - 1):

            @pl.when(k == sent[c + 1] - 1)
            def _send(c=c):
                result(c).start()

        return _

    lax.fori_loop(0, levels, level, 0)

    west_lanes = lane < 64
    ends = (lane == 0) | (lane == 127)

    def inserted(packs, field):
        made = []
        for s, pack in enumerate(packs):
            here = pl.ds(8 * s, 8)
            both = jnp.where(west_lanes, field[here, 0:128], field[here, cols - 128 : cols])
            made.append(jnp.where(ends, both, pltpu.roll(pack, 2, 1)))
        return tuple(made)

    def second(i, packs):
        return inserted(packs, tv.at[1, levels - 1 - i])

    def first(i, packs):
        k = levels - 1 - i
        return inserted(packs[0], tv.at[0, k]), inserted(packs[1], ev.at[k])

    blank = (jnp.zeros((8, 128), F32),) * strips
    fields = lax.fori_loop(0, levels, second, blank)
    fields, speeds = lax.fori_loop(0, levels, first, (fields, blank))
    fields = pltpu.roll(jnp.concatenate(fields, axis=0), 1, 1)
    fields = jnp.where(lane_all == EAST_WET, wetf[:, cols - 1 : cols], fields)
    ew[:, 0:128] = jnp.where(lane_all == WEST_WET, wetf[:, 0:1], fields)
    speeds = jnp.concatenate(speeds, axis=0)
    ew[:, 128:256] = jnp.where(
        lane_all < 2 * levels, pltpu.roll(speeds, 1, 1), pltpu.roll(speeds, 2 * levels + 1, 1)
    )
    pltpu.make_async_copy(ov, part_hbm, sem_o).wait()


def stencil(tracers, east_speed, north_speed, wet):
    count, levels, rows, cols = tracers.shape
    edge_rows = -(-(3 * levels + 1) // 8) * 8
    dma = pltpu.SemaphoreType.DMA((len(FIRSTS),))
    return pl.pallas_call(
        stencil_kernel,
        out_shape=(
            pltpu.HBM(tracers.shape, F32),
            jax.ShapeDtypeStruct((rows, 256), F32),
            jax.ShapeDtypeStruct((edge_rows, cols), F32),
            jax.ShapeDtypeStruct((edge_rows, cols), F32),
        ),
        in_specs=[ANY_SPEC, VMEM_SPEC, ANY_SPEC, ANY_SPEC],
        out_specs=(ANY_SPEC,) + (VMEM_SPEC,) * 3,
        scratch_shapes=[
            VM(tracers.shape, F32),
            VM(north_speed.shape, F32),
            VM(tracers.shape, F32),
            VM((4, rows, cols), F32),
            VM((rows, cols), F32),
            VM((rows, cols), jnp.int32),
            dma,
            dma,
            pltpu.SemaphoreType.DMA,
            pltpu.SemaphoreType.DMA,
        ],
        compiler_params=pltpu.CompilerParams(vmem_limit_bytes=20 << 20),
        name="stencil",
    )(*in_hbm(tracers), east_speed, *in_hbm(north_speed, wet))


def fix_kernel(
    fold_ref, ew, ns_a, ns_b, ew_a_in, ew_b_in, ns_a_in, ns_b_in,
    fix_c, fix_n, fix_s, north, south,
):
    levels = fix_n.shape[0] // 2
    cols = ns_a.shape[1]
    lon_count, lat_count = lax.axis_size("lon"), lax.axis_size("lat")
    lon_index, lat_index = lax.axis_index("lon"), lax.axis_index("lat")
    odd_lon = lax.rem(lon_index, 2) == 1
    odd_lat = lax.rem(lat_index, 2) == 1

    def faces(q, s, w, q_next, s_next, w_next):
        face = w * w_next
        speed = (0.25 * time_step) * face * (s + s_next)
        spread = (diffuse_h * time_step) * face
        return q * (speed + spread) + q_next * (speed - spread)

    def pick(odd, a, b):
        return jnp.where(odd, a, b)

    def column(value, turn, mask):
        field, speed = value[:, 0:128], value[:, 128:256]
        if turn:
            field, speed = pltpu.roll(field, turn, 1), pltpu.roll(speed, turn, 1)
        return field, speed, value[:, mask : mask + 1]

    own, far_a, far_b = ew[...], ew_a_in[...], ew_b_in[...]
    east_own = column(own, 0, EAST_WET)
    west_own = column(own, 0, WEST_WET)
    east_far = column(pick(odd_lon, far_b, far_a), 127, WEST_WET)
    west_far = column(pick(odd_lon, far_a, far_b), 1, EAST_WET)
    lane = lax.broadcasted_iota(jnp.int32, (own.shape[0], 128), 1)
    even = jnp.bitwise_and(lane, 1) == 0
    first = lax.broadcasted_iota(jnp.int32, lane.shape, 0) * cols
    for at, value, cell in (
        (0, -(east_own[2] * faces(*east_own, *east_far)), first + (cols - 1)),
        (1, west_own[2] * faces(*west_far, *west_own), first),
    ):
        high = value.astype(BF16).astype(F32)
        low = value - high
        if at:
            body = jnp.where(even, pltpu.roll(high, 127, 1), low)
        else:
            body = jnp.where(even, high, pltpu.roll(low, 1, 1))
        fix_c[at] = jnp.where(lane == CELL_LANE, cell.astype(F32), body)

    north[...] = pick(odd_lat, ns_a_in[...], ns_b_in[...])
    south[...] = pick(odd_lat, ns_b_in[...], ns_a_in[...])

    @pl.when(lat_index == lat_count - 1)
    def _fold():
        picks = fold_ref[...].reshape(1, cols) - (lon_count - 1 - lon_index) * cols
        hot = (lax.broadcasted_iota(jnp.int32, (cols, cols), 0) == picks).astype(F32).astype(BF16)
        across = north[...]
        high, low = split(across)
        least = ((across - high.astype(F32)) - low.astype(F32)).astype(BF16)
        picked = dot_nn(high, hot) + (dot_nn(low, hot) + dot_nn(least, hot))
        at = lax.broadcasted_iota(jnp.int32, picked.shape, 0)
        is_speed = (at >= 2 * levels) & (at < 3 * levels)
        north[...] = jnp.where(is_speed, -picked, picked)

    def fields(value, t):
        return (
            value[t * levels : (t + 1) * levels],
            value[2 * levels : 3 * levels],
            value[3 * levels : 3 * levels + 1],
        )

    north_own = pick(odd_lat, ns_a[...], ns_b[...])
    south_own = pick(odd_lat, ns_b[...], ns_a[...])
    north_far, south_far = north[...], south[...]
    for t in range(2):
        at = pl.ds(t * levels, levels)
        own = fields(north_own, t)
        fix_n[at, :] = -(own[2] * faces(*own, *fields(north_far, t)))
        own = fields(south_own, t)
        fix_s[at, :] = own[2] * faces(*fields(south_far, t), *own)


def fixes(fold_partner, own, far, levels):
    rows, cols = own[0].shape[0], own[1].shape[1]
    return pl.pallas_call(
        fix_kernel,
        out_shape=(
            jax.ShapeDtypeStruct((2, rows, 128), F32),
            jax.ShapeDtypeStruct((2 * levels, cols), F32),
            jax.ShapeDtypeStruct((2 * levels, cols), F32),
        ),
        in_specs=[VMEM_SPEC] * 8,
        out_specs=(VMEM_SPEC,) * 3,
        scratch_shapes=[VM(own[1].shape, F32), VM(own[1].shape, F32)],
        compiler_params=pltpu.CompilerParams(vmem_limit_bytes=LIMIT),
        name="fix",
    )(*in_hbm(fold_partner), *own, *far)


def order_kernel(cell_ref, place_ref, start_ref, mark_ref, base_ref, *, rows, cols, pairs):
    blocks = cell_ref.shape[0]
    count = blocks * 128
    half = count // 2
    cell = cell_ref[...].astype(F32)
    row = jnp.floor((cell + 0.5) * (1.0 / cols))
    hot = [jnp.where(row == float(r), 1.0, 0.0) for r in range(rows)]
    hot16 = jnp.concatenate([h.astype(BF16) for h in hot], axis=0)
    down = lax.broadcasted_iota(jnp.int32, (128, 128), 0)
    along = lax.broadcasted_iota(jnp.int32, (128, 128), 1)
    before = jnp.where(down < along, 1.0, 0.0).astype(BF16)
    after = jnp.where(along < down, 1.0, 0.0).astype(BF16)
    ones = jnp.ones((128, 128), BF16)
    within = dot_nn(hot16, before)
    totals = dot_nn(hot16, ones)
    carry = jnp.zeros((1, 128), F32)
    place = jnp.zeros(cell.shape, F32)
    per = 128 // blocks
    for c in range(rows // per):
        part = totals[c * 128 : (c + 1) * 128]
        base = dot_nn(after, part.astype(BF16)) + carry
        carry = base[127:128] + part[127:128]
        base_ref[c * 128 : (c + 1) * 128, :] = base
        spot = base + within[c * 128 : (c + 1) * 128]
        for j in range(per):
            extra = 2.0 * (c * per + j + 1)
            place = place + hot[c * per + j] * (spot[j * blocks : (j + 1) * blocks] + extra)
    place_ref[...] = place.astype(jnp.int32)
    starts = base_ref[pl.ds(0, rows, stride=blocks), :]
    high = jnp.floor(starts * (1.0 / 128))
    low = starts - 128 * high
    first = jnp.where(along[:8] == 0, 1.0, 0.0).astype(BF16)
    starts = 128 * dot_nt(first, high.astype(BF16)) + dot_nt(first, low.astype(BF16))
    extra = 2.0 * lax.broadcasted_iota(jnp.int32, starts.shape, 1).astype(F32)
    start_ref[...] = jnp.full(start_ref.shape, count + 2 * rows, jnp.int32)
    start_ref[:, 0:rows] = (starts + extra).astype(jnp.int32)
    for i in range(blocks):
        turned = jnp.broadcast_to(cell[i : i + 1], (128, 128)).T
        for j in range(128 // pairs):
            at = (j % 2) * half + (i * (128 // pairs) + j) // 2 * pairs
            mark_ref[at : at + pairs, :] = turned[j * pairs : (j + 1) * pairs]


def order(berg_cell, rows, cols, pairs):
    count = berg_cell.shape[0]
    blocks = count // 128
    return pl.pallas_call(
        functools.partial(order_kernel, rows=rows, cols=cols, pairs=pairs),
        out_shape=(
            jax.ShapeDtypeStruct((blocks, 128), jnp.int32),
            jax.ShapeDtypeStruct((8, 128), jnp.int32),
            jax.ShapeDtypeStruct((count, 128), F32),
        ),
        in_specs=[VMEM_SPEC],
        out_specs=(VMEM_SPEC,) * 3,
        scratch_shapes=[VM((blocks * rows, 128), F32)],
        compiler_params=pltpu.CompilerParams(vmem_limit_bytes=LIMIT),
        name="order",
    )(*in_hbm(berg_cell.reshape(blocks, 128)))


def final_kernel(
    place_in, start_in, recv_ref, mark_ref, part_hbm, wet_hbm, fix_c, fix_n, fix_s,
    out_hbm,
    rows_v, sorted_v, pv, wet_v, wetf, acc, place_ref, start_ref, sem_i, sem_o, sem_s, *, pairs,
):
    _, levels, rows, cols = pv.shape
    groups = rows // 8
    tiles = cols // 128
    maps = 2 * levels
    n_rows = recv_ref.shape[0]
    count = 2 * (n_rows + rows)

    def load(i):
        here = pl.ds(8 * PARTS[i], 8 * ((PARTS[1:] + (groups,))[i] - PARTS[i]))
        return pltpu.make_async_copy(part_hbm.at[:, :, here], pv.at[:, :, here], sem_i.at[i])

    def store(g):
        here = pl.ds(pl.multiple_of(8 * g, 8), 8)
        return pltpu.make_async_copy(pv.at[:, :, here], out_hbm.at[:, :, here], sem_o)

    small = (
        pltpu.make_async_copy(place_in, place_ref, sem_s.at[0]),
        pltpu.make_async_copy(start_in, start_ref, sem_s.at[1]),
        pltpu.make_async_copy(wet_hbm, wet_v, sem_s.at[2]),
    )
    for copy in small:
        copy.start()
    for i in range(len(PARTS)):
        load(i).start()
    lane_all = lax.broadcasted_iota(jnp.int32, (128, 128), 1)
    even = jnp.bitwise_and(lane_all, 1) == 0
    cell_lane = lane_all == CELL_LANE

    def halves(i, _):
        at = pl.multiple_of(i * 128, 128)
        both = recv_ref[pl.ds(at, 128), :]
        high = both.astype(BF16).astype(F32)
        low = both - high
        for h, body in enumerate(
            (
                jnp.where(even, high, pltpu.roll(low, 1, 1)),
                jnp.where(even, pltpu.roll(high, 127, 1), low),
            )
        ):
            there = pl.ds(pl.multiple_of(h * n_rows + at, 128), 128)
            rows_v[there, :] = jnp.where(cell_lane, mark_ref[there, :], body)
        return _

    lax.fori_loop(0, n_rows // 128, halves, 0)
    for copy in small:
        copy.wait()
    wetf[...] = wet_v[...].astype(F32)
    sorted_v[count:, :] = jnp.full((WINDOW, 128), -1.0, F32)

    for i in range(place_ref.shape[0]):
        first = i * 64
        for j in range(128):
            source, h, pair = j // (2 * pairs), j // pairs % 2, j % pairs
            line = rows_v[pl.ds(h * n_rows + first + source * pairs + pair, 1), :]
            sorted_v[pl.ds(place_ref[i, j], 1), :] = line
    for r in range(rows):
        first = start_ref[0, r]
        for h in range(2):
            sorted_v[pl.ds(first + h, 1), :] = fix_c[h, r : r + 1, :]

    lanef = lax.broadcasted_iota(jnp.int32, (WINDOW, 128), 1).astype(F32)

    def row_sources(r, at):
        at = pl.multiple_of(at, 8)
        lines = sorted_v[pl.ds(at, WINDOW), :]
        lhs = lines.astype(BF16).T
        near = jnp.broadcast_to(lines[:, CELL_LANE : CELL_LANE + 1], (WINDOW, 128)) - (r * cols).astype(F32)
        hot = [jnp.where(near - float(128 * c) == lanef, 1.0, 0.0).astype(BF16) for c in range(tiles)]
        return dot_nn(lhs, jnp.concatenate(hot, axis=1))

    def group(g, _):
        here = pl.ds(pl.multiple_of(8 * g, 8), 8)
        firsts, windows = [], []
        for j in range(8):
            s = start_ref[0, 8 * g + j]
            e = start_ref[0, 8 * g + j + 1]
            first = lax.div(s, 8) * 8
            firsts.append(first)
            windows.append(lax.div(e - first + (WINDOW - 1), WINDOW))
        for j in range(8):
            made = row_sources(8 * g + j, firsts[j])
            for c in range(tiles):
                for m in range(0, 2 * maps, 8):
                    acc[c, pl.ds(m * 9 + j, 8, stride=9), :] = made[m : m + 8, c * 128 : (c + 1) * 128]
        most = functools.reduce(jnp.maximum, windows)

        @pl.when(most > 1)
        def _more():
            for j in range(8):

                def again(i, _, j=j):
                    made = row_sources(8 * g + j, firsts[j] + i * WINDOW)
                    for c in range(tiles):
                        for m in range(0, 2 * maps, 8):
                            acc[c, pl.ds(m * 9 + j, 8, stride=9), :] += made[
                                m : m + 8, c * 128 : (c + 1) * 128
                            ]
                    return _

                lax.fori_loop(1, windows[j], again, 0)

        for i in range(len(PARTS)):

            @pl.when(g == PARTS[i])
            def _wait(i=i):
                load(i).wait()

        w = wetf[here, :]

        for edge, ref, at in ((groups - 1, fix_n, rows - 1), (0, fix_s, 0)):

            @pl.when(g == edge)
            def _edge_row(ref=ref, at=at):
                for m in range(maps):
                    t, k = m // levels, m % levels
                    pv[t, k, at : at + 1, :] += ref[m : m + 1, :]

        for m in range(maps):
            t, k = m // levels, m % levels
            at = 18 * m
            for c in range(tiles):
                lanes = slice(c * 128, (c + 1) * 128)
                pv[t, k, here, lanes] += w[:, lanes] * (acc[c, at : at + 8, :] + acc[c, at + 9 : at + 17, :])
        store(g).start()
        return _

    lax.fori_loop(0, groups, group, 0)
    pltpu.make_async_copy(pv, out_hbm, sem_o).wait()


def finish(place, start, recv, mark, part, wet, fix, pairs):
    _, levels, rows, cols = part.shape
    return pl.pallas_call(
        functools.partial(final_kernel, pairs=pairs),
        out_shape=jax.ShapeDtypeStruct(part.shape, F32),
        in_specs=[VMEM_SPEC] * 4 + [ANY_SPEC] * 2 + [VMEM_SPEC] * 3,
        out_specs=ANY_SPEC,
        scratch_shapes=[
            VM((2 * recv.shape[0], 128), F32),
            VM((2 * recv.shape[0] + 2 * rows + WINDOW, 128), F32),
            VM(part.shape, F32),
            VM((rows, cols), jnp.int32),
            VM((rows, cols), F32),
            VM((cols // 128, 9 * 128, 128), F32),
            pltpu.SMEM(place.shape, jnp.int32),
            pltpu.SMEM(start.shape, jnp.int32),
            pltpu.SemaphoreType.DMA((len(PARTS),)),
            pltpu.SemaphoreType.DMA,
            pltpu.SemaphoreType.DMA((3,)),
        ],
        compiler_params=pltpu.CompilerParams(vmem_limit_bytes=24 << 20),
        name="final",
    )(place, start, recv, mark, *in_hbm(part, wet), *fix)


def swap(value, axes, pairs):
    return lax.ppermute(value, axes, pairs + [(b, a) for a, b in pairs])


def shards(
    tracers, east_speed, north_speed, wet, fold_partner, bergs, berg_count, berg_cell, melt_map
):
    lon_count, lat_count = lax.axis_size("lon"), lax.axis_size("lat")
    levels, cols = tracers.shape[1], tracers.shape[3]

    melt = melt_rows(bergs, berg_count, melt_map)
    recv = lax.all_to_all(melt, ("lon", "lat"), split_axis=0, concat_axis=0, tiled=True)
    part, *own = stencil(tracers, east_speed, north_speed, wet)
    ew, ns_a, ns_b = own

    lon_even = [(i, i + 1) for i in range(0, lon_count, 2)]
    lon_odd = [(i, (i + 1) % lon_count) for i in range(1, lon_count, 2)]

    def place(i, j):
        return i * lat_count + j

    lat_odd = [(place(i, j), place(i, j + 1)) for i in range(lon_count) for j in range(1, lat_count - 1, 2)]
    lat_odd += [
        (place(i, lat_count - 1), place(lon_count - 1 - i, lat_count - 1))
        for i in range(lon_count // 2)
    ]
    lat_even = [(j, j + 1) for j in range(0, lat_count, 2)]
    far = (
        swap(ew, "lon", lon_even),
        swap(ew, "lon", lon_odd),
        swap(ns_a, ("lon", "lat"), lat_odd),
        swap(ns_b, "lat", lat_even),
    )
    fix = fixes(fold_partner, own, far, levels)
    pairs = melt.shape[1]
    spots, start, mark = order(berg_cell, tracers.shape[2], cols, pairs)
    recv = recv.reshape(-1, 128)
    return finish(spots, start, recv, mark, part, wet, fix, pairs)


def solution(mesh):
    in_specs = (
        P(None, None, "lat", "lon"),
        P(None, "lat", "lon"),
        P(None, "lat", "lon"),
        P("lat", "lon"),
        P("lon"),
        P(("lon", "lat"), None),
        P(("lon", "lat")),
        P(("lon", "lat")),
        P(),
    )
    out_specs = P(None, None, "lat", "lon")
    return jax.shard_map(shards, mesh=mesh, in_specs=in_specs, out_specs=out_specs, check_vma=False)
```

```python
import functools

import jax
import jax.numpy as jnp
from jax import lax
from jax.experimental import pallas as pl
from jax.experimental.pallas import tpu as pltpu
from jax.sharding import PartitionSpec as P

diffuse_h = 0.1
diffuse_v = 0.1
time_step = 0.5

F32 = jnp.float32
BF16 = jnp.bfloat16
VM = pltpu.VMEM
VMEM_SPEC = pl.BlockSpec(memory_space=pltpu.VMEM)
SMEM_SPEC = pl.BlockSpec(memory_space=pltpu.SMEM)
ANY_SPEC = pl.BlockSpec(memory_space=pl.ANY)
LIMIT = 12 << 20

EAST_WET = 126
WEST_WET = 127
MELT_STEPS = 4
FIRSTS = (0, 1, 3, 6, 10, 15, 20)
AHEAD = 3
SENDS = (6, 12, 18, 22, 24)
PARTS = (0, 2)
WINDOW = 128
CELL_LANE = 100


def in_hbm(*values):
    return tuple(pltpu.with_memory_space_constraint(v, pltpu.HBM) for v in values)


def split(value):
    high = value.astype(BF16)
    low = (value - high.astype(F32)).astype(BF16)
    return high, low


def dot_nt(a, b):
    return lax.dot_general(a, b, (((1,), (1,)), ((), ())), preferred_element_type=F32)


def dot_nn(a, b):
    return lax.dot_general(a, b, (((1,), (0,)), ((), ())), preferred_element_type=F32)


def melt_kernel(
    count_hbm, berg_hbm, map_hbm, out_hbm,
    berg_v, out_v, weight_ref, map_v, count_ref, sem_i, sem_o, sem_s,
):
    maps = map_v.shape[0]
    width = berg_v.shape[1]
    owners, pairs = out_v.shape[:2]
    steps = MELT_STEPS
    per = owners // steps
    rows = per * pairs

    def load(i):
        span = pl.ds(i * 2 * rows, 2 * rows)
        return pltpu.make_async_copy(berg_hbm.at[span], berg_v.at[span], sem_i.at[i])

    def store(i):
        span = pl.ds(i * per, per)
        return pltpu.make_async_copy(out_v.at[span], out_hbm.at[span], sem_o)

    small = (
        pltpu.make_async_copy(map_hbm, map_v, sem_s.at[0]),
        pltpu.make_async_copy(count_hbm, count_ref, sem_s.at[1]),
    )
    for copy in small:
        copy.start()
    for i in range(steps):
        load(i).start()
    for copy in small:
        copy.wait()
    weight_ref[...] = jnp.zeros_like(weight_ref)
    for h in range(2):
        weight_ref[h, pl.ds(h, maps, stride=2), :] = map_v[...]
    w_high, w_low = split(jnp.concatenate([weight_ref[0], weight_ref[1]], axis=1))
    w_both = jnp.concatenate([w_high, w_low], axis=0)
    lane = lax.broadcasted_iota(jnp.int32, (pairs, 128), 1)
    slot = lax.broadcasted_iota(jnp.int32, (pairs, 128), 0) + pairs * jnp.bitwise_and(lane, 1)
    for i in range(steps):
        load(i).wait()
        slots = berg_v[i * 2 * rows : (i + 1) * 2 * rows, :].reshape(per, 2, pairs, width)
        both = jnp.concatenate([slots[:, h].reshape(rows, width) for h in range(2)], axis=1)
        b_high, b_low = split(both)
        wide = dot_nt(b_high, w_both)
        made = wide[:, :128] + (wide[:, 128:] + dot_nt(b_low, w_high))
        for o in range(per):
            out_v[i * per + o] = jnp.where(
                slot < count_ref[i * per + o], made[o * pairs : (o + 1) * pairs], 0.0
            )
        store(i).start()
    pltpu.make_async_copy(out_v, out_hbm, sem_o).wait()


def melt_rows(bergs, berg_count, melt_map):
    owners = berg_count.shape[0]
    pairs = bergs.shape[0] // owners // 2
    width = bergs.shape[1]
    dma = pltpu.SemaphoreType.DMA((MELT_STEPS,))
    return pl.pallas_call(
        melt_kernel,
        out_shape=jax.ShapeDtypeStruct((owners, pairs, 128), F32),
        in_specs=[ANY_SPEC] * 3,
        out_specs=ANY_SPEC,
        scratch_shapes=[
            VM(bergs.shape, F32),
            VM((owners, pairs, 128), F32),
            VM((2, 128, width), F32),
            VM(melt_map.shape[::-1], F32),
            pltpu.SMEM((owners,), jnp.int32),
            dma,
            pltpu.SemaphoreType.DMA,
            pltpu.SemaphoreType.DMA((2,)),
        ],
        compiler_params=pltpu.CompilerParams(vmem_limit_bytes=LIMIT),
        name="melt",
    )(*in_hbm(berg_count, bergs, melt_map.T))


def stencil_kernel(
    tr_hbm, ev, no_hbm, wet_hbm, cell_hbm, fold_hbm,
    part_hbm, ew, ns_a, ns_b, cell_v, fold_v,
    tv, nv, ov, faces, wetf, wet_v, sem_t, sem_n, sem_o, sem_w,
):
    levels, rows, cols = no_hbm.shape
    strips = rows // 8

    firsts = FIRSTS
    lasts = firsts[1:] + (levels,)
    sent = (0,) + SENDS + (levels,)

    def copies(c):
        span = pl.ds(firsts[c], lasts[c] - firsts[c])
        return (
            pltpu.make_async_copy(tr_hbm.at[:, span], tv.at[:, span], sem_t.at[c]),
            pltpu.make_async_copy(no_hbm.at[span], nv.at[span], sem_n.at[c]),
        )

    def result(c):
        span = pl.ds(sent[c], sent[c + 1] - sent[c])
        return pltpu.make_async_copy(ov.at[:, span], part_hbm.at[:, span], sem_o)

    mask_copy = pltpu.make_async_copy(wet_hbm, wet_v, sem_w.at[0])
    mask_copy.start()
    passed = (
        pltpu.make_async_copy(cell_hbm, cell_v, sem_w.at[1]),
        pltpu.make_async_copy(fold_hbm, fold_v, sem_w.at[2]),
    )
    for c in range(AHEAD):
        for copy in copies(c):
            copy.start()
    for copy in passed:
        copy.start()
    mask_copy.wait()
    odd_lat = lax.rem(lax.axis_index("lat"), 2)
    row_a = odd_lat * (rows - 1)
    row_b = (1 - odd_lat) * (rows - 1)

    wet = wet_v[...].astype(F32)
    wetf[...] = wet
    col = lax.broadcasted_iota(jnp.int32, (rows, cols), 1)
    row = lax.broadcasted_iota(jnp.int32, (rows, cols), 0)
    for at, face in enumerate(
        (
            jnp.where(col == cols - 1, 0.0, wet * pltpu.roll(wet, cols - 1, 1)),
            jnp.where(row == rows - 1, 0.0, wet * pltpu.roll(wet, rows - 1, 0)),
        )
    ):
        faces[2 * at] = (0.25 * time_step) * face
        faces[2 * at + 1] = (diffuse_h * time_step) * face
    lane_all = lax.broadcasted_iota(jnp.int32, (rows, 128), 1)
    ns_a[...] = jnp.zeros_like(ns_a)
    ns_b[...] = jnp.zeros_like(ns_b)
    ns_a[3 * levels : 3 * levels + 1, :] = wetf[pl.ds(row_a, 1), :]
    ns_b[3 * levels : 3 * levels + 1, :] = wetf[pl.ds(row_b, 1), :]

    lane = lax.broadcasted_iota(jnp.int32, (8, 128), 1)
    top = lax.broadcasted_iota(jnp.int32, (8, cols), 0) == 0

    bottom = lax.broadcasted_iota(jnp.int32, (8, cols), 0) == 7

    def level(k, _):
        above = jnp.minimum(k + 1, levels - 1)
        below = jnp.maximum(k - 1, 0)
        for c in range(len(firsts)):

            @pl.when(k == max(firsts[c] - 1, 0))
            def _wait(c=c):
                for copy in copies(c):
                    copy.wait()
                if c + AHEAD < len(firsts):
                    for copy in copies(c + AHEAD):
                        copy.start()

        carried = [None, None]
        fields = [tv.at[0, k], tv.at[1, k], nv.at[k]]
        own = [f[0:8, :] for f in fields]
        risen = [pltpu.roll(f, 7, 0) for f in own]
        for s in range(strips):
            here = pl.ds(8 * s, 8)
            if s < strips - 1:
                later = [f[8 * s + 8 : 8 * s + 16, :] for f in fields]
                later_risen = [pltpu.roll(f, 7, 0) for f in later]
                north = [jnp.where(bottom, b, a) for a, b in zip(risen, later_risen)]
            else:
                later, later_risen, north = own, risen, risen
            u = ev[k, here, :]
            v = own[2]
            w = wetf[here, :]
            u_next = pltpu.roll(u, cols - 1, 1)
            s_e = faces[0, here, :] * (u + u_next)
            s_n = faces[2, here, :] * (v + north[2])
            d_e = faces[1, here, :]
            d_n = faces[3, here, :]
            a_e, b_e, a_n, b_n = s_e + d_e, s_e - d_e, s_n + d_n, s_n - d_n
            for t in range(2):
                q = own[t]
                up = tv[t, above, here, :]
                dn = tv[t, below, here, :]
                q_next = pltpu.roll(q, cols - 1, 1)
                fe = q * a_e + q_next * b_e
                fn = q * a_n + north[t] * b_n
                fw = pltpu.roll(fe, 1, 1)
                turned = pltpu.roll(fn, 1, 0)
                last = jnp.zeros_like(turned) if carried[t] is None else carried[t]
                fs = jnp.where(top, last, turned)
                carried[t] = turned
                mix = (1 - 2 * diffuse_v * time_step) * q + (diffuse_v * time_step) * (up + dn)
                ov[t, k, here, :] = w * ((mix - (fe - fw)) - (fn - fs))
            own, risen = later, later_risen
        for ref, at in ((ns_a, row_a), (ns_b, row_b)):
            ref[pl.ds(k, 1), :] = tv[0, k, pl.ds(at, 1), :]
            ref[pl.ds(levels + k, 1), :] = tv[1, k, pl.ds(at, 1), :]
            ref[pl.ds(2 * levels + k, 1), :] = nv[k, pl.ds(at, 1), :]
        for c in range(len(sent) - 1):

            @pl.when(k == sent[c + 1] - 1)
            def _send(c=c):
                result(c).start()

        return _

    lax.fori_loop(0, levels, level, 0)

    west_lanes = lane < 64
    ends = (lane == 0) | (lane == 127)

    def inserted(packs, field):
        made = []
        for s, pack in enumerate(packs):
            here = pl.ds(8 * s, 8)
            both = jnp.where(west_lanes, field[here, 0:128], field[here, cols - 128 : cols])
            made.append(jnp.where(ends, both, pltpu.roll(pack, 2, 1)))
        return tuple(made)

    def second(i, packs):
        return inserted(packs, tv.at[1, levels - 1 - i])

    def first(i, packs):
        k = levels - 1 - i
        return inserted(packs[0], tv.at[0, k]), inserted(packs[1], ev.at[k])

    blank = (jnp.zeros((8, 128), F32),) * strips
    fields = lax.fori_loop(0, levels, second, blank)
    fields, speeds = lax.fori_loop(0, levels, first, (fields, blank))
    fields = pltpu.roll(jnp.concatenate(fields, axis=0), 1, 1)
    fields = jnp.where(lane_all == EAST_WET, wetf[:, cols - 1 : cols], fields)
    ew[:, 0:128] = jnp.where(lane_all == WEST_WET, wetf[:, 0:1], fields)
    speeds = jnp.concatenate(speeds, axis=0)
    ew[:, 128:256] = jnp.where(
        lane_all < 2 * levels, pltpu.roll(speeds, 1, 1), pltpu.roll(speeds, 2 * levels + 1, 1)
    )
    for copy in passed:
        copy.wait()
    pltpu.make_async_copy(ov, part_hbm, sem_o).wait()


def stencil(tracers, east_speed, north_speed, wet, cells, fold_partner):
    count, levels, rows, cols = tracers.shape
    edge_rows = -(-(3 * levels + 1) // 8) * 8
    dma = pltpu.SemaphoreType.DMA((len(FIRSTS),))
    return pl.pallas_call(
        stencil_kernel,
        out_shape=(
            pltpu.HBM(tracers.shape, F32),
            jax.ShapeDtypeStruct((rows, 256), F32),
            jax.ShapeDtypeStruct((edge_rows, cols), F32),
            jax.ShapeDtypeStruct((edge_rows, cols), F32),
            jax.ShapeDtypeStruct(cells.shape, cells.dtype),
            jax.ShapeDtypeStruct(fold_partner.shape, fold_partner.dtype),
        ),
        in_specs=[ANY_SPEC, VMEM_SPEC] + [ANY_SPEC] * 4,
        out_specs=(ANY_SPEC,) + (VMEM_SPEC,) * 5,
        scratch_shapes=[
            VM(tracers.shape, F32),
            VM(north_speed.shape, F32),
            VM(tracers.shape, F32),
            VM((4, rows, cols), F32),
            VM((rows, cols), F32),
            VM((rows, cols), jnp.int32),
            dma,
            dma,
            pltpu.SemaphoreType.DMA,
            pltpu.SemaphoreType.DMA((3,)),
        ],
        compiler_params=pltpu.CompilerParams(vmem_limit_bytes=20 << 20),
        name="stencil",
    )(*in_hbm(tracers), east_speed, *in_hbm(north_speed, wet, cells, fold_partner))


def fix_kernel(
    fold_ref, ew, ns_a, ns_b, ew_a_in, ew_b_in, ns_a_in, ns_b_in,
    fix_c, fix_n, fix_s, north, south,
):
    levels = fix_n.shape[0] // 2
    cols = ns_a.shape[1]
    lon_count, lat_count = lax.axis_size("lon"), lax.axis_size("lat")
    lon_index, lat_index = lax.axis_index("lon"), lax.axis_index("lat")
    odd_lon = lax.rem(lon_index, 2) == 1
    odd_lat = lax.rem(lat_index, 2) == 1

    def faces(q, s, w, q_next, s_next, w_next):
        face = w * w_next
        speed = (0.25 * time_step) * face * (s + s_next)
        spread = (diffuse_h * time_step) * face
        return q * (speed + spread) + q_next * (speed - spread)

    def pick(odd, a, b):
        return jnp.where(odd, a, b)

    def column(value, turn, mask):
        field, speed = value[:, 0:128], value[:, 128:256]
        if turn:
            field, speed = pltpu.roll(field, turn, 1), pltpu.roll(speed, turn, 1)
        return field, speed, value[:, mask : mask + 1]

    own, far_a, far_b = ew[...], ew_a_in[...], ew_b_in[...]
    east_own = column(own, 0, EAST_WET)
    west_own = column(own, 0, WEST_WET)
    east_far = column(pick(odd_lon, far_b, far_a), 127, WEST_WET)
    west_far = column(pick(odd_lon, far_a, far_b), 1, EAST_WET)
    lane = lax.broadcasted_iota(jnp.int32, (own.shape[0], 128), 1)
    even = jnp.bitwise_and(lane, 1) == 0
    first = lax.broadcasted_iota(jnp.int32, lane.shape, 0) * cols
    for at, value, cell in (
        (0, -(east_own[2] * faces(*east_own, *east_far)), first + (cols - 1)),
        (1, west_own[2] * faces(*west_far, *west_own), first),
    ):
        high = value.astype(BF16).astype(F32)
        low = value - high
        if at:
            body = jnp.where(even, pltpu.roll(high, 127, 1), low)
        else:
            body = jnp.where(even, high, pltpu.roll(low, 1, 1))
        fix_c[at] = jnp.where(lane == CELL_LANE, cell.astype(F32), body)

    north[...] = pick(odd_lat, ns_a_in[...], ns_b_in[...])
    south[...] = pick(odd_lat, ns_b_in[...], ns_a_in[...])

    @pl.when(lat_index == lat_count - 1)
    def _fold():
        picks = fold_ref[...].reshape(1, cols) - (lon_count - 1 - lon_index) * cols
        hot = (lax.broadcasted_iota(jnp.int32, (cols, cols), 0) == picks).astype(F32).astype(BF16)
        across = north[...]
        high, low = split(across)
        least = ((across - high.astype(F32)) - low.astype(F32)).astype(BF16)
        picked = dot_nn(high, hot) + (dot_nn(low, hot) + dot_nn(least, hot))
        at = lax.broadcasted_iota(jnp.int32, picked.shape, 0)
        is_speed = (at >= 2 * levels) & (at < 3 * levels)
        north[...] = jnp.where(is_speed, -picked, picked)

    def fields(value, t):
        return (
            value[t * levels : (t + 1) * levels],
            value[2 * levels : 3 * levels],
            value[3 * levels : 3 * levels + 1],
        )

    north_own = pick(odd_lat, ns_a[...], ns_b[...])
    south_own = pick(odd_lat, ns_b[...], ns_a[...])
    north_far, south_far = north[...], south[...]
    for t in range(2):
        at = pl.ds(t * levels, levels)
        own = fields(north_own, t)
        fix_n[at, :] = -(own[2] * faces(*own, *fields(north_far, t)))
        own = fields(south_own, t)
        fix_s[at, :] = own[2] * faces(*fields(south_far, t), *own)


def fixes(fold_partner, own, far, levels):
    rows, cols = own[0].shape[0], own[1].shape[1]
    return pl.pallas_call(
        fix_kernel,
        out_shape=(
            jax.ShapeDtypeStruct((2, rows, 128), F32),
            jax.ShapeDtypeStruct((2 * levels, cols), F32),
            jax.ShapeDtypeStruct((2 * levels, cols), F32),
        ),
        in_specs=[VMEM_SPEC] * 8,
        out_specs=(VMEM_SPEC,) * 3,
        scratch_shapes=[VM(own[1].shape, F32), VM(own[1].shape, F32)],
        compiler_params=pltpu.CompilerParams(vmem_limit_bytes=LIMIT),
        name="fix",
    )(fold_partner, *own, *far)


def order_kernel(cell_ref, place_ref, start_ref, mark_ref, base_ref, *, rows, cols, pairs):
    blocks = cell_ref.shape[0]
    count = blocks * 128
    half = count // 2
    cell = cell_ref[...].astype(F32)
    row = jnp.floor((cell + 0.5) * (1.0 / cols))
    hot = [jnp.where(row == float(r), 1.0, 0.0) for r in range(rows)]
    hot16 = jnp.concatenate([h.astype(BF16) for h in hot], axis=0)
    down = lax.broadcasted_iota(jnp.int32, (128, 128), 0)
    along = lax.broadcasted_iota(jnp.int32, (128, 128), 1)
    before = jnp.where(down < along, 1.0, 0.0).astype(BF16)
    after = jnp.where(along < down, 1.0, 0.0).astype(BF16)
    ones = jnp.ones((128, 128), BF16)
    within = dot_nn(hot16, before)
    totals = dot_nn(hot16, ones)
    carry = jnp.zeros((1, 128), F32)
    place = jnp.zeros(cell.shape, F32)
    per = 128 // blocks
    for c in range(rows // per):
        part = totals[c * 128 : (c + 1) * 128]
        base = dot_nn(after, part.astype(BF16)) + carry
        carry = base[127:128] + part[127:128]
        base_ref[c * 128 : (c + 1) * 128, :] = base
        spot = base + within[c * 128 : (c + 1) * 128]
        for j in range(per):
            extra = 2.0 * (c * per + j + 1)
            place = place + hot[c * per + j] * (spot[j * blocks : (j + 1) * blocks] + extra)
    place_ref[...] = place.astype(jnp.int32)
    starts = base_ref[pl.ds(0, rows, stride=blocks), :]
    high = jnp.floor(starts * (1.0 / 128))
    low = starts - 128 * high
    first = jnp.where(along[:8] == 0, 1.0, 0.0).astype(BF16)
    starts = 128 * dot_nt(first, high.astype(BF16)) + dot_nt(first, low.astype(BF16))
    extra = 2.0 * lax.broadcasted_iota(jnp.int32, starts.shape, 1).astype(F32)
    start_ref[...] = jnp.full(start_ref.shape, count + 2 * rows, jnp.int32)
    start_ref[:, 0:rows] = (starts + extra).astype(jnp.int32)
    for i in range(blocks):
        turned = jnp.broadcast_to(cell[i : i + 1], (128, 128)).T
        for j in range(128 // pairs):
            at = (j % 2) * half + (i * (128 // pairs) + j) // 2 * pairs
            mark_ref[at : at + pairs, :] = turned[j * pairs : (j + 1) * pairs]


def order(cells, rows, cols, pairs):
    count = cells.size
    blocks = count // 128
    return pl.pallas_call(
        functools.partial(order_kernel, rows=rows, cols=cols, pairs=pairs),
        out_shape=(
            jax.ShapeDtypeStruct((blocks, 128), jnp.int32),
            jax.ShapeDtypeStruct((8, 128), jnp.int32),
            jax.ShapeDtypeStruct((count, 128), F32),
        ),
        in_specs=[VMEM_SPEC],
        out_specs=(VMEM_SPEC,) * 3,
        scratch_shapes=[VM((blocks * rows, 128), F32)],
        compiler_params=pltpu.CompilerParams(vmem_limit_bytes=LIMIT),
        name="order",
    )(cells)


def final_kernel(
    place_in, start_in, recv_ref, mark_ref, part_hbm, wet_hbm, fix_c, fix_n, fix_s,
    out_hbm,
    rows_v, sorted_v, pv, wet_v, wetf, acc, place_ref, start_ref, sem_i, sem_o, sem_s, *, pairs,
):
    _, levels, rows, cols = pv.shape
    groups = rows // 8
    tiles = cols // 128
    maps = 2 * levels
    n_rows = recv_ref.shape[0]
    count = 2 * (n_rows + rows)

    def load(i):
        here = pl.ds(8 * PARTS[i], 8 * ((PARTS[1:] + (groups,))[i] - PARTS[i]))
        return pltpu.make_async_copy(part_hbm.at[:, :, here], pv.at[:, :, here], sem_i.at[i])

    def store(g):
        here = pl.ds(pl.multiple_of(8 * g, 8), 8)
        return pltpu.make_async_copy(pv.at[:, :, here], out_hbm.at[:, :, here], sem_o)

    small = (
        pltpu.make_async_copy(place_in, place_ref, sem_s.at[0]),
        pltpu.make_async_copy(start_in, start_ref, sem_s.at[1]),
        pltpu.make_async_copy(wet_hbm, wet_v, sem_s.at[2]),
    )
    for copy in small:
        copy.start()
    for i in range(len(PARTS)):
        load(i).start()
    lane_all = lax.broadcasted_iota(jnp.int32, (128, 128), 1)
    even = jnp.bitwise_and(lane_all, 1) == 0
    cell_lane = lane_all == CELL_LANE

    def halves(i, _):
        at = pl.multiple_of(i * 128, 128)
        both = recv_ref[pl.ds(at, 128), :]
        high = both.astype(BF16).astype(F32)
        low = both - high
        for h, body in enumerate(
            (
                jnp.where(even, high, pltpu.roll(low, 1, 1)),
                jnp.where(even, pltpu.roll(high, 127, 1), low),
            )
        ):
            there = pl.ds(pl.multiple_of(h * n_rows + at, 128), 128)
            rows_v[there, :] = jnp.where(cell_lane, mark_ref[there, :], body)
        return _

    lax.fori_loop(0, n_rows // 128, halves, 0)
    for copy in small:
        copy.wait()
    wetf[...] = wet_v[...].astype(F32)
    sorted_v[count:, :] = jnp.full((WINDOW, 128), -1.0, F32)

    for i in range(place_ref.shape[0]):
        first = i * 64
        for j in range(128):
            source, h, pair = j // (2 * pairs), j // pairs % 2, j % pairs
            line = rows_v[pl.ds(h * n_rows + first + source * pairs + pair, 1), :]
            sorted_v[pl.ds(place_ref[i, j], 1), :] = line
    for r in range(rows):
        first = start_ref[0, r]
        for h in range(2):
            sorted_v[pl.ds(first + h, 1), :] = fix_c[h, r : r + 1, :]

    lanef = lax.broadcasted_iota(jnp.int32, (WINDOW, 128), 1).astype(F32)

    def row_sources(r, at):
        at = pl.multiple_of(at, 8)
        lines = sorted_v[pl.ds(at, WINDOW), :]
        lhs = lines.astype(BF16).T
        near = jnp.broadcast_to(lines[:, CELL_LANE : CELL_LANE + 1], (WINDOW, 128)) - (r * cols).astype(F32)
        hot = [jnp.where(near - float(128 * c) == lanef, 1.0, 0.0).astype(BF16) for c in range(tiles)]
        return dot_nn(lhs, jnp.concatenate(hot, axis=1))

    def group(g, _):
        here = pl.ds(pl.multiple_of(8 * g, 8), 8)
        firsts, windows = [], []
        for j in range(8):
            s = start_ref[0, 8 * g + j]
            e = start_ref[0, 8 * g + j + 1]
            first = lax.div(s, 8) * 8
            firsts.append(first)
            windows.append(lax.div(e - first + (WINDOW - 1), WINDOW))
        for j in range(8):
            made = row_sources(8 * g + j, firsts[j])
            for c in range(tiles):
                for m in range(0, 2 * maps, 8):
                    acc[c, pl.ds(m * 9 + j, 8, stride=9), :] = made[m : m + 8, c * 128 : (c + 1) * 128]
        most = functools.reduce(jnp.maximum, windows)

        @pl.when(most > 1)
        def _more():
            for j in range(8):

                def again(i, _, j=j):
                    made = row_sources(8 * g + j, firsts[j] + i * WINDOW)
                    for c in range(tiles):
                        for m in range(0, 2 * maps, 8):
                            acc[c, pl.ds(m * 9 + j, 8, stride=9), :] += made[
                                m : m + 8, c * 128 : (c + 1) * 128
                            ]
                    return _

                lax.fori_loop(1, windows[j], again, 0)

        for i in range(len(PARTS)):

            @pl.when(g == PARTS[i])
            def _wait(i=i):
                load(i).wait()

        w = wetf[here, :]

        for edge, ref, at in ((groups - 1, fix_n, rows - 1), (0, fix_s, 0)):

            @pl.when(g == edge)
            def _edge_row(ref=ref, at=at):
                for m in range(maps):
                    t, k = m // levels, m % levels
                    pv[t, k, at : at + 1, :] += ref[m : m + 1, :]

        for m in range(maps):
            t, k = m // levels, m % levels
            at = 18 * m
            for c in range(tiles):
                lanes = slice(c * 128, (c + 1) * 128)
                pv[t, k, here, lanes] += w[:, lanes] * (acc[c, at : at + 8, :] + acc[c, at + 9 : at + 17, :])
        store(g).start()
        return _

    lax.fori_loop(0, groups, group, 0)
    pltpu.make_async_copy(pv, out_hbm, sem_o).wait()


def finish(place, start, recv, mark, part, wet, fix, pairs):
    _, levels, rows, cols = part.shape
    return pl.pallas_call(
        functools.partial(final_kernel, pairs=pairs),
        out_shape=jax.ShapeDtypeStruct(part.shape, F32),
        in_specs=[VMEM_SPEC] * 4 + [ANY_SPEC] * 2 + [VMEM_SPEC] * 3,
        out_specs=ANY_SPEC,
        scratch_shapes=[
            VM((2 * recv.shape[0], 128), F32),
            VM((2 * recv.shape[0] + 2 * rows + WINDOW, 128), F32),
            VM(part.shape, F32),
            VM((rows, cols), jnp.int32),
            VM((rows, cols), F32),
            VM((cols // 128, 9 * 128, 128), F32),
            pltpu.SMEM(place.shape, jnp.int32),
            pltpu.SMEM(start.shape, jnp.int32),
            pltpu.SemaphoreType.DMA((len(PARTS),)),
            pltpu.SemaphoreType.DMA,
            pltpu.SemaphoreType.DMA((3,)),
        ],
        compiler_params=pltpu.CompilerParams(vmem_limit_bytes=24 << 20),
        name="final",
    )(place, start, recv, mark, *in_hbm(part, wet), *fix)


def swap(value, axes, pairs):
    return lax.ppermute(value, axes, pairs + [(b, a) for a, b in pairs])


def shards(
    tracers, east_speed, north_speed, wet, fold_partner, bergs, berg_count, berg_cell, melt_map
):
    lon_count, lat_count = lax.axis_size("lon"), lax.axis_size("lat")
    levels, cols = tracers.shape[1], tracers.shape[3]

    melt = melt_rows(bergs, berg_count, melt_map)
    recv = lax.all_to_all(melt, ("lon", "lat"), split_axis=0, concat_axis=0, tiled=True)
    cells = berg_cell.reshape(-1, 128)
    part, *own, cells, fold_partner = stencil(
        tracers, east_speed, north_speed, wet, cells, fold_partner
    )
    ew, ns_a, ns_b = own

    lon_even = [(i, i + 1) for i in range(0, lon_count, 2)]
    lon_odd = [(i, (i + 1) % lon_count) for i in range(1, lon_count, 2)]

    def place(i, j):
        return i * lat_count + j

    lat_odd = [(place(i, j), place(i, j + 1)) for i in range(lon_count) for j in range(1, lat_count - 1, 2)]
    lat_odd += [
        (place(i, lat_count - 1), place(lon_count - 1 - i, lat_count - 1))
        for i in range(lon_count // 2)
    ]
    lat_even = [(j, j + 1) for j in range(0, lat_count, 2)]
    far = (
        swap(ew, "lon", lon_even),
        swap(ew, "lon", lon_odd),
        swap(ns_a, ("lon", "lat"), lat_odd),
        swap(ns_b, "lat", lat_even),
    )
    fix = fixes(fold_partner, own, far, levels)
    pairs = melt.shape[1]
    spots, start, mark = order(cells, tracers.shape[2], cols, pairs)
    recv = recv.reshape(-1, 128)
    return finish(spots, start, recv, mark, part, wet, fix, pairs)


def solution(mesh):
    in_specs = (
        P(None, None, "lat", "lon"),
        P(None, "lat", "lon"),
        P(None, "lat", "lon"),
        P("lat", "lon"),
        P("lon"),
        P(("lon", "lat"), None),
        P(("lon", "lat")),
        P(("lon", "lat")),
        P(),
    )
    out_specs = P(None, None, "lat", "lon")
    return jax.shard_map(shards, mesh=mesh, in_specs=in_specs, out_specs=out_specs, check_vma=False)
```

```python
import functools

import jax
import jax.numpy as jnp
from jax import lax
from jax.experimental import pallas as pl
from jax.experimental.pallas import tpu as pltpu
from jax.sharding import PartitionSpec as P

diffuse_h = 0.1
diffuse_v = 0.1
time_step = 0.5

F32 = jnp.float32
BF16 = jnp.bfloat16
VM = pltpu.VMEM
VMEM_SPEC = pl.BlockSpec(memory_space=pltpu.VMEM)
SMEM_SPEC = pl.BlockSpec(memory_space=pltpu.SMEM)
ANY_SPEC = pl.BlockSpec(memory_space=pl.ANY)
LIMIT = 12 << 20

EAST_WET = 126
WEST_WET = 127
MELT_STEPS = 4
FIRSTS = (0, 1, 3, 6, 10, 15, 20)
AHEAD = 3
SENDS = (6, 12, 18, 22, 24)
PARTS = (0, 2)
WINDOW = 128
CELL_LANE = 100


def in_hbm(*values):
    return tuple(pltpu.with_memory_space_constraint(v, pltpu.HBM) for v in values)


def split(value):
    high = value.astype(BF16)
    low = (value - high.astype(F32)).astype(BF16)
    return high, low


def dot_nt(a, b):
    return lax.dot_general(a, b, (((1,), (1,)), ((), ())), preferred_element_type=F32)


def dot_nn(a, b):
    return lax.dot_general(a, b, (((1,), (0,)), ((), ())), preferred_element_type=F32)


def melt_kernel(
    count_hbm, berg_hbm, map_hbm, out_hbm,
    berg_v, out_v, weight_ref, map_v, count_ref, sem_i, sem_o, sem_s,
):
    maps = map_v.shape[0]
    width = berg_v.shape[1]
    owners, pairs = out_v.shape[:2]
    steps = MELT_STEPS
    per = owners // steps
    rows = per * pairs

    def load(i):
        span = pl.ds(i * 2 * rows, 2 * rows)
        return pltpu.make_async_copy(berg_hbm.at[span], berg_v.at[span], sem_i.at[i])

    def store(i):
        span = pl.ds(i * per, per)
        return pltpu.make_async_copy(out_v.at[span], out_hbm.at[span], sem_o)

    small = (
        pltpu.make_async_copy(map_hbm, map_v, sem_s.at[0]),
        pltpu.make_async_copy(count_hbm, count_ref, sem_s.at[1]),
    )
    for copy in small:
        copy.start()
    for i in range(steps):
        load(i).start()
    for copy in small:
        copy.wait()
    weight_ref[...] = jnp.zeros_like(weight_ref)
    for h in range(2):
        weight_ref[h, pl.ds(h, maps, stride=2), :] = map_v[...]
    w_high, w_low = split(jnp.concatenate([weight_ref[0], weight_ref[1]], axis=1))
    w_both = jnp.concatenate([w_high, w_low], axis=0)
    lane = lax.broadcasted_iota(jnp.int32, (pairs, 128), 1)
    slot = lax.broadcasted_iota(jnp.int32, (pairs, 128), 0) + pairs * jnp.bitwise_and(lane, 1)
    for i in range(steps):
        load(i).wait()
        slots = berg_v[i * 2 * rows : (i + 1) * 2 * rows, :].reshape(per, 2, pairs, width)
        both = jnp.concatenate([slots[:, h].reshape(rows, width) for h in range(2)], axis=1)
        b_high, b_low = split(both)
        wide = dot_nt(b_high, w_both)
        made = wide[:, :128] + (wide[:, 128:] + dot_nt(b_low, w_high))
        for o in range(per):
            out_v[i * per + o] = jnp.where(
                slot < count_ref[i * per + o], made[o * pairs : (o + 1) * pairs], 0.0
            )
        store(i).start()
    pltpu.make_async_copy(out_v, out_hbm, sem_o).wait()


def melt_rows(bergs, berg_count, melt_map):
    owners = berg_count.shape[0]
    pairs = bergs.shape[0] // owners // 2
    width = bergs.shape[1]
    dma = pltpu.SemaphoreType.DMA((MELT_STEPS,))
    return pl.pallas_call(
        melt_kernel,
        out_shape=jax.ShapeDtypeStruct((owners, pairs, 128), F32),
        in_specs=[ANY_SPEC] * 3,
        out_specs=ANY_SPEC,
        scratch_shapes=[
            VM(bergs.shape, F32),
            VM((owners, pairs, 128), F32),
            VM((2, 128, width), F32),
            VM(melt_map.shape[::-1], F32),
            pltpu.SMEM((owners,), jnp.int32),
            dma,
            pltpu.SemaphoreType.DMA,
            pltpu.SemaphoreType.DMA((2,)),
        ],
        compiler_params=pltpu.CompilerParams(vmem_limit_bytes=LIMIT),
        name="melt",
    )(*in_hbm(berg_count, bergs, melt_map.T))


def stencil_kernel(
    tr_hbm, ev, no_hbm, wet_hbm, cell_hbm, fold_hbm,
    part_hbm, ew, ns_a, ns_b, cell_v, fold_v,
    tv, nv, ov, faces, wetf, wet_v, sem_t, sem_n, sem_o, sem_w,
):
    levels, rows, cols = no_hbm.shape
    strips = rows // 8

    firsts = FIRSTS
    lasts = firsts[1:] + (levels,)
    sent = (0,) + SENDS + (levels,)

    def copies(c):
        span = pl.ds(firsts[c], lasts[c] - firsts[c])
        return (
            pltpu.make_async_copy(tr_hbm.at[:, span], tv.at[:, span], sem_t.at[c]),
            pltpu.make_async_copy(no_hbm.at[span], nv.at[span], sem_n.at[c]),
        )

    def result(c):
        span = pl.ds(sent[c], sent[c + 1] - sent[c])
        return pltpu.make_async_copy(ov.at[:, span], part_hbm.at[:, span], sem_o)

    mask_copy = pltpu.make_async_copy(wet_hbm, wet_v, sem_w.at[0])
    mask_copy.start()
    passed = (
        pltpu.make_async_copy(cell_hbm, cell_v, sem_w.at[1]),
        pltpu.make_async_copy(fold_hbm, fold_v, sem_w.at[2]),
    )
    for c in range(AHEAD):
        for copy in copies(c):
            copy.start()
    for copy in passed:
        copy.start()
    mask_copy.wait()
    odd_lat = lax.rem(lax.axis_index("lat"), 2)
    row_a = odd_lat * (rows - 1)
    row_b = (1 - odd_lat) * (rows - 1)

    wet = wet_v[...].astype(F32)
    wetf[...] = wet
    col = lax.broadcasted_iota(jnp.int32, (rows, cols), 1)
    row = lax.broadcasted_iota(jnp.int32, (rows, cols), 0)
    for at, face in enumerate(
        (
            jnp.where(col == cols - 1, 0.0, wet * pltpu.roll(wet, cols - 1, 1)),
            jnp.where(row == rows - 1, 0.0, wet * pltpu.roll(wet, rows - 1, 0)),
        )
    ):
        faces[2 * at] = (0.25 * time_step) * face
        faces[2 * at + 1] = (diffuse_h * time_step) * face
    lane_all = lax.broadcasted_iota(jnp.int32, (rows, 128), 1)
    ns_a[...] = jnp.zeros_like(ns_a)
    ns_b[...] = jnp.zeros_like(ns_b)
    ns_a[3 * levels : 3 * levels + 1, :] = wetf[pl.ds(row_a, 1), :]
    ns_b[3 * levels : 3 * levels + 1, :] = wetf[pl.ds(row_b, 1), :]

    lane = lax.broadcasted_iota(jnp.int32, (8, 128), 1)
    top = lax.broadcasted_iota(jnp.int32, (8, cols), 0) == 0

    bottom = lax.broadcasted_iota(jnp.int32, (8, cols), 0) == 7

    def level(k, _):
        above = jnp.minimum(k + 1, levels - 1)
        below = jnp.maximum(k - 1, 0)
        for c in range(len(firsts)):

            @pl.when(k == max(firsts[c] - 1, 0))
            def _wait(c=c):
                for copy in copies(c):
                    copy.wait()
                if c + AHEAD < len(firsts):
                    for copy in copies(c + AHEAD):
                        copy.start()

        carried = [None, None]
        fields = [tv.at[0, k], tv.at[1, k], nv.at[k]]
        own = [f[0:8, :] for f in fields]
        risen = [pltpu.roll(f, 7, 0) for f in own]
        for s in range(strips):
            here = pl.ds(8 * s, 8)
            if s < strips - 1:
                later = [f[8 * s + 8 : 8 * s + 16, :] for f in fields]
                later_risen = [pltpu.roll(f, 7, 0) for f in later]
                north = [jnp.where(bottom, b, a) for a, b in zip(risen, later_risen)]
            else:
                later, later_risen, north = own, risen, risen
            u = ev[k, here, :]
            v = own[2]
            w = wetf[here, :]
            u_next = pltpu.roll(u, cols - 1, 1)
            s_e = faces[0, here, :] * (u + u_next)
            s_n = faces[2, here, :] * (v + north[2])
            d_e = faces[1, here, :]
            d_n = faces[3, here, :]
            a_e, b_e, a_n, b_n = s_e + d_e, s_e - d_e, s_n + d_n, s_n - d_n
            for t in range(2):
                q = own[t]
                up = tv[t, above, here, :]
                dn = tv[t, below, here, :]
                q_next = pltpu.roll(q, cols - 1, 1)
                fe = q * a_e + q_next * b_e
                fn = q * a_n + north[t] * b_n
                fw = pltpu.roll(fe, 1, 1)
                turned = pltpu.roll(fn, 1, 0)
                last = jnp.zeros_like(turned) if carried[t] is None else carried[t]
                fs = jnp.where(top, last, turned)
                carried[t] = turned
                mix = (1 - 2 * diffuse_v * time_step) * q + (diffuse_v * time_step) * (up + dn)
                ov[t, k, here, :] = w * ((mix - (fe - fw)) - (fn - fs))
            own, risen = later, later_risen
        for ref, at in ((ns_a, row_a), (ns_b, row_b)):
            ref[pl.ds(k, 1), :] = tv[0, k, pl.ds(at, 1), :]
            ref[pl.ds(levels + k, 1), :] = tv[1, k, pl.ds(at, 1), :]
            ref[pl.ds(2 * levels + k, 1), :] = nv[k, pl.ds(at, 1), :]
        for c in range(len(sent) - 1):

            @pl.when(k == sent[c + 1] - 1)
            def _send(c=c):
                result(c).start()

        return _

    lax.fori_loop(0, levels, level, 0)

    west_lanes = lane < 64
    ends = (lane == 0) | (lane == 127)

    def inserted(packs, field):
        made = []
        for s, pack in enumerate(packs):
            here = pl.ds(8 * s, 8)
            both = jnp.where(west_lanes, field[here, 0:128], field[here, cols - 128 : cols])
            made.append(jnp.where(ends, both, pltpu.roll(pack, 2, 1)))
        return tuple(made)

    def second(i, packs):
        return inserted(packs, tv.at[1, levels - 1 - i])

    def first(i, packs):
        k = levels - 1 - i
        return inserted(packs[0], tv.at[0, k]), inserted(packs[1], ev.at[k])

    blank = (jnp.zeros((8, 128), F32),) * strips
    fields = lax.fori_loop(0, levels, second, blank)
    fields, speeds = lax.fori_loop(0, levels, first, (fields, blank))
    fields = pltpu.roll(jnp.concatenate(fields, axis=0), 1, 1)
    fields = jnp.where(lane_all == EAST_WET, wetf[:, cols - 1 : cols], fields)
    ew[:, 0:128] = jnp.where(lane_all == WEST_WET, wetf[:, 0:1], fields)
    speeds = jnp.concatenate(speeds, axis=0)
    ew[:, 128:256] = jnp.where(
        lane_all < 2 * levels, pltpu.roll(speeds, 1, 1), pltpu.roll(speeds, 2 * levels + 1, 1)
    )
    for copy in passed:
        copy.wait()
    pltpu.make_async_copy(ov, part_hbm, sem_o).wait()


def stencil(tracers, east_speed, north_speed, wet, cells, fold_partner):
    count, levels, rows, cols = tracers.shape
    edge_rows = -(-(3 * levels + 1) // 8) * 8
    dma = pltpu.SemaphoreType.DMA((len(FIRSTS),))
    return pl.pallas_call(
        stencil_kernel,
        out_shape=(
            pltpu.HBM(tracers.shape, F32),
            jax.ShapeDtypeStruct((rows, 256), F32),
            jax.ShapeDtypeStruct((edge_rows, cols), F32),
            jax.ShapeDtypeStruct((edge_rows, cols), F32),
            jax.ShapeDtypeStruct(cells.shape, cells.dtype),
            jax.ShapeDtypeStruct(fold_partner.shape, fold_partner.dtype),
        ),
        in_specs=[ANY_SPEC, VMEM_SPEC] + [ANY_SPEC] * 4,
        out_specs=(ANY_SPEC,) + (VMEM_SPEC,) * 5,
        scratch_shapes=[
            VM(tracers.shape, F32),
            VM(north_speed.shape, F32),
            VM(tracers.shape, F32),
            VM((4, rows, cols), F32),
            VM((rows, cols), F32),
            VM((rows, cols), jnp.int32),
            dma,
            dma,
            pltpu.SemaphoreType.DMA,
            pltpu.SemaphoreType.DMA((3,)),
        ],
        compiler_params=pltpu.CompilerParams(vmem_limit_bytes=20 << 20),
        name="stencil",
    )(*in_hbm(tracers), east_speed, *in_hbm(north_speed, wet, cells, fold_partner))


def fix_kernel(
    fold_ref, ew, ns_a, ns_b, ew_a_in, ew_b_in, ns_a_in, ns_b_in,
    fix_c, fix_n, fix_s, north, south,
):
    levels = fix_n.shape[0] // 2
    cols = ns_a.shape[1]
    lon_count, lat_count = lax.axis_size("lon"), lax.axis_size("lat")
    lon_index, lat_index = lax.axis_index("lon"), lax.axis_index("lat")
    odd_lon = lax.rem(lon_index, 2) == 1
    odd_lat = lax.rem(lat_index, 2) == 1

    def faces(q, s, w, q_next, s_next, w_next):
        face = w * w_next
        speed = (0.25 * time_step) * face * (s + s_next)
        spread = (diffuse_h * time_step) * face
        return q * (speed + spread) + q_next * (speed - spread)

    def pick(odd, a, b):
        return jnp.where(odd, a, b)

    def column(value, turn, mask):
        field, speed = value[:, 0:128], value[:, 128:256]
        if turn:
            field, speed = pltpu.roll(field, turn, 1), pltpu.roll(speed, turn, 1)
        return field, speed, value[:, mask : mask + 1]

    own, far_a, far_b = ew[...], ew_a_in[...], ew_b_in[...]
    east_own = column(own, 0, EAST_WET)
    west_own = column(own, 0, WEST_WET)
    east_far = column(pick(odd_lon, far_b, far_a), 127, WEST_WET)
    west_far = column(pick(odd_lon, far_a, far_b), 1, EAST_WET)
    lane = lax.broadcasted_iota(jnp.int32, (own.shape[0], 128), 1)
    even = jnp.bitwise_and(lane, 1) == 0
    first = lax.broadcasted_iota(jnp.int32, lane.shape, 0) * cols
    for at, value, cell in (
        (0, -(east_own[2] * faces(*east_own, *east_far)), first + (cols - 1)),
        (1, west_own[2] * faces(*west_far, *west_own), first),
    ):
        high = value.astype(BF16).astype(F32)
        low = value - high
        if at:
            body = jnp.where(even, pltpu.roll(high, 127, 1), low)
        else:
            body = jnp.where(even, high, pltpu.roll(low, 1, 1))
        fix_c[at] = jnp.where(lane == CELL_LANE, cell.astype(F32), body)

    north[...] = pick(odd_lat, ns_a_in[...], ns_b_in[...])
    south[...] = pick(odd_lat, ns_b_in[...], ns_a_in[...])

    @pl.when(lat_index == lat_count - 1)
    def _fold():
        picks = fold_ref[...].reshape(1, cols) - (lon_count - 1 - lon_index) * cols
        hot = (lax.broadcasted_iota(jnp.int32, (cols, cols), 0) == picks).astype(F32).astype(BF16)
        across = north[...]
        high, low = split(across)
        least = ((across - high.astype(F32)) - low.astype(F32)).astype(BF16)
        picked = dot_nn(high, hot) + (dot_nn(low, hot) + dot_nn(least, hot))
        at = lax.broadcasted_iota(jnp.int32, picked.shape, 0)
        is_speed = (at >= 2 * levels) & (at < 3 * levels)
        north[...] = jnp.where(is_speed, -picked, picked)

    def fields(value, t):
        return (
            value[t * levels : (t + 1) * levels],
            value[2 * levels : 3 * levels],
            value[3 * levels : 3 * levels + 1],
        )

    north_own = pick(odd_lat, ns_a[...], ns_b[...])
    south_own = pick(odd_lat, ns_b[...], ns_a[...])
    north_far, south_far = north[...], south[...]
    for t in range(2):
        at = pl.ds(t * levels, levels)
        own = fields(north_own, t)
        fix_n[at, :] = -(own[2] * faces(*own, *fields(north_far, t)))
        own = fields(south_own, t)
        fix_s[at, :] = own[2] * faces(*fields(south_far, t), *own)


def fixes(fold_partner, own, far, levels):
    rows, cols = own[0].shape[0], own[1].shape[1]
    return pl.pallas_call(
        fix_kernel,
        out_shape=(
            jax.ShapeDtypeStruct((2, rows, 128), F32),
            jax.ShapeDtypeStruct((2 * levels, cols), F32),
            jax.ShapeDtypeStruct((2 * levels, cols), F32),
        ),
        in_specs=[VMEM_SPEC] * 8,
        out_specs=(VMEM_SPEC,) * 3,
        scratch_shapes=[VM(own[1].shape, F32), VM(own[1].shape, F32)],
        compiler_params=pltpu.CompilerParams(vmem_limit_bytes=LIMIT),
        name="fix",
    )(fold_partner, *own, *far)


def order_kernel(
    cell_ref, recv_ref, sorted_v, start_ref,
    mark_ref, base_ref, rows_v, place_v, place_ref, sem, *, rows, cols, pairs,
):
    blocks = cell_ref.shape[0]
    count = blocks * 128
    half = count // 2
    cell = cell_ref[...].astype(F32)
    row = jnp.floor((cell + 0.5) * (1.0 / cols))
    hot = [jnp.where(row == float(r), 1.0, 0.0) for r in range(rows)]
    hot16 = jnp.concatenate([h.astype(BF16) for h in hot], axis=0)
    down = lax.broadcasted_iota(jnp.int32, (128, 128), 0)
    along = lax.broadcasted_iota(jnp.int32, (128, 128), 1)
    before = jnp.where(down < along, 1.0, 0.0).astype(BF16)
    after = jnp.where(along < down, 1.0, 0.0).astype(BF16)
    ones = jnp.ones((128, 128), BF16)
    within = dot_nn(hot16, before)
    totals = dot_nn(hot16, ones)
    carry = jnp.zeros((1, 128), F32)
    place = jnp.zeros(cell.shape, F32)
    per = 128 // blocks
    for c in range(rows // per):
        part = totals[c * 128 : (c + 1) * 128]
        base = dot_nn(after, part.astype(BF16)) + carry
        carry = base[127:128] + part[127:128]
        base_ref[c * 128 : (c + 1) * 128, :] = base
        spot = base + within[c * 128 : (c + 1) * 128]
        for j in range(per):
            extra = 2.0 * (c * per + j + 1)
            place = place + hot[c * per + j] * (spot[j * blocks : (j + 1) * blocks] + extra)
    place_v[...] = place.astype(jnp.int32)
    to_scalars = pltpu.make_async_copy(place_v, place_ref, sem)
    to_scalars.start()
    starts = base_ref[pl.ds(0, rows, stride=blocks), :]
    high = jnp.floor(starts * (1.0 / 128))
    low = starts - 128 * high
    first = jnp.where(along[:8] == 0, 1.0, 0.0).astype(BF16)
    starts = 128 * dot_nt(first, high.astype(BF16)) + dot_nt(first, low.astype(BF16))
    extra = 2.0 * lax.broadcasted_iota(jnp.int32, starts.shape, 1).astype(F32)
    start_ref[...] = jnp.full(start_ref.shape, count + 2 * rows, jnp.int32)
    start_ref[:, 0:rows] = (starts + extra).astype(jnp.int32)
    for i in range(blocks):
        turned = jnp.broadcast_to(cell[i : i + 1], (128, 128)).T
        for j in range(128 // pairs):
            at = (j % 2) * half + (i * (128 // pairs) + j) // 2 * pairs
            mark_ref[at : at + pairs, :] = turned[j * pairs : (j + 1) * pairs]
    n_rows = half
    lane_all = lax.broadcasted_iota(jnp.int32, (128, 128), 1)
    even = jnp.bitwise_and(lane_all, 1) == 0
    cell_lane = lane_all == CELL_LANE

    def halves(i, _):
        at = pl.multiple_of(i * 128, 128)
        both = recv_ref[pl.ds(at, 128), :]
        high = both.astype(BF16).astype(F32)
        low = both - high
        for h, body in enumerate(
            (
                jnp.where(even, high, pltpu.roll(low, 1, 1)),
                jnp.where(even, pltpu.roll(high, 127, 1), low),
            )
        ):
            there = pl.ds(pl.multiple_of(h * n_rows + at, 128), 128)
            rows_v[there, :] = jnp.where(cell_lane, mark_ref[there, :], body)
        return _

    lax.fori_loop(0, n_rows // 128, halves, 0)
    filled = count + 2 * rows
    sorted_v[filled:, :] = jnp.full((WINDOW, 128), -1.0, F32)
    to_scalars.wait()
    for i in range(place_ref.shape[0]):
        first = i * 64
        for j in range(128):
            source, h, pair = j // (2 * pairs), j // pairs % 2, j % pairs
            line = rows_v[pl.ds(h * n_rows + first + source * pairs + pair, 1), :]
            sorted_v[pl.ds(place_ref[i, j], 1), :] = line


def order(cells, recv, rows, cols, pairs):
    count = cells.size
    blocks = count // 128
    return pl.pallas_call(
        functools.partial(order_kernel, rows=rows, cols=cols, pairs=pairs),
        out_shape=(
            jax.ShapeDtypeStruct((count + 2 * rows + WINDOW, 128), F32),
            jax.ShapeDtypeStruct((8, 128), jnp.int32),
        ),
        in_specs=[VMEM_SPEC] * 2,
        out_specs=(VMEM_SPEC,) * 2,
        scratch_shapes=[
            VM((count, 128), F32),
            VM((blocks * rows, 128), F32),
            VM((count, 128), F32),
            VM((blocks, 128), jnp.int32),
            pltpu.SMEM((blocks, 128), jnp.int32),
            pltpu.SemaphoreType.DMA,
        ],
        compiler_params=pltpu.CompilerParams(vmem_limit_bytes=LIMIT),
        name="order",
    )(cells, recv)


def final_kernel(
    sorted_in, start_in, part_hbm, wet_hbm, fix_c, fix_n, fix_s,
    out_hbm,
    sorted_v, pv, wet_v, wetf, acc, start_ref, sem_i, sem_o, sem_s,
):
    _, levels, rows, cols = pv.shape
    groups = rows // 8
    tiles = cols // 128
    maps = 2 * levels

    def load(i):
        here = pl.ds(8 * PARTS[i], 8 * ((PARTS[1:] + (groups,))[i] - PARTS[i]))
        return pltpu.make_async_copy(part_hbm.at[:, :, here], pv.at[:, :, here], sem_i.at[i])

    def store(g):
        here = pl.ds(pl.multiple_of(8 * g, 8), 8)
        return pltpu.make_async_copy(pv.at[:, :, here], out_hbm.at[:, :, here], sem_o)

    small = (
        pltpu.make_async_copy(start_in, start_ref, sem_s.at[0]),
        pltpu.make_async_copy(wet_hbm, wet_v, sem_s.at[1]),
    )
    for copy in small:
        copy.start()
    for i in range(len(PARTS)):
        load(i).start()
    sorted_v[...] = sorted_in[...]
    for copy in small:
        copy.wait()
    wetf[...] = wet_v[...].astype(F32)

    for r in range(rows):
        first = start_ref[0, r]
        for h in range(2):
            sorted_v[pl.ds(first + h, 1), :] = fix_c[h, r : r + 1, :]

    lanef = lax.broadcasted_iota(jnp.int32, (WINDOW, 128), 1).astype(F32)

    def row_sources(r, at):
        at = pl.multiple_of(at, 8)
        lines = sorted_v[pl.ds(at, WINDOW), :]
        lhs = lines.astype(BF16).T
        near = jnp.broadcast_to(lines[:, CELL_LANE : CELL_LANE + 1], (WINDOW, 128)) - (r * cols).astype(F32)
        hot = [jnp.where(near - float(128 * c) == lanef, 1.0, 0.0).astype(BF16) for c in range(tiles)]
        return dot_nn(lhs, jnp.concatenate(hot, axis=1))

    def group(g, _):
        here = pl.ds(pl.multiple_of(8 * g, 8), 8)
        firsts, windows = [], []
        for j in range(8):
            s = start_ref[0, 8 * g + j]
            e = start_ref[0, 8 * g + j + 1]
            first = lax.div(s, 8) * 8
            firsts.append(first)
            windows.append(lax.div(e - first + (WINDOW - 1), WINDOW))
        for j in range(8):
            made = row_sources(8 * g + j, firsts[j])
            for c in range(tiles):
                for m in range(0, 2 * maps, 8):
                    acc[c, pl.ds(m * 9 + j, 8, stride=9), :] = made[m : m + 8, c * 128 : (c + 1) * 128]
        most = functools.reduce(jnp.maximum, windows)

        @pl.when(most > 1)
        def _more():
            for j in range(8):

                def again(i, _, j=j):
                    made = row_sources(8 * g + j, firsts[j] + i * WINDOW)
                    for c in range(tiles):
                        for m in range(0, 2 * maps, 8):
                            acc[c, pl.ds(m * 9 + j, 8, stride=9), :] += made[
                                m : m + 8, c * 128 : (c + 1) * 128
                            ]
                    return _

                lax.fori_loop(1, windows[j], again, 0)

        for i in range(len(PARTS)):

            @pl.when(g == PARTS[i])
            def _wait(i=i):
                load(i).wait()

        w = wetf[here, :]

        for edge, ref, at in ((groups - 1, fix_n, rows - 1), (0, fix_s, 0)):

            @pl.when(g == edge)
            def _edge_row(ref=ref, at=at):
                for m in range(maps):
                    t, k = m // levels, m % levels
                    pv[t, k, at : at + 1, :] += ref[m : m + 1, :]

        for m in range(maps):
            t, k = m // levels, m % levels
            at = 18 * m
            for c in range(tiles):
                lanes = slice(c * 128, (c + 1) * 128)
                pv[t, k, here, lanes] += w[:, lanes] * (acc[c, at : at + 8, :] + acc[c, at + 9 : at + 17, :])
        store(g).start()
        return _

    lax.fori_loop(0, groups, group, 0)
    pltpu.make_async_copy(pv, out_hbm, sem_o).wait()


def finish(lines, start, part, wet, fix):
    _, levels, rows, cols = part.shape
    return pl.pallas_call(
        final_kernel,
        out_shape=jax.ShapeDtypeStruct(part.shape, F32),
        in_specs=[VMEM_SPEC] * 2 + [ANY_SPEC] * 2 + [VMEM_SPEC] * 3,
        out_specs=ANY_SPEC,
        scratch_shapes=[
            VM(lines.shape, F32),
            VM(part.shape, F32),
            VM((rows, cols), jnp.int32),
            VM((rows, cols), F32),
            VM((cols // 128, 9 * 128, 128), F32),
            pltpu.SMEM(start.shape, jnp.int32),
            pltpu.SemaphoreType.DMA((len(PARTS),)),
            pltpu.SemaphoreType.DMA,
            pltpu.SemaphoreType.DMA((2,)),
        ],
        compiler_params=pltpu.CompilerParams(vmem_limit_bytes=24 << 20),
        name="final",
    )(lines, start, *in_hbm(part, wet), *fix)


def swap(value, axes, pairs):
    return lax.ppermute(value, axes, pairs + [(b, a) for a, b in pairs])


def shards(
    tracers, east_speed, north_speed, wet, fold_partner, bergs, berg_count, berg_cell, melt_map
):
    lon_count, lat_count = lax.axis_size("lon"), lax.axis_size("lat")
    levels, cols = tracers.shape[1], tracers.shape[3]

    melt = melt_rows(bergs, berg_count, melt_map)
    recv = lax.all_to_all(melt, ("lon", "lat"), split_axis=0, concat_axis=0, tiled=True)
    cells = berg_cell.reshape(-1, 128)
    part, *own, cells, fold_partner = stencil(
        tracers, east_speed, north_speed, wet, cells, fold_partner
    )
    ew, ns_a, ns_b = own

    lon_even = [(i, i + 1) for i in range(0, lon_count, 2)]
    lon_odd = [(i, (i + 1) % lon_count) for i in range(1, lon_count, 2)]

    def place(i, j):
        return i * lat_count + j

    lat_odd = [(place(i, j), place(i, j + 1)) for i in range(lon_count) for j in range(1, lat_count - 1, 2)]
    lat_odd += [
        (place(i, lat_count - 1), place(lon_count - 1 - i, lat_count - 1))
        for i in range(lon_count // 2)
    ]
    lat_even = [(j, j + 1) for j in range(0, lat_count, 2)]
    far = (
        swap(ew, "lon", lon_even),
        swap(ew, "lon", lon_odd),
        swap(ns_a, ("lon", "lat"), lat_odd),
        swap(ns_b, "lat", lat_even),
    )
    recv = recv.reshape(-1, 128)
    lines, start = order(cells, recv, tracers.shape[2], cols, melt.shape[1])
    far, start = lax.optimization_barrier((far, start))
    fix = fixes(fold_partner, own, far, levels)
    return finish(lines, start, part, wet, fix)


def solution(mesh):
    in_specs = (
        P(None, None, "lat", "lon"),
        P(None, "lat", "lon"),
        P(None, "lat", "lon"),
        P("lat", "lon"),
        P("lon"),
        P(("lon", "lat"), None),
        P(("lon", "lat")),
        P(("lon", "lat")),
        P(),
    )
    out_specs = P(None, None, "lat", "lon")
    return jax.shard_map(shards, mesh=mesh, in_specs=in_specs, out_specs=out_specs, check_vma=False)
```
